256 devices in a mesh: vocab: 256 (over z, x, y, core).
Axes of the slice: x: 4, y: 4, z: 8, core: 2. Of those that a mesh axis runs over, the one named last changes fastest.
Arguments:
- hidden: bfloat16 [4096, 2560], P('vocab'), may hold values from -3 to 3
- norm_gain: float32 [2560], replicated, may hold values from 0.1 to 1.9
- head: bfloat16 [2560, 73728], P(None, 'vocab'), may hold values from -50 to 50
- token_ids: int32 [4096], P('vocab'), may hold values from 0 to 73447
- req_len: int32 [512], replicated, may hold values from 1 to 8, as said below
- req_owner: int32 [512], replicated, may hold values from 0 to 255, as said below
Outputs:
- logprob: float32 [4096], P('vocab')
- entropy: float32 [4096], P('vocab')
The draws below stay inside these ranges and needn't reach their ends.
Inputs may be any that keep to these rules, and one draw needn't show every extreme that they name: `req_len`: each device owns exactly 2 requests; the lengths of one device's requests sum to at most 16, and to exactly 16 on some device. `req_owner`: each device index appears exactly 2 times.
All inputs are finite; a program needn't handle non-finite values.
Results may differ from the reference program's by a relative error of at most 0.0037.
Values may be sent and summed in bfloat16 or wider, within the bound.
A program may use at most 128 MiB of HBM per device.

```python
import jax
import jax.numpy as jnp
from jax import lax

D = 2560
VOCAB_REAL = 73448
VOCAB = 73728
CAP = 16
REQ_DEV = 2
REQS = 512
SLOTS = 4096
N_VOCAB = 256


def row_values(key):
    return jnp.clip(jax.random.normal(jax.random.fold_in(key, 9), (SLOTS, D), jnp.float32), -3.0, 3.0)


def drawn_plan(key):
    count = SLOTS // 8
    rows = jax.random.permutation(jax.random.fold_in(key, 31), SLOTS)[:count]
    pairs = jax.random.permutation(jax.random.fold_in(key, 33), VOCAB_REAL // 2)[:count]
    levels = jax.random.randint(jax.random.fold_in(key, 35), (count,), 0, 5)
    strength = 0.6 + 0.1 * levels.astype(jnp.float32)
    return (rows.astype(jnp.int32), (2 * pairs).astype(jnp.int32), strength)


def draw_head(key, part):
    base = jnp.clip(jax.random.normal(jax.random.fold_in(key, 5), (D, VOCAB), jnp.float32), -6.0, 6.0) * 0.6
    rows, first_cols, strength = drawn_plan(key)
    amp = 3000.0 / D
    planted = row_values(key)[rows] * (amp * strength)[:, None]
    base = base.at[:, first_cols].set(planted.T)
    base = base.at[:, first_cols + 1].set(0.993 * planted.T)
    return base.astype(jnp.bfloat16)


def draw_hidden(key, part):
    return row_values(key).astype(jnp.bfloat16)


def request_plan(key):
    inner = jax.random.fold_in(key, 21)
    owners_count = REQS // REQ_DEV
    order = jax.random.permutation(jax.random.fold_in(inner, 1), REQS)
    owners = (order % owners_count).astype(jnp.int32)
    most = CAP // REQ_DEV
    first = jax.random.randint(jax.random.fold_in(inner, 2), (REQS,), 1, most + 1)
    second = jax.random.randint(jax.random.fold_in(inner, 3), (REQS,), 1, most + 1)
    lengths = jnp.maximum(first, second)
    heavy = jax.random.randint(jax.random.fold_in(inner, 5), (), 0, owners_count)
    lengths = jnp.where(owners == heavy, most, lengths).astype(jnp.int32)
    return (lengths, owners)


def draw_req_len(key, part):
    return request_plan(key)[0]


def draw_req_owner(key, part):
    return request_plan(key)[1]


def place_ends(array, stream_key, smallest, largest):
    place = [jax.random.randint(jax.random.fold_in(stream_key, axis), (), 0, length) for axis, length in enumerate(array.shape)]
    widest = array.shape.index(max(array.shape))
    neighbour = place[:widest] + [(place[widest] + 1) % array.shape[widest]] + place[widest + 1:]
    return array.at[tuple(place)].set(smallest).at[tuple(neighbour)].set(largest)


def setup_inputs(seed: int = 0) -> dict:
    key_of = jax.random.split(jax.random.key(seed), 7)
    return {
        "hidden": draw_hidden(jax.random.fold_in(key_of[6], 71), 0),
        "norm_gain": jnp.clip(1.0 + 0.18 * jax.random.normal(key_of[1], (D,), jnp.float32), 0.1, 1.9),
        "head": draw_head(jax.random.fold_in(key_of[6], 71), 0),
        "token_ids": place_ends(jax.random.randint(key_of[3], (SLOTS,), 0, VOCAB_REAL), jax.random.fold_in(key_of[3], 1), 0, VOCAB_REAL - 1).astype(jnp.int32),
        "req_len": draw_req_len(jax.random.fold_in(key_of[6], 71), 0),
        "req_owner": draw_req_owner(jax.random.fold_in(key_of[6], 71), 0),
    }


EPS = 1e-05
NEG = -1e+30

def reference(hidden, norm_gain, head, token_ids, req_len, req_owner):
    values = hidden.astype(jnp.float32)
    scale = lax.rsqrt(lax.optimization_barrier(jnp.mean(values * values, axis=-1, keepdims=True)) + EPS)
    normed = (values * scale * norm_gain[None, :]).astype(jnp.bfloat16)
    owner_grid = jnp.arange(N_VOCAB, dtype=jnp.int32)[:, None] == req_owner[None, :]
    loads = lax.optimization_barrier(jnp.sum(jnp.where(owner_grid, req_len[None, :], 0), axis=1)).astype(jnp.int32)
    slot_index = jnp.arange(SLOTS, dtype=jnp.int32)
    live = slot_index % CAP < loads[slot_index // CAP]
    real_cols = jnp.arange(VOCAB, dtype=jnp.int32) < VOCAB_REAL
    blocks = normed.reshape(N_VOCAB, CAP, D)
    id_blocks = token_ids.reshape(N_VOCAB, CAP)

    def one_block(inputs):
        rows, chosen = inputs
        logits = jnp.dot(rows, head, preferred_element_type=jnp.float32) / 10.0
        logits = jnp.where(real_cols[None, :], logits, NEG)
        rowmax = lax.optimization_barrier(jnp.max(logits, axis=1))
        expo = jnp.where(real_cols[None, :], jnp.exp(logits - rowmax[:, None]), 0.0)
        total = lax.optimization_barrier(jnp.sum(expo, axis=1))
        weighted = lax.optimization_barrier(jnp.sum(jnp.where(real_cols[None, :], expo * logits, 0.0), axis=1))
        picked = jnp.take_along_axis(logits, chosen[:, None].astype(jnp.int32), axis=1)[:, 0]
        log_total = jnp.log(total)
        return (picked - rowmax - log_total, rowmax + log_total - weighted / total)
    logprob, entropy = lax.map(one_block, (blocks, id_blocks))
    logprob = jnp.where(live, logprob.reshape(SLOTS), 0.0)
    entropy = jnp.where(live, entropy.reshape(SLOTS), 0.0)
    return (logprob, entropy)
```

```python
import jax
import jax.numpy as jnp
from jax import lax
from jax.sharding import PartitionSpec as P

VOCAB_REAL = 73448


EPS = 1e-05
NEG = -1e30
DIGIT = 64


def slice_stats(rows, chosen, head, col_index, real_cols):
    logits = jnp.dot(rows, head, preferred_element_type=jnp.float32) / 10.0
    logits = jnp.where(real_cols[None, :], logits, NEG)
    rowmax = jnp.max(logits, axis=1)
    expo = jnp.where(real_cols[None, :], jnp.exp(logits - rowmax[:, None]), 0.0)
    total = jnp.sum(expo, axis=1)
    weighted = jnp.sum(jnp.where(real_cols[None, :], expo * logits, 0.0), axis=1)
    picked = jnp.sum(jnp.where(col_index[None, :] == chosen[:, None], logits, 0.0), axis=1)
    return (rowmax, total, weighted, picked)


def code_ids(ids):
    digits = [ids // (DIGIT * DIGIT), (ids // DIGIT) % DIGIT, ids % DIGIT]
    return jnp.stack(digits, axis=1).astype(jnp.bfloat16)


def decode_ids(coded):
    d = coded.astype(jnp.int32)
    return (d[:, 0] * DIGIT + d[:, 1]) * DIGIT + d[:, 2]


def body(hidden, norm_gain, head, token_ids, req_len, req_owner):
    local_rows, width = hidden.shape
    columns = head.shape[1]
    n_dev = lax.axis_size("vocab")
    me = lax.axis_index("vocab")
    values = hidden.astype(jnp.float32)
    scale = lax.rsqrt(jnp.mean(values * values, axis=-1, keepdims=True) + EPS)
    normed = (values * scale * norm_gain[None, :]).astype(jnp.bfloat16)
    packed = jnp.concatenate([normed, code_ids(token_ids)], axis=1)
    col_index = me * columns + jnp.arange(columns, dtype=jnp.int32)
    real_cols = col_index < VOCAB_REAL
    gathered = lax.all_gather(packed, "vocab", axis=0, tiled=True)
    all_rows = gathered[:, :width]
    all_ids = decode_ids(gathered[:, width:])
    rowmax, total, weighted, picked = slice_stats(all_rows, all_ids, head, col_index, real_cols)

    stats = jnp.stack([rowmax, total, weighted, picked], axis=0).reshape(4, n_dev, local_rows)
    stats = jnp.transpose(stats, (1, 0, 2))
    got = lax.all_to_all(stats, "vocab", 0, 0, tiled=True)
    m_i, s_i, w_i, p_i = got[:, 0], got[:, 1], got[:, 2], got[:, 3]
    top = jnp.max(m_i, axis=0)
    factor = jnp.exp(m_i - top[None, :])
    total_all = jnp.sum(s_i * factor, axis=0)
    weighted_all = jnp.sum(w_i * factor, axis=0)
    picked_all = jnp.sum(p_i, axis=0)

    load = jnp.sum(jnp.where(req_owner == me, req_len, 0))
    live = jnp.arange(local_rows, dtype=jnp.int32) < load
    log_total = jnp.log(total_all)
    logprob = jnp.where(live, picked_all - top - log_total, 0.0)
    entropy = jnp.where(live, top + log_total - weighted_all / total_all, 0.0)
    return (logprob, entropy)


def solution(mesh):
    placed = (P("vocab", None), P(), P(None, "vocab"), P("vocab"), P(), P())
    return jax.shard_map(
        body, mesh=mesh, in_specs=placed, out_specs=(P("vocab"), P("vocab")), check_vma=False
    )
```

```python
import jax
import jax.numpy as jnp
from jax import lax
from jax.sharding import Mesh, PartitionSpec as P

VOCAB_REAL = 73448


EPS = 1e-05
NEG = -1e30
DIGIT = 64


def slice_stats(rows, chosen, head, col_index, real_cols):
    logits = jnp.dot(rows, head, preferred_element_type=jnp.float32) / 10.0
    logits = jnp.where(real_cols[None, :], logits, NEG)
    rowmax = jnp.max(logits, axis=1)
    expo = jnp.where(real_cols[None, :], jnp.exp(logits - rowmax[:, None]), 0.0)
    total = jnp.sum(expo, axis=1)
    weighted = jnp.sum(jnp.where(real_cols[None, :], expo * logits, 0.0), axis=1)
    picked = jnp.sum(jnp.where(col_index[None, :] == chosen[:, None], logits, 0.0), axis=1)
    return (rowmax, total, weighted, picked)


def code_ids(ids):
    digits = [ids // (DIGIT * DIGIT), (ids // DIGIT) % DIGIT, ids % DIGIT]
    return jnp.stack(digits, axis=1).astype(jnp.bfloat16)


def decode_ids(coded):
    d = coded.astype(jnp.int32)
    return (d[:, 0] * DIGIT + d[:, 1]) * DIGIT + d[:, 2]


def body(hidden, norm_gain, head, token_ids, req_len, req_owner):
    local_rows, width = hidden.shape
    columns = head.shape[1]
    chips = lax.axis_size("chip")
    cores = lax.axis_size("core")
    me = lax.axis_index("chip") * cores + lax.axis_index("core")
    values = hidden.astype(jnp.float32)
    scale = lax.rsqrt(jnp.mean(values * values, axis=-1, keepdims=True) + EPS)
    normed = (values * scale * norm_gain[None, :]).astype(jnp.bfloat16)
    packed = jnp.concatenate([normed, code_ids(token_ids)], axis=1)
    col_index = me * columns + jnp.arange(columns, dtype=jnp.int32)
    real_cols = col_index < VOCAB_REAL
    by_chip = lax.all_gather(packed, "chip", axis=0, tiled=True)
    gathered = lax.all_gather(by_chip, "core", axis=0, tiled=True)
    all_rows = gathered[:, :width]
    all_ids = decode_ids(gathered[:, width:])
    rowmax, total, weighted, picked = slice_stats(all_rows, all_ids, head, col_index, real_cols)

    stats = jnp.stack([rowmax, total, weighted, picked], axis=0).reshape(4, cores, chips, local_rows)
    stats = jnp.transpose(stats, (2, 1, 0, 3)).reshape(chips * cores, 4, local_rows)
    got = lax.all_to_all(stats, ("chip", "core"), 0, 0, tiled=True)
    m_i, s_i, w_i, p_i = got[:, 0], got[:, 1], got[:, 2], got[:, 3]
    top = jnp.max(m_i, axis=0)
    factor = jnp.exp(m_i - top[None, :])
    total_all = jnp.sum(s_i * factor, axis=0)
    weighted_all = jnp.sum(w_i * factor, axis=0)
    picked_all = jnp.sum(p_i, axis=0)

    load = jnp.sum(jnp.where(req_owner == me, req_len, 0))
    live = jnp.arange(local_rows, dtype=jnp.int32) < load
    log_total = jnp.log(total_all)
    logprob = jnp.where(live, picked_all - top - log_total, 0.0)
    entropy = jnp.where(live, top + log_total - weighted_all / total_all, 0.0)
    return (logprob, entropy)


def solution(mesh):
    split = Mesh(mesh.devices.reshape(-1, 2), ("chip", "core"))
    rows = ("chip", "core")
    placed = (P(rows, None), P(), P(None, rows), P(rows), P(), P())
    return jax.shard_map(
        body, mesh=split, in_specs=placed, out_specs=(P(rows), P(rows)), check_vma=False
    )
```

```python
import jax
import jax.numpy as jnp
from jax import lax
from jax.sharding import Mesh, PartitionSpec as P

VOCAB_REAL = 73448


EPS = 1e-05
NEG = -1e30
DIGIT = 64
AXES = ("z", "x", "y", "core")
CHIP_AXES = ("z", "x", "y")


def slice_stats(rows, chosen, head, col_index, real_cols):
    logits = jnp.dot(rows, head, preferred_element_type=jnp.float32) / 10.0
    logits = jnp.where(real_cols[None, :], logits, NEG)
    rowmax = jnp.max(logits, axis=1)
    expo = jnp.where(real_cols[None, :], jnp.exp(logits - rowmax[:, None]), 0.0)
    total = jnp.sum(expo, axis=1)
    weighted = jnp.sum(jnp.where(real_cols[None, :], expo * logits, 0.0), axis=1)
    picked = jnp.sum(jnp.where(col_index[None, :] == chosen[:, None], logits, 0.0), axis=1)
    return (rowmax, total, weighted, picked)


def code_ids(ids):
    digits = [ids // (DIGIT * DIGIT), (ids // DIGIT) % DIGIT, ids % DIGIT]
    return jnp.stack(digits, axis=1).astype(jnp.bfloat16)


def decode_ids(coded):
    d = coded.astype(jnp.int32)
    return (d[:, 0] * DIGIT + d[:, 1]) * DIGIT + d[:, 2]


def ring(a, axis, n):
    fwd = [(i, (i + 1) % n) for i in range(n)]
    bwd = [(i, (i - 1) % n) for i in range(n)]
    rel = [None] * n
    rel[0] = a
    f = b = a
    half = n // 2
    for s in range(1, half + n % 2):
        f = lax.ppermute(f, axis, fwd)
        b = lax.ppermute(b, axis, bwd)
        rel[n - s] = f
        rel[s] = b
    if n % 2 == 0:
        cut = a.shape[0] // 2
        f2 = lax.ppermute(f[:cut], axis, fwd)
        b2 = lax.ppermute(b[cut:], axis, bwd)
        rel[half] = jnp.concatenate([f2, b2], axis=0)
    return jnp.stack(rel)


def body(hidden, norm_gain, head, token_ids, req_len, req_owner):
    local_rows, width = hidden.shape
    columns = head.shape[1]
    size = {a: lax.axis_size(a) for a in AXES}
    pos = {a: lax.axis_index(a) for a in AXES}
    chip = (pos["z"] * size["x"] + pos["x"]) * size["y"] + pos["y"]
    core = pos["core"]
    me = chip * size["core"] + core

    values = hidden.astype(jnp.float32)
    scale = lax.rsqrt(jnp.mean(values * values, axis=-1, keepdims=True) + EPS)
    normed = (values * scale * norm_gain[None, :]).astype(jnp.bfloat16)
    packed = jnp.concatenate([normed, code_ids(token_ids)], axis=1)

    other = lax.ppermute(head, "core", [(0, 1), (1, 0)])
    chip_head = jnp.where(core == 0, jnp.concatenate([head, other], axis=1), jnp.concatenate([other, head], axis=1))
    col_index = chip * (2 * columns) + jnp.arange(2 * columns, dtype=jnp.int32)
    real_cols = col_index < VOCAB_REAL

    third = local_rows // 3
    cuts = [0, local_rows - 2 * third, local_rows - third, local_rows]
    orders = [("z", "x", "y"), ("x", "y", "z"), ("y", "z", "x")]
    streams = []
    for i, order in enumerate(orders):
        part = packed[cuts[i]:cuts[i + 1]]
        for axis in order:
            part = ring(part, axis, size[axis])
        streams.append(part)
    flat = jnp.concatenate([s.reshape(-1, s.shape[-1]) for s in streams], axis=0)
    all_rows = flat[:, :width]
    all_ids = decode_ids(flat[:, width:])
    stats = jnp.stack(slice_stats(all_rows, all_ids, chip_head, col_index, real_cols), axis=0)

    pieces = []
    start = 0
    for i, order in enumerate(orders):
        rows_i = cuts[i + 1] - cuts[i]
        dims = [size[a] for a in reversed(order)]
        count = dims[0] * dims[1] * dims[2] * rows_i
        piece = stats[:, start:start + count].reshape(4, *dims, rows_i)
        start += count
        held = list(reversed(order))
        piece = jnp.transpose(piece, (0, 1 + held.index("z"), 1 + held.index("x"), 1 + held.index("y"), 4))
        pieces.append(piece)
    rel = jnp.concatenate(pieces, axis=-1)
    absolute = jnp.roll(rel, (pos["z"], pos["x"], pos["y"]), axis=(1, 2, 3))
    chips = size["z"] * size["x"] * size["y"]
    send = jnp.transpose(absolute.reshape(4, chips, local_rows), (1, 0, 2))
    got = lax.all_to_all(send, CHIP_AXES, 0, 0, tiled=True)

    m_i, s_i, w_i, p_i = got[:, 0], got[:, 1], got[:, 2], got[:, 3]
    top = jnp.max(m_i, axis=0)
    factor = jnp.exp(m_i - top[None, :])
    total_all = jnp.sum(s_i * factor, axis=0)
    weighted_all = jnp.sum(w_i * factor, axis=0)
    picked_all = jnp.sum(p_i, axis=0)

    load = jnp.sum(jnp.where(req_owner == me, req_len, 0))
    live = jnp.arange(local_rows, dtype=jnp.int32) < load
    log_total = jnp.log(total_all)
    logprob = jnp.where(live, picked_all - top - log_total, 0.0)
    entropy = jnp.where(live, top + log_total - weighted_all / total_all, 0.0)
    return (logprob, entropy)


def solution(mesh):
    split = Mesh(mesh.devices.reshape(8, 4, 4, 2), AXES)
    placed = (P(AXES, None), P(), P(None, AXES), P(AXES), P(), P())
    return jax.shard_map(
        body, mesh=split, in_specs=placed, out_specs=(P(AXES), P(AXES)), check_vma=False
    )
```

```python
import functools

import jax
import jax.numpy as jnp
from jax import lax
from jax.experimental import pallas as pl
from jax.experimental.pallas import tpu as pltpu
from jax.sharding import Mesh, PartitionSpec as P

VOCAB_REAL = 73448


EPS = 1e-05
NEG = -1e30
DIGIT = 64
AXES = ("z", "x", "y", "core")
CHIP_AXES = ("z", "x", "y")


def slice_stats(rows, chosen, head, col_index, real_cols):
    logits = jnp.dot(rows, head, preferred_element_type=jnp.float32) / 10.0
    logits = jnp.where(real_cols[None, :], logits, NEG)
    rowmax = jnp.max(logits, axis=1)
    expo = jnp.where(real_cols[None, :], jnp.exp(logits - rowmax[:, None]), 0.0)
    total = jnp.sum(expo, axis=1)
    weighted = jnp.sum(jnp.where(real_cols[None, :], expo * logits, 0.0), axis=1)
    picked = jnp.sum(jnp.where(col_index[None, :] == chosen[:, None], logits, 0.0), axis=1)
    return (rowmax, total, weighted, picked)


def code_ids(ids):
    digits = [ids // (DIGIT * DIGIT), (ids // DIGIT) % DIGIT, ids % DIGIT]
    return jnp.stack(digits, axis=1).astype(jnp.bfloat16)


def decode_ids(coded):
    d = coded.astype(jnp.int32)
    return (d[:, 0] * DIGIT + d[:, 1]) * DIGIT + d[:, 2]


STREAMS = (("z", "x", "y"), ("x", "y", "z"), ("y", "z", "x"))
LANES = 128


def gather_kernel(sizes, spans, x_ref, g_ref, send_sem, recv_sem, own_sem):
    pos = {a: lax.axis_index(a) for a in AXES}
    core = pos["core"]

    def peer(axis, k):
        at = dict(pos)
        at[axis] = lax.rem(pos[axis] + k, sizes[axis])
        return tuple(at[a] for a in AXES)

    def view(ref, held, axis_at, cols):
        idx = []
        for a in ("y", "x", "z"):
            if a in held:
                idx.append(slice(None))
            elif a in axis_at:
                idx.append(axis_at[a])
            else:
                idx.append(pos[a])
        return ref.at[tuple(idx) + (slice(None), cols)]

    barrier = pltpu.get_barrier_semaphore()
    count = 0
    for axis in CHIP_AXES:
        for k in range(1, sizes[axis]):
            pl.semaphore_signal(barrier, inc=1, device_id=peer(axis, k), device_id_type=pl.DeviceIdType.MESH)
            count += 1
    pl.semaphore_wait(barrier, count)

    own = pltpu.make_async_copy(x_ref, g_ref.at[pos["y"], pos["x"], pos["z"]], own_sem)
    own.start()
    sends = []
    for t in range(3):
        for s, order in enumerate(STREAMS):
            cols = pl.ds(spans[s][0], spans[s][1])
            axis = order[t]
            n = sizes[axis]
            held = order[:t]
            if t > 0:
                prev = order[t - 1]
                for j in range(1, sizes[prev]):
                    src_at = {prev: lax.rem(pos[prev] + j, sizes[prev])}
                    slot = view(g_ref, order[:t - 1], src_at, cols)
                    pltpu.make_async_remote_copy(
                        src_ref=slot, dst_ref=slot, send_sem=send_sem.at[s, t - 1, j],
                        recv_sem=recv_sem.at[s, t - 1, j], device_id=peer(prev, j),
                        device_id_type=pl.DeviceIdType.MESH,
                    ).wait_recv()
                if t == 1 and s == 0:
                    own.wait()
            src = x_ref.at[:, cols] if t == 0 else view(g_ref, held, {}, cols)
            dst = view(g_ref, held, {}, cols)
            for k in range(1, n):
                copy = pltpu.make_async_remote_copy(
                    src_ref=src, dst_ref=dst, send_sem=send_sem.at[s, t, k],
                    recv_sem=recv_sem.at[s, t, (n - k) % n], device_id=peer(axis, k),
                    device_id_type=pl.DeviceIdType.MESH,
                )
                copy.start()
                sends.append(copy)
    for s, order in enumerate(STREAMS):
        cols = pl.ds(spans[s][0], spans[s][1])
        last = order[2]
        for j in range(1, sizes[last]):
            slot = view(g_ref, order[:2], {last: lax.rem(pos[last] + j, sizes[last])}, cols)
            pltpu.make_async_remote_copy(
                src_ref=slot, dst_ref=slot, send_sem=send_sem.at[s, 2, j],
                recv_sem=recv_sem.at[s, 2, j], device_id=peer(last, j),
                device_id_type=pl.DeviceIdType.MESH,
            ).wait_recv()
    for copy in sends:
        copy.wait_send()


def gather_rows(packed, sizes):
    rows, width = packed.shape
    tiles = width // LANES
    part = tiles * 3 // 7
    counts = [part, tiles - 2 * part, part]
    spans, at = [], 0
    for c in counts:
        spans.append((at * LANES, c * LANES))
        at += c
    shape = (sizes["y"], sizes["x"], sizes["z"], rows, width)
    longest = max(sizes[a] for a in CHIP_AXES)
    return pl.pallas_call(
        functools.partial(gather_kernel, sizes, spans),
        out_shape=jax.ShapeDtypeStruct(shape, packed.dtype),
        in_specs=[pl.BlockSpec(memory_space=pl.ANY)],
        out_specs=pl.BlockSpec(memory_space=pl.ANY),
        scratch_shapes=[
            pltpu.SemaphoreType.DMA((3, 3, longest)),
            pltpu.SemaphoreType.DMA((3, 3, longest)),
            pltpu.SemaphoreType.DMA(()),
        ],
        compiler_params=pltpu.CompilerParams(collective_id=0, has_side_effects=True),
    )(packed)


def body(hidden, norm_gain, head, token_ids, req_len, req_owner):
    local_rows, width = hidden.shape
    columns = head.shape[1]
    size = {a: lax.axis_size(a) for a in AXES}
    pos = {a: lax.axis_index(a) for a in AXES}
    chip = (pos["z"] * size["x"] + pos["x"]) * size["y"] + pos["y"]
    core = pos["core"]
    me = chip * size["core"] + core

    values = hidden.astype(jnp.float32)
    scale = lax.rsqrt(jnp.mean(values * values, axis=-1, keepdims=True) + EPS)
    normed = (values * scale * norm_gain[None, :]).astype(jnp.bfloat16)
    coded = code_ids(token_ids)
    pad = jnp.zeros((local_rows, LANES - coded.shape[1]), jnp.bfloat16)
    packed = jnp.concatenate([normed, coded, pad], axis=1)

    other = lax.ppermute(head, "core", [(0, 1), (1, 0)])
    chip_head = jnp.where(core == 0, jnp.concatenate([head, other], axis=1), jnp.concatenate([other, head], axis=1))
    col_index = chip * (2 * columns) + jnp.arange(2 * columns, dtype=jnp.int32)
    real_cols = col_index < VOCAB_REAL

    gathered = gather_rows(packed, size).reshape(-1, packed.shape[1])
    all_rows = gathered[:, :width]
    all_ids = decode_ids(gathered[:, width:width + 3])
    stats = jnp.stack(slice_stats(all_rows, all_ids, chip_head, col_index, real_cols), axis=0)

    stats = stats.reshape(4, size["y"], size["x"], size["z"], local_rows)
    chips = size["z"] * size["x"] * size["y"]
    send = jnp.transpose(stats, (3, 2, 1, 0, 4)).reshape(chips, 4, local_rows)
    got = lax.all_to_all(send, CHIP_AXES, 0, 0, tiled=True)

    m_i, s_i, w_i, p_i = got[:, 0], got[:, 1], got[:, 2], got[:, 3]
    top = jnp.max(m_i, axis=0)
    factor = jnp.exp(m_i - top[None, :])
    total_all = jnp.sum(s_i * factor, axis=0)
    weighted_all = jnp.sum(w_i * factor, axis=0)
    picked_all = jnp.sum(p_i, axis=0)

    load = jnp.sum(jnp.where(req_owner == me, req_len, 0))
    live = jnp.arange(local_rows, dtype=jnp.int32) < load
    log_total = jnp.log(total_all)
    logprob = jnp.where(live, picked_all - top - log_total, 0.0)
    entropy = jnp.where(live, top + log_total - weighted_all / total_all, 0.0)
    return (logprob, entropy)


def solution(mesh):
    split = Mesh(mesh.devices.reshape(8, 4, 4, 2), AXES)
    placed = (P(AXES, None), P(), P(None, AXES), P(AXES), P(), P())
    return jax.shard_map(
        body, mesh=split, in_specs=placed, out_specs=(P(AXES), P(AXES)), check_vma=False
    )
```

```python
import functools

import jax
import jax.numpy as jnp
from jax import lax
from jax.experimental import pallas as pl
from jax.experimental.pallas import tpu as pltpu
from jax.sharding import Mesh, PartitionSpec as P

VOCAB_REAL = 73448


EPS = 1e-05
NEG = -1e30
DIGIT = 64
AXES = ("z", "x", "y", "core")
CHIP_AXES = ("z", "x", "y")


def slice_stats(rows, chosen, head, col_index, real_cols):
    logits = jnp.dot(rows, head, preferred_element_type=jnp.float32) / 10.0
    logits = jnp.where(real_cols[None, :], logits, NEG)
    rowmax = jnp.max(logits, axis=1)
    expo = jnp.where(real_cols[None, :], jnp.exp(logits - rowmax[:, None]), 0.0)
    total = jnp.sum(expo, axis=1)
    weighted = jnp.sum(jnp.where(real_cols[None, :], expo * logits, 0.0), axis=1)
    picked = jnp.sum(jnp.where(col_index[None, :] == chosen[:, None], logits, 0.0), axis=1)
    return (rowmax, total, weighted, picked)


def code_ids(ids):
    digits = [ids // (DIGIT * DIGIT), (ids // DIGIT) % DIGIT, ids % DIGIT]
    return jnp.stack(digits, axis=1).astype(jnp.bfloat16)


def decode_ids(coded):
    d = coded.astype(jnp.int32)
    return (d[:, 0] * DIGIT + d[:, 1]) * DIGIT + d[:, 2]


STREAMS = (("z", "x", "y"), ("x", "y", "z"), ("y", "z", "x"))
LANES = 128


def gather_kernel(sizes, spans, x_ref, g_ref, send_sem, recv_sem, own_sem):
    pos = {a: lax.axis_index(a) for a in AXES}

    def peer(axis, k):
        at = dict(pos)
        at[axis] = lax.rem(pos[axis] + k + sizes[axis], sizes[axis])
        return tuple(at[a] for a in AXES)

    def view(ref, held, axis, k, cols):
        idx = []
        for a in ("y", "x", "z"):
            if a in held:
                idx.append(slice(None))
            elif a == axis:
                idx.append(lax.rem(pos[a] + k + sizes[a], sizes[a]))
            else:
                idx.append(pos[a])
        return ref.at[tuple(idx) + (slice(None), cols)]

    barrier = pltpu.get_barrier_semaphore()
    count = 0
    for axis in CHIP_AXES:
        for k in (1, -1):
            pl.semaphore_signal(barrier, inc=1, device_id=peer(axis, k), device_id_type=pl.DeviceIdType.MESH)
            count += 1
    pl.semaphore_wait(barrier, count)

    own = pltpu.make_async_copy(x_ref, g_ref.at[pos["y"], pos["x"], pos["z"]], own_sem)
    own.start()

    plans = []
    for order in STREAMS:
        plan = []
        for t, axis in enumerate(order):
            n = sizes[axis]
            for q in range(1, n // 2 + 1):
                plan.append((t, axis, q, n % 2 == 0 and q == n // 2))
        plans.append(plan)

    def step_copies(s, step, sending):
        t, axis, q, split = plans[s][step]
        c0, w = spans[s]
        order = STREAMS[s]
        held = order[:t]
        if split:
            cut = (w // LANES // 2) * LANES
            col_of = [pl.ds(c0, cut), pl.ds(c0 + cut, w - cut)]
        else:
            col_of = [pl.ds(c0, w), pl.ds(c0, w)]
        out = []
        for d, sign in enumerate((1, -1)):
            cols = col_of[d]
            if sending:
                k = -sign * (q - 1)
                dst = view(g_ref, held, axis, k, cols)
                src = x_ref.at[:, cols] if (t == 0 and q == 1) else dst
                target = peer(axis, sign)
            else:
                k = -sign * q
                src = dst = view(g_ref, held, axis, k, cols)
                target = peer(axis, -sign)
            out.append(pltpu.make_async_remote_copy(
                src_ref=src, dst_ref=dst, send_sem=send_sem.at[s, step, d],
                recv_sem=recv_sem.at[s, step, d], device_id=target,
                device_id_type=pl.DeviceIdType.MESH,
            ))
        return out

    steps = len(plans[0])
    sends = []
    for g in range(steps):
        for s in range(len(STREAMS)):
            if g > 0:
                for copy in step_copies(s, g - 1, False):
                    copy.wait_recv()
            if g == 1 and s == 0:
                own.wait()
            for copy in step_copies(s, g, True):
                copy.start()
                sends.append(copy)
    for s in range(len(STREAMS)):
        for copy in step_copies(s, steps - 1, False):
            copy.wait_recv()
    for copy in sends:
        copy.wait_send()


def gather_rows(packed, sizes):
    rows, width = packed.shape
    tiles = width // LANES
    counts = [tiles * 8 // 21, tiles * 6 // 21]
    counts.append(tiles - sum(counts))
    spans, at = [], 0
    for c in counts:
        spans.append((at * LANES, c * LANES))
        at += c
    shape = (sizes["y"], sizes["x"], sizes["z"], rows, width)
    steps = sum(sizes[a] // 2 for a in CHIP_AXES)
    return pl.pallas_call(
        functools.partial(gather_kernel, sizes, spans),
        out_shape=jax.ShapeDtypeStruct(shape, packed.dtype),
        in_specs=[pl.BlockSpec(memory_space=pl.ANY)],
        out_specs=pl.BlockSpec(memory_space=pl.ANY),
        scratch_shapes=[
            pltpu.SemaphoreType.DMA((3, steps, 2)),
            pltpu.SemaphoreType.DMA((3, steps, 2)),
            pltpu.SemaphoreType.DMA(()),
        ],
        compiler_params=pltpu.CompilerParams(collective_id=0, has_side_effects=True),
    )(packed)


def body(hidden, norm_gain, head, token_ids, req_len, req_owner):
    local_rows, width = hidden.shape
    columns = head.shape[1]
    size = {a: lax.axis_size(a) for a in AXES}
    pos = {a: lax.axis_index(a) for a in AXES}
    chip = (pos["z"] * size["x"] + pos["x"]) * size["y"] + pos["y"]
    core = pos["core"]
    me = chip * size["core"] + core

    values = hidden.astype(jnp.float32)
    scale = lax.rsqrt(jnp.mean(values * values, axis=-1, keepdims=True) + EPS)
    normed = (values * scale * norm_gain[None, :]).astype(jnp.bfloat16)
    coded = code_ids(token_ids)
    pad = jnp.zeros((local_rows, LANES - coded.shape[1]), jnp.bfloat16)
    packed = jnp.concatenate([normed, coded, pad], axis=1)

    other = lax.ppermute(head, "core", [(0, 1), (1, 0)])
    chip_head = jnp.where(core == 0, jnp.concatenate([head, other], axis=1), jnp.concatenate([other, head], axis=1))
    col_index = chip * (2 * columns) + jnp.arange(2 * columns, dtype=jnp.int32)
    real_cols = col_index < VOCAB_REAL

    gathered = gather_rows(packed, size).reshape(-1, packed.shape[1])
    all_rows = gathered[:, :width]
    all_ids = decode_ids(gathered[:, width:width + 3])
    stats = jnp.stack(slice_stats(all_rows, all_ids, chip_head, col_index, real_cols), axis=0)

    stats = stats.reshape(4, size["y"], size["x"], size["z"], local_rows)
    chips = size["z"] * size["x"] * size["y"]
    send = jnp.transpose(stats, (3, 2, 1, 0, 4)).reshape(chips, 4, local_rows)
    got = lax.all_to_all(send, CHIP_AXES, 0, 0, tiled=True)

    m_i, s_i, w_i, p_i = got[:, 0], got[:, 1], got[:, 2], got[:, 3]
    top = jnp.max(m_i, axis=0)
    factor = jnp.exp(m_i - top[None, :])
    total_all = jnp.sum(s_i * factor, axis=0)
    weighted_all = jnp.sum(w_i * factor, axis=0)
    picked_all = jnp.sum(p_i, axis=0)

    load = jnp.sum(jnp.where(req_owner == me, req_len, 0))
    live = jnp.arange(local_rows, dtype=jnp.int32) < load
    log_total = jnp.log(total_all)
    logprob = jnp.where(live, picked_all - top - log_total, 0.0)
    entropy = jnp.where(live, top + log_total - weighted_all / total_all, 0.0)
    return (logprob, entropy)


def solution(mesh):
    split = Mesh(mesh.devices.reshape(8, 4, 4, 2), AXES)
    placed = (P(AXES, None), P(), P(None, AXES), P(AXES), P(), P())
    return jax.shard_map(
        body, mesh=split, in_specs=placed, out_specs=(P(AXES), P(AXES)), check_vma=False
    )
```

```python
import functools

import jax
import jax.numpy as jnp
from jax import lax
from jax.experimental import pallas as pl
from jax.experimental.pallas import tpu as pltpu
from jax.sharding import Mesh, PartitionSpec as P

VOCAB_REAL = 73448


EPS = 1e-05
NEG = -1e30
DIGIT = 64
AXES = ("z", "x", "y", "core")
CHIP_AXES = ("z", "x", "y")


def slice_stats(rows, chosen, head, col_index, real_cols):
    logits = jnp.dot(rows, head, preferred_element_type=jnp.float32) / 10.0
    logits = jnp.where(real_cols[None, :], logits, NEG)
    rowmax = jnp.max(logits, axis=1)
    expo = jnp.where(real_cols[None, :], jnp.exp(logits - rowmax[:, None]), 0.0)
    total = jnp.sum(expo, axis=1)
    weighted = jnp.sum(jnp.where(real_cols[None, :], expo * logits, 0.0), axis=1)
    picked = jnp.sum(jnp.where(col_index[None, :] == chosen[:, None], logits, 0.0), axis=1)
    return (rowmax, total, weighted, picked)


def code_ids(ids):
    digits = [ids // (DIGIT * DIGIT), (ids // DIGIT) % DIGIT, ids % DIGIT]
    return jnp.stack(digits, axis=1).astype(jnp.bfloat16)


def decode_ids(coded):
    d = coded.astype(jnp.int32)
    return (d[:, 0] * DIGIT + d[:, 1]) * DIGIT + d[:, 2]


STREAMS = (("z", "x", "y"), ("x", "y", "z"), ("y", "z", "x"))
LANES = 128


def gather_kernel(sizes, spans, x_ref, g_ref, send_sem, recv_sem, own_sem):
    pos = {a: lax.axis_index(a) for a in AXES}

    def peer(axis, k):
        at = dict(pos)
        at[axis] = lax.rem(pos[axis] + k + sizes[axis], sizes[axis])
        return tuple(at[a] for a in AXES)

    def view(ref, held, axis, k, cols):
        idx = []
        for a in ("y", "x", "z"):
            if a in held:
                idx.append(slice(None))
            elif a == axis:
                idx.append(lax.rem(pos[a] + k + sizes[a], sizes[a]))
            else:
                idx.append(pos[a])
        return ref.at[tuple(idx) + (slice(None), cols)]

    barrier = pltpu.get_barrier_semaphore()
    count = 0
    for axis in CHIP_AXES:
        for k in (1, -1):
            pl.semaphore_signal(barrier, inc=1, device_id=peer(axis, k), device_id_type=pl.DeviceIdType.MESH)
            count += 1
    pl.semaphore_wait(barrier, count)

    own = pltpu.make_async_copy(x_ref, g_ref.at[pos["y"], pos["x"], pos["z"]], own_sem)
    own.start()

    plans = []
    for order in STREAMS:
        plan = []
        for t, axis in enumerate(order):
            n = sizes[axis]
            for q in range(1, n // 2 + 1):
                plan.append((t, axis, q, n % 2 == 0 and q == n // 2))
        plans.append(plan)

    def step_copies(s, step, sending):
        t, axis, q, split = plans[s][step]
        c0, w = spans[s]
        order = STREAMS[s]
        held = order[:t]
        if split:
            cut = (w // LANES // 2) * LANES
            col_of = [pl.ds(c0, cut), pl.ds(c0 + cut, w - cut)]
        else:
            col_of = [pl.ds(c0, w), pl.ds(c0, w)]
        out = []
        for d, sign in enumerate((1, -1)):
            cols = col_of[d]
            if sending:
                k = -sign * (q - 1)
                dst = view(g_ref, held, axis, k, cols)
                src = x_ref.at[:, cols] if (t == 0 and q == 1) else dst
                target = peer(axis, sign)
            else:
                k = -sign * q
                src = dst = view(g_ref, held, axis, k, cols)
                target = peer(axis, -sign)
            out.append(pltpu.make_async_remote_copy(
                src_ref=src, dst_ref=dst, send_sem=send_sem.at[s, step, d],
                recv_sem=recv_sem.at[s, step, d], device_id=target,
                device_id_type=pl.DeviceIdType.MESH,
            ))
        return out

    steps = len(plans[0])
    sends = []
    for g in range(steps):
        for s in range(len(STREAMS)):
            if g > 0:
                for copy in step_copies(s, g - 1, False):
                    copy.wait_recv()
            if g == 1 and s == 0:
                own.wait()
            for copy in step_copies(s, g, True):
                copy.start()
                sends.append(copy)
    for s in range(len(STREAMS)):
        for copy in step_copies(s, steps - 1, False):
            copy.wait_recv()
    for copy in sends:
        copy.wait_send()


def gather_rows(packed, sizes):
    rows, width = packed.shape
    tiles = width // LANES
    counts = [tiles * 8 // 21, tiles * 6 // 21]
    counts.append(tiles - sum(counts))
    spans, at = [], 0
    for c in counts:
        spans.append((at * LANES, c * LANES))
        at += c
    shape = (sizes["y"], sizes["x"], sizes["z"], rows, width)
    steps = sum(sizes[a] // 2 for a in CHIP_AXES)
    return pl.pallas_call(
        functools.partial(gather_kernel, sizes, spans),
        out_shape=jax.ShapeDtypeStruct(shape, packed.dtype),
        in_specs=[pl.BlockSpec(memory_space=pl.ANY)],
        out_specs=pl.BlockSpec(memory_space=pl.ANY),
        scratch_shapes=[
            pltpu.SemaphoreType.DMA((3, steps, 2)),
            pltpu.SemaphoreType.DMA((3, steps, 2)),
            pltpu.SemaphoreType.DMA(()),
        ],
        compiler_params=pltpu.CompilerParams(collective_id=0, has_side_effects=True),
    )(packed)


def combine(parts):
    top = jnp.max(parts[:, 0], axis=0)
    factor = jnp.exp(parts[:, 0] - top[None])
    total = jnp.sum(parts[:, 1] * factor, axis=0)
    weighted = jnp.sum(parts[:, 2] * factor, axis=0)
    picked = jnp.sum(parts[:, 3], axis=0)
    return jnp.stack([top, total, weighted, picked], axis=0)


def reduce_kernel(sizes, a_ref, out_ref, r1, c1, r2, c2, r3, send_sem, recv_sem):
    pos = {a: lax.axis_index(a) for a in AXES}

    def peer(axis, k):
        at = dict(pos)
        at[axis] = lax.rem(pos[axis] + k, sizes[axis])
        return tuple(at[a] for a in AXES)

    barrier = pltpu.get_barrier_semaphore()
    count = 0
    for axis in CHIP_AXES:
        for k in range(1, sizes[axis]):
            pl.semaphore_signal(barrier, inc=1, device_id=peer(axis, k), device_id_type=pl.DeviceIdType.MESH)
            count += 1
    pl.semaphore_wait(barrier, count)

    sends = []

    def stage(t, axis, src_of, land):
        n = sizes[axis]
        for k in range(1, n):
            copy = pltpu.make_async_remote_copy(
                src_ref=src_of(lax.rem(pos[axis] + k, n)), dst_ref=land.at[pos[axis]],
                send_sem=send_sem.at[t, k], recv_sem=recv_sem.at[t, (n - k) % n],
                device_id=peer(axis, k), device_id_type=pl.DeviceIdType.MESH,
            )
            copy.start()
            sends.append(copy)
        for j in range(1, n):
            slot = land.at[lax.rem(pos[axis] + j, n)]
            pltpu.make_async_remote_copy(
                src_ref=slot, dst_ref=slot, send_sem=send_sem.at[t, j], recv_sem=recv_sem.at[t, j],
                device_id=peer(axis, j), device_id_type=pl.DeviceIdType.MESH,
            ).wait_recv()

    r1[pos["y"]] = a_ref[pos["y"]]
    stage(0, "y", lambda i: a_ref.at[i], r1)
    c1[...] = combine(r1[...])
    own_x = pl.multiple_of(pos["x"] * LANES, LANES)
    r2[pos["x"]] = c1[:, pl.ds(own_x, LANES)]
    stage(1, "x", lambda i: c1.at[:, pl.ds(pl.multiple_of(i * LANES, LANES), LANES)], r2)
    c2[...] = combine(r2[...])
    r3[pos["z"]] = c2[...]
    stage(2, "z", lambda i: c2, r3)
    out_ref[...] = combine(r3[...])
    for copy in sends:
        copy.wait_send()


def reduce_stats(parts, sizes):
    ny, nx, nz = sizes["y"], sizes["x"], sizes["z"]
    longest = max(ny, nx, nz)
    width = parts.shape[-1]
    return pl.pallas_call(
        functools.partial(reduce_kernel, sizes),
        out_shape=jax.ShapeDtypeStruct((4, LANES), jnp.float32),
        scratch_shapes=[
            pltpu.VMEM((ny, 4, width), jnp.float32),
            pltpu.VMEM((4, width), jnp.float32),
            pltpu.VMEM((nx, 4, LANES), jnp.float32),
            pltpu.VMEM((4, LANES), jnp.float32),
            pltpu.VMEM((nz, 4, LANES), jnp.float32),
            pltpu.SemaphoreType.DMA((3, longest)),
            pltpu.SemaphoreType.DMA((3, longest)),
        ],
        compiler_params=pltpu.CompilerParams(collective_id=1, has_side_effects=True),
    )(parts)


def body(hidden, norm_gain, head, token_ids, req_len, req_owner):
    local_rows, width = hidden.shape
    columns = head.shape[1]
    size = {a: lax.axis_size(a) for a in AXES}
    pos = {a: lax.axis_index(a) for a in AXES}
    chip = (pos["z"] * size["x"] + pos["x"]) * size["y"] + pos["y"]
    core = pos["core"]
    me = chip * size["core"] + core

    values = hidden.astype(jnp.float32)
    scale = lax.rsqrt(jnp.mean(values * values, axis=-1, keepdims=True) + EPS)
    normed = (values * scale * norm_gain[None, :]).astype(jnp.bfloat16)
    coded = code_ids(token_ids)
    pad = jnp.zeros((local_rows, LANES - coded.shape[1]), jnp.bfloat16)
    packed = jnp.concatenate([normed, coded, pad], axis=1)

    other = lax.ppermute(head, "core", [(0, 1), (1, 0)])
    chip_head = jnp.where(core == 0, jnp.concatenate([head, other], axis=1), jnp.concatenate([other, head], axis=1))
    col_index = chip * (2 * columns) + jnp.arange(2 * columns, dtype=jnp.int32)
    real_cols = col_index < VOCAB_REAL

    gathered = gather_rows(packed, size).reshape(-1, packed.shape[1])
    all_rows = gathered[:, :width]
    all_ids = decode_ids(gathered[:, width:width + 3])
    stats = jnp.stack(slice_stats(all_rows, all_ids, chip_head, col_index, real_cols), axis=0)

    parts = jnp.transpose(stats.reshape(4, size["y"], -1), (1, 0, 2))
    reduced = reduce_stats(parts, size)
    mine = lax.dynamic_slice_in_dim(reduced, pos["z"] * local_rows, local_rows, axis=1)
    top, total_all, weighted_all, picked_all = mine[0], mine[1], mine[2], mine[3]

    load = jnp.sum(jnp.where(req_owner == me, req_len, 0))
    live = jnp.arange(local_rows, dtype=jnp.int32) < load
    log_total = jnp.log(total_all)
    logprob = jnp.where(live, picked_all - top - log_total, 0.0)
    entropy = jnp.where(live, top + log_total - weighted_all / total_all, 0.0)
    return (logprob, entropy)


def solution(mesh):
    split = Mesh(mesh.devices.reshape(8, 4, 4, 2), AXES)
    placed = (P(AXES, None), P(), P(None, AXES), P(AXES), P(), P())
    return jax.shard_map(
        body, mesh=split, in_specs=placed, out_specs=(P(AXES), P(AXES)), check_vma=False
    )
```

```python
import functools

import jax
import jax.numpy as jnp
from jax import lax
from jax.experimental import pallas as pl
from jax.experimental.pallas import tpu as pltpu
from jax.sharding import Mesh, PartitionSpec as P

VOCAB_REAL = 73448


EPS = 1e-05
NEG = -1e30
DIGIT = 64
AXES = ("z", "x", "y", "core")
CHIP_AXES = ("z", "x", "y")


def slice_stats(rows, chosen, head, col_index, real_cols):
    logits = jnp.dot(rows, head, preferred_element_type=jnp.float32) / 10.0
    logits = jnp.where(real_cols[None, :], logits, NEG)
    rowmax = jnp.max(logits, axis=1)
    expo = jnp.where(real_cols[None, :], jnp.exp(logits - rowmax[:, None]), 0.0)
    total = jnp.sum(expo, axis=1)
    weighted = jnp.sum(jnp.where(real_cols[None, :], expo * logits, 0.0), axis=1)
    picked = jnp.sum(jnp.where(col_index[None, :] == chosen[:, None], logits, 0.0), axis=1)
    return (rowmax, total, weighted, picked)


def code_ids(ids):
    digits = [ids // (DIGIT * DIGIT), (ids // DIGIT) % DIGIT, ids % DIGIT]
    return jnp.stack(digits, axis=1).astype(jnp.bfloat16)


def decode_ids(coded):
    d = coded.astype(jnp.int32)
    return (d[:, 0] * DIGIT + d[:, 1]) * DIGIT + d[:, 2]


STREAMS = (("z", "x", "y"), ("x", "y", "z"), ("y", "z", "x"))
LANES = 128


def gather_kernel(sizes, spans, x_ref, g_ref, send_sem, recv_sem, own_sem):
    pos = {a: lax.axis_index(a) for a in AXES}

    def peer(axis, k):
        at = dict(pos)
        at[axis] = lax.rem(pos[axis] + k + sizes[axis], sizes[axis])
        return tuple(at[a] for a in AXES)

    def view(ref, held, axis, k, cols):
        idx = []
        for a in ("y", "x", "z"):
            if a in held:
                idx.append(slice(None))
            elif a == axis:
                idx.append(lax.rem(pos[a] + k + sizes[a], sizes[a]))
            else:
                idx.append(pos[a])
        return ref.at[tuple(idx) + (slice(None), cols)]

    barrier = pltpu.get_barrier_semaphore()
    count = 0
    for axis in CHIP_AXES:
        for k in range(1, sizes[axis]):
            pl.semaphore_signal(barrier, inc=1, device_id=peer(axis, k), device_id_type=pl.DeviceIdType.MESH)
            count += 1
    pl.semaphore_wait(barrier, count)

    own = pltpu.make_async_copy(x_ref, g_ref.at[pos["y"], pos["x"], pos["z"]], own_sem)
    own.start()

    plans = []
    for order in STREAMS:
        plan = [(0, order[0], 0, False)]
        for t, axis in enumerate(order[1:], start=1):
            n = sizes[axis]
            for q in range(1, n // 2 + 1):
                plan.append((t, axis, q, n % 2 == 0 and q == n // 2))
        plans.append(plan)

    def step_copies(s, step, sending):
        t, axis, q, split = plans[s][step]
        c0, w = spans[s]
        order = STREAMS[s]
        held = order[:t]
        n = sizes[axis]
        out = []
        if q == 0:
            cols = pl.ds(c0, w)
            for k in range(1, n):
                if sending:
                    dst = view(g_ref, held, axis, 0, cols)
                    src = x_ref.at[:, cols] if t == 0 else dst
                    target, label = peer(axis, k), (n - k) % n
                else:
                    src = dst = view(g_ref, held, axis, k, cols)
                    target, label = peer(axis, k), k
                out.append(pltpu.make_async_remote_copy(
                    src_ref=src, dst_ref=dst, send_sem=send_sem.at[s, step, k if sending else label],
                    recv_sem=recv_sem.at[s, step, label], device_id=target,
                    device_id_type=pl.DeviceIdType.MESH,
                ))
            return out
        if split:
            cut = (w // LANES // 2) * LANES
            col_of = [pl.ds(c0, cut), pl.ds(c0 + cut, w - cut)]
        else:
            col_of = [pl.ds(c0, w), pl.ds(c0, w)]
        for d, sign in enumerate((1, -1)):
            cols = col_of[d]
            if sending:
                k = -sign * (q - 1)
                dst = view(g_ref, held, axis, k, cols)
                src = x_ref.at[:, cols] if (t == 0 and q == 1) else dst
                target = peer(axis, sign)
            else:
                k = -sign * q
                src = dst = view(g_ref, held, axis, k, cols)
                target = peer(axis, -sign)
            out.append(pltpu.make_async_remote_copy(
                src_ref=src, dst_ref=dst, send_sem=send_sem.at[s, step, d],
                recv_sem=recv_sem.at[s, step, d], device_id=target,
                device_id_type=pl.DeviceIdType.MESH,
            ))
        return out

    steps = max(len(p) for p in plans)
    sends = []
    for g in range(steps):
        for s in range(len(STREAMS)):
            if g >= len(plans[s]):
                continue
            if g > 0:
                for copy in step_copies(s, g - 1, False):
                    copy.wait_recv()
            if g == 1 and s == 0:
                own.wait()
            for copy in step_copies(s, g, True):
                copy.start()
                sends.append(copy)
    for s in range(len(STREAMS)):
        for copy in step_copies(s, len(plans[s]) - 1, False):
            copy.wait_recv()
    for copy in sends:
        copy.wait_send()


def gather_rows(packed, sizes):
    rows, width = packed.shape
    tiles = width // LANES
    counts = [tiles * 8 // 21, tiles * 6 // 21]
    counts.append(tiles - sum(counts))
    spans, at = [], 0
    for c in counts:
        spans.append((at * LANES, c * LANES))
        at += c
    shape = (sizes["y"], sizes["x"], sizes["z"], rows, width)
    steps = 1 + max(sizes[a] // 2 for a in CHIP_AXES) + max(sizes[a] // 2 for a in CHIP_AXES)
    longest = max(sizes[a] for a in CHIP_AXES)
    return pl.pallas_call(
        functools.partial(gather_kernel, sizes, spans),
        out_shape=jax.ShapeDtypeStruct(shape, packed.dtype),
        in_specs=[pl.BlockSpec(memory_space=pl.ANY)],
        out_specs=pl.BlockSpec(memory_space=pl.ANY),
        scratch_shapes=[
            pltpu.SemaphoreType.DMA((3, steps, longest)),
            pltpu.SemaphoreType.DMA((3, steps, longest)),
            pltpu.SemaphoreType.DMA(()),
        ],
        compiler_params=pltpu.CompilerParams(collective_id=0, has_side_effects=True),
    )(packed)


def combine(parts):
    top = jnp.max(parts[:, 0], axis=0)
    factor = jnp.exp(parts[:, 0] - top[None])
    total = jnp.sum(parts[:, 1] * factor, axis=0)
    weighted = jnp.sum(parts[:, 2] * factor, axis=0)
    picked = jnp.sum(parts[:, 3], axis=0)
    return jnp.stack([top, total, weighted, picked], axis=0)


def reduce_kernel(sizes, a_ref, out_ref, r1, c1, r2, c2, r3, send_sem, recv_sem):
    pos = {a: lax.axis_index(a) for a in AXES}

    def peer(axis, k):
        at = dict(pos)
        at[axis] = lax.rem(pos[axis] + k, sizes[axis])
        return tuple(at[a] for a in AXES)

    barrier = pltpu.get_barrier_semaphore()
    count = 0
    for axis in CHIP_AXES:
        for k in range(1, sizes[axis]):
            pl.semaphore_signal(barrier, inc=1, device_id=peer(axis, k), device_id_type=pl.DeviceIdType.MESH)
            count += 1
    pl.semaphore_wait(barrier, count)

    sends = []

    def stage(t, axis, src_of, land):
        n = sizes[axis]
        for k in range(1, n):
            copy = pltpu.make_async_remote_copy(
                src_ref=src_of(lax.rem(pos[axis] + k, n)), dst_ref=land.at[pos[axis]],
                send_sem=send_sem.at[t, k], recv_sem=recv_sem.at[t, (n - k) % n],
                device_id=peer(axis, k), device_id_type=pl.DeviceIdType.MESH,
            )
            copy.start()
            sends.append(copy)
        for j in range(1, n):
            slot = land.at[lax.rem(pos[axis] + j, n)]
            pltpu.make_async_remote_copy(
                src_ref=slot, dst_ref=slot, send_sem=send_sem.at[t, j], recv_sem=recv_sem.at[t, j],
                device_id=peer(axis, j), device_id_type=pl.DeviceIdType.MESH,
            ).wait_recv()

    r1[pos["y"]] = a_ref[pos["y"]]
    stage(0, "y", lambda i: a_ref.at[i], r1)
    c1[...] = combine(r1[...])
    own_x = pl.multiple_of(pos["x"] * LANES, LANES)
    r2[pos["x"]] = c1[:, pl.ds(own_x, LANES)]
    stage(1, "x", lambda i: c1.at[:, pl.ds(pl.multiple_of(i * LANES, LANES), LANES)], r2)
    c2[...] = combine(r2[...])
    r3[pos["z"]] = c2[...]
    stage(2, "z", lambda i: c2, r3)
    out_ref[...] = combine(r3[...])
    for copy in sends:
        copy.wait_send()


def reduce_stats(parts, sizes):
    ny, nx, nz = sizes["y"], sizes["x"], sizes["z"]
    longest = max(ny, nx, nz)
    width = parts.shape[-1]
    return pl.pallas_call(
        functools.partial(reduce_kernel, sizes),
        out_shape=jax.ShapeDtypeStruct((4, LANES), jnp.float32),
        scratch_shapes=[
            pltpu.VMEM((ny, 4, width), jnp.float32),
            pltpu.VMEM((4, width), jnp.float32),
            pltpu.VMEM((nx, 4, LANES), jnp.float32),
            pltpu.VMEM((4, LANES), jnp.float32),
            pltpu.VMEM((nz, 4, LANES), jnp.float32),
            pltpu.SemaphoreType.DMA((3, longest)),
            pltpu.SemaphoreType.DMA((3, longest)),
        ],
        compiler_params=pltpu.CompilerParams(collective_id=1, has_side_effects=True),
    )(parts)


def body(hidden, norm_gain, head, token_ids, req_len, req_owner):
    local_rows, width = hidden.shape
    columns = head.shape[1]
    size = {a: lax.axis_size(a) for a in AXES}
    pos = {a: lax.axis_index(a) for a in AXES}
    chip = (pos["z"] * size["x"] + pos["x"]) * size["y"] + pos["y"]
    core = pos["core"]
    me = chip * size["core"] + core

    values = hidden.astype(jnp.float32)
    scale = lax.rsqrt(jnp.mean(values * values, axis=-1, keepdims=True) + EPS)
    normed = (values * scale * norm_gain[None, :]).astype(jnp.bfloat16)
    coded = code_ids(token_ids)
    pad = jnp.zeros((local_rows, LANES - coded.shape[1]), jnp.bfloat16)
    packed = jnp.concatenate([normed, coded, pad], axis=1)

    other = lax.ppermute(head, "core", [(0, 1), (1, 0)])
    chip_head = jnp.where(core == 0, jnp.concatenate([head, other], axis=1), jnp.concatenate([other, head], axis=1))
    col_index = chip * (2 * columns) + jnp.arange(2 * columns, dtype=jnp.int32)
    real_cols = col_index < VOCAB_REAL

    gathered = gather_rows(packed, size).reshape(-1, packed.shape[1])
    all_rows = gathered[:, :width]
    all_ids = decode_ids(gathered[:, width:width + 3])
    stats = jnp.stack(slice_stats(all_rows, all_ids, chip_head, col_index, real_cols), axis=0)

    parts = jnp.transpose(stats.reshape(4, size["y"], -1), (1, 0, 2))
    reduced = reduce_stats(parts, size)
    mine = lax.dynamic_slice_in_dim(reduced, pos["z"] * local_rows, local_rows, axis=1)
    top, total_all, weighted_all, picked_all = mine[0], mine[1], mine[2], mine[3]

    load = jnp.sum(jnp.where(req_owner == me, req_len, 0))
    live = jnp.arange(local_rows, dtype=jnp.int32) < load
    log_total = jnp.log(total_all)
    logprob = jnp.where(live, picked_all - top - log_total, 0.0)
    entropy = jnp.where(live, top + log_total - weighted_all / total_all, 0.0)
    return (logprob, entropy)


def solution(mesh):
    split = Mesh(mesh.devices.reshape(8, 4, 4, 2), AXES)
    placed = (P(AXES, None), P(), P(None, AXES), P(AXES), P(), P())
    return jax.shard_map(
        body, mesh=split, in_specs=placed, out_specs=(P(AXES), P(AXES)), check_vma=False
    )
```

```python
import functools

import jax
import jax.numpy as jnp
from jax import lax
from jax.experimental import pallas as pl
from jax.experimental.pallas import tpu as pltpu
from jax.sharding import Mesh, PartitionSpec as P

VOCAB_REAL = 73448


EPS = 1e-05
NEG = -1e30
DIGIT = 64
AXES = ("z", "x", "y", "core")
CHIP_AXES = ("z", "x", "y")


def slice_stats(rows, chosen, head, col_index, real_cols):
    logits = jnp.dot(rows, head, preferred_element_type=jnp.float32) / 10.0
    logits = jnp.where(real_cols[None, :], logits, NEG)
    rowmax = jnp.max(logits, axis=1)
    expo = jnp.where(real_cols[None, :], jnp.exp(logits - rowmax[:, None]), 0.0)
    total = jnp.sum(expo, axis=1)
    weighted = jnp.sum(jnp.where(real_cols[None, :], expo * logits, 0.0), axis=1)
    picked = jnp.sum(jnp.where(col_index[None, :] == chosen[:, None], logits, 0.0), axis=1)
    return (rowmax, total, weighted, picked)


def code_ids(ids):
    digits = [ids // (DIGIT * DIGIT), (ids // DIGIT) % DIGIT, ids % DIGIT]
    return jnp.stack(digits, axis=1).astype(jnp.bfloat16)


def decode_ids(coded):
    d = coded.astype(jnp.int32)
    return (d[:, 0] * DIGIT + d[:, 1]) * DIGIT + d[:, 2]


STREAMS = (("z", "x", "y"), ("x", "y", "z"), ("y", "z", "x"))
LANES = 128


def gather_kernel(sizes, spans, x_ref, g_ref, send_sem, recv_sem, own_sem):
    pos = {a: lax.axis_index(a) for a in AXES}

    def peer(axis, k):
        at = dict(pos)
        at[axis] = lax.rem(pos[axis] + k + sizes[axis], sizes[axis])
        return tuple(at[a] for a in AXES)

    def view(ref, held, axis, k, cols):
        idx = []
        for a in ("y", "x", "z"):
            if a in held:
                idx.append(slice(None))
            elif a == axis:
                idx.append(lax.rem(pos[a] + k + sizes[a], sizes[a]))
            else:
                idx.append(pos[a])
        return ref.at[tuple(idx) + (slice(None), cols)]

    barrier = pltpu.get_barrier_semaphore()
    count = 0
    for axis in CHIP_AXES:
        for k in (1, -1):
            pl.semaphore_signal(barrier, inc=1, device_id=peer(axis, k), device_id_type=pl.DeviceIdType.MESH)
            count += 1
    pl.semaphore_wait(barrier, count)

    own = pltpu.make_async_copy(x_ref, g_ref.at[pos["y"], pos["x"], pos["z"]], own_sem)
    own.start()

    plans = []
    for order in STREAMS:
        plan = []
        for t, axis in enumerate(order):
            n = sizes[axis]
            for q in range(1, n // 2 + 1):
                plan.append((t, axis, q, n % 2 == 0 and q == n // 2))
        plans.append(plan)

    def step_copies(s, step, sending):
        t, axis, q, split = plans[s][step]
        c0, w = spans[s]
        order = STREAMS[s]
        held = order[:t]
        if split:
            cut = (w // LANES // 2) * LANES
            col_of = [pl.ds(c0, cut), pl.ds(c0 + cut, w - cut)]
        else:
            col_of = [pl.ds(c0, w), pl.ds(c0, w)]
        out = []
        for d, sign in enumerate((1, -1)):
            cols = col_of[d]
            if sending:
                k = -sign * (q - 1)
                dst = view(g_ref, held, axis, k, cols)
                src = x_ref.at[:, cols] if (t == 0 and q == 1) else dst
                target = peer(axis, sign)
            else:
                k = -sign * q
                src = dst = view(g_ref, held, axis, k, cols)
                target = peer(axis, -sign)
            out.append(pltpu.make_async_remote_copy(
                src_ref=src, dst_ref=dst, send_sem=send_sem.at[s, step, d],
                recv_sem=recv_sem.at[s, step, d], device_id=target,
                device_id_type=pl.DeviceIdType.MESH,
            ))
        return out

    steps = len(plans[0])
    sends = []
    for g in range(steps):
        for s in range(len(STREAMS)):
            if g > 0:
                for copy in step_copies(s, g - 1, False):
                    copy.wait_recv()
            if g == 1 and s == 0:
                own.wait()
            for copy in step_copies(s, g, True):
                copy.start()
                sends.append(copy)
    for s in range(len(STREAMS)):
        for copy in step_copies(s, steps - 1, False):
            copy.wait_recv()
    for copy in sends:
        copy.wait_send()


def gather_rows(packed, sizes):
    rows, width = packed.shape
    tiles = width // LANES
    counts = [tiles * 7 // 21, tiles * 8 // 21]
    counts.append(tiles - sum(counts))
    spans, at = [], 0
    for c in counts:
        spans.append((at * LANES, c * LANES))
        at += c
    shape = (sizes["y"], sizes["x"], sizes["z"], rows, width)
    steps = sum(sizes[a] // 2 for a in CHIP_AXES)
    return pl.pallas_call(
        functools.partial(gather_kernel, sizes, spans),
        out_shape=jax.ShapeDtypeStruct(shape, packed.dtype),
        in_specs=[pl.BlockSpec(memory_space=pl.ANY)],
        out_specs=pl.BlockSpec(memory_space=pl.ANY),
        scratch_shapes=[
            pltpu.SemaphoreType.DMA((3, steps, 2)),
            pltpu.SemaphoreType.DMA((3, steps, 2)),
            pltpu.SemaphoreType.DMA(()),
        ],
        compiler_params=pltpu.CompilerParams(collective_id=0, has_side_effects=True),
    )(packed)


def combine(parts):
    top = jnp.max(parts[:, 0], axis=0)
    factor = jnp.exp(parts[:, 0] - top[None])
    total = jnp.sum(parts[:, 1] * factor, axis=0)
    weighted = jnp.sum(parts[:, 2] * factor, axis=0)
    picked = jnp.sum(parts[:, 3], axis=0)
    return jnp.stack([top, total, weighted, picked], axis=0)


def reduce_kernel(sizes, a_ref, out_ref, r1, c1, r2, c2, r3, send_sem, recv_sem):
    pos = {a: lax.axis_index(a) for a in AXES}

    def peer(axis, k):
        at = dict(pos)
        at[axis] = lax.rem(pos[axis] + k, sizes[axis])
        return tuple(at[a] for a in AXES)

    barrier = pltpu.get_barrier_semaphore()
    count = 0
    for axis in CHIP_AXES:
        for k in range(1, sizes[axis]):
            pl.semaphore_signal(barrier, inc=1, device_id=peer(axis, k), device_id_type=pl.DeviceIdType.MESH)
            count += 1
    pl.semaphore_wait(barrier, count)

    sends = []

    def stage(t, axis, src_of, land):
        n = sizes[axis]
        for k in range(1, n):
            copy = pltpu.make_async_remote_copy(
                src_ref=src_of(lax.rem(pos[axis] + k, n)), dst_ref=land.at[pos[axis]],
                send_sem=send_sem.at[t, k], recv_sem=recv_sem.at[t, (n - k) % n],
                device_id=peer(axis, k), device_id_type=pl.DeviceIdType.MESH,
            )
            copy.start()
            sends.append(copy)
        for j in range(1, n):
            slot = land.at[lax.rem(pos[axis] + j, n)]
            pltpu.make_async_remote_copy(
                src_ref=slot, dst_ref=slot, send_sem=send_sem.at[t, j], recv_sem=recv_sem.at[t, j],
                device_id=peer(axis, j), device_id_type=pl.DeviceIdType.MESH,
            ).wait_recv()

    r1[pos["y"]] = a_ref[pos["y"]]
    stage(0, "y", lambda i: a_ref.at[i], r1)
    c1[...] = combine(r1[...])
    own_x = pl.multiple_of(pos["x"] * LANES, LANES)
    r2[pos["x"]] = c1[:, pl.ds(own_x, LANES)]
    stage(1, "x", lambda i: c1.at[:, pl.ds(pl.multiple_of(i * LANES, LANES), LANES)], r2)
    c2[...] = combine(r2[...])
    r3[pos["z"]] = c2[...]
    stage(2, "z", lambda i: c2, r3)
    out_ref[...] = combine(r3[...])
    for copy in sends:
        copy.wait_send()


def reduce_stats(parts, sizes):
    ny, nx, nz = sizes["y"], sizes["x"], sizes["z"]
    longest = max(ny, nx, nz)
    width = parts.shape[-1]
    return pl.pallas_call(
        functools.partial(reduce_kernel, sizes),
        out_shape=jax.ShapeDtypeStruct((4, LANES), jnp.float32),
        scratch_shapes=[
            pltpu.VMEM((ny, 4, width), jnp.float32),
            pltpu.VMEM((4, width), jnp.float32),
            pltpu.VMEM((nx, 4, LANES), jnp.float32),
            pltpu.VMEM((4, LANES), jnp.float32),
            pltpu.VMEM((nz, 4, LANES), jnp.float32),
            pltpu.SemaphoreType.DMA((3, longest)),
            pltpu.SemaphoreType.DMA((3, longest)),
        ],
        compiler_params=pltpu.CompilerParams(collective_id=1, has_side_effects=True),
    )(parts)


def body(hidden, norm_gain, head, token_ids, req_len, req_owner):
    local_rows, width = hidden.shape
    columns = head.shape[1]
    size = {a: lax.axis_size(a) for a in AXES}
    pos = {a: lax.axis_index(a) for a in AXES}
    chip = (pos["z"] * size["x"] + pos["x"]) * size["y"] + pos["y"]
    core = pos["core"]
    me = chip * size["core"] + core

    values = hidden.astype(jnp.float32)
    scale = lax.rsqrt(jnp.mean(values * values, axis=-1, keepdims=True) + EPS)
    normed = (values * scale * norm_gain[None, :]).astype(jnp.bfloat16)
    coded = code_ids(token_ids)
    pad = jnp.zeros((local_rows, LANES - coded.shape[1]), jnp.bfloat16)
    packed = jnp.concatenate([normed, coded, pad], axis=1)

    other = lax.ppermute(head, "core", [(0, 1), (1, 0)])
    chip_head = jnp.where(core == 0, jnp.concatenate([head, other], axis=1), jnp.concatenate([other, head], axis=1))
    col_index = chip * (2 * columns) + jnp.arange(2 * columns, dtype=jnp.int32)
    real_cols = col_index < VOCAB_REAL

    gathered = gather_rows(packed, size).reshape(-1, packed.shape[1])
    all_rows = gathered[:, :width]
    all_ids = decode_ids(gathered[:, width:width + 3])
    stats = jnp.stack(slice_stats(all_rows, all_ids, chip_head, col_index, real_cols), axis=0)

    parts = jnp.transpose(stats.reshape(4, size["y"], -1), (1, 0, 2))
    reduced = reduce_stats(parts, size)
    mine = lax.dynamic_slice_in_dim(reduced, pos["z"] * local_rows, local_rows, axis=1)
    top, total_all, weighted_all, picked_all = mine[0], mine[1], mine[2], mine[3]

    load = jnp.sum(jnp.where(req_owner == me, req_len, 0))
    live = jnp.arange(local_rows, dtype=jnp.int32) < load
    log_total = jnp.log(total_all)
    logprob = jnp.where(live, picked_all - top - log_total, 0.0)
    entropy = jnp.where(live, top + log_total - weighted_all / total_all, 0.0)
    return (logprob, entropy)


def solution(mesh):
    split = Mesh(mesh.devices.reshape(8, 4, 4, 2), AXES)
    placed = (P(AXES, None), P(), P(None, AXES), P(AXES), P(), P())
    return jax.shard_map(
        body, mesh=split, in_specs=placed, out_specs=(P(AXES), P(AXES)), check_vma=False
    )
```

```python
import functools

import jax
import jax.numpy as jnp
from jax import lax
from jax.experimental import pallas as pl
from jax.experimental.pallas import tpu as pltpu
from jax.sharding import Mesh, PartitionSpec as P

VOCAB_REAL = 73448


EPS = 1e-05
NEG = -1e30
DIGIT = 64
AXES = ("z", "x", "y", "core")
CHIP_AXES = ("z", "x", "y")


def slice_stats(rows, chosen, head, col_index, real_cols):
    logits = jnp.dot(rows, head, preferred_element_type=jnp.float32) / 10.0
    logits = jnp.where(real_cols[None, :], logits, NEG)
    rowmax = jnp.max(logits, axis=1)
    expo = jnp.where(real_cols[None, :], jnp.exp(logits - rowmax[:, None]), 0.0)
    total = jnp.sum(expo, axis=1)
    weighted = jnp.sum(jnp.where(real_cols[None, :], expo * logits, 0.0), axis=1)
    picked = jnp.sum(jnp.where(col_index[None, :] == chosen[:, None], logits, 0.0), axis=1)
    return (rowmax, total, weighted, picked)


def code_ids(ids):
    digits = [ids // (DIGIT * DIGIT), (ids // DIGIT) % DIGIT, ids % DIGIT]
    return jnp.stack(digits, axis=1).astype(jnp.bfloat16)


def decode_ids(coded):
    d = coded.astype(jnp.int32)
    return (d[:, 0] * DIGIT + d[:, 1]) * DIGIT + d[:, 2]


STREAMS = (("z", "x", "y"), ("x", "y", "z"), ("y", "z", "x"))
LANES = 128


def gather_kernel(sizes, spans, x_ref, g_ref, send_sem, recv_sem, own_sem):
    pos = {a: lax.axis_index(a) for a in AXES}

    def peer(axis, k):
        at = dict(pos)
        at[axis] = lax.rem(pos[axis] + k + sizes[axis], sizes[axis])
        return tuple(at[a] for a in AXES)

    def view(ref, held, axis, k, cols):
        idx = []
        for a in ("y", "x", "z"):
            if a in held:
                idx.append(slice(None))
            elif a == axis:
                idx.append(lax.rem(pos[a] + k + sizes[a], sizes[a]))
            else:
                idx.append(pos[a])
        return ref.at[tuple(idx) + (slice(None), cols)]

    barrier = pltpu.get_barrier_semaphore()
    count = 0
    for axis in CHIP_AXES:
        for k in (1, -1):
            pl.semaphore_signal(barrier, inc=1, device_id=peer(axis, k), device_id_type=pl.DeviceIdType.MESH)
            count += 1
    pl.semaphore_wait(barrier, count)

    own = pltpu.make_async_copy(x_ref, g_ref.at[pos["y"], pos["x"], pos["z"]], own_sem)
    own.start()

    plans = []
    for order in STREAMS:
        plan = []
        for t, axis in enumerate(order):
            n = sizes[axis]
            for q in range(1, n // 2 + 1):
                plan.append((t, axis, q, n % 2 == 0 and q == n // 2))
        plans.append(plan)

    def step_copies(s, step, sending):
        t, axis, q, split = plans[s][step]
        c0, w = spans[s]
        order = STREAMS[s]
        held = order[:t]
        if split:
            cut = (w // LANES // 2) * LANES
            col_of = [pl.ds(c0, cut), pl.ds(c0 + cut, w - cut)]
        else:
            col_of = [pl.ds(c0, w), pl.ds(c0, w)]
        out = []
        for d, sign in enumerate((1, -1)):
            cols = col_of[d]
            if sending:
                k = -sign * (q - 1)
                dst = view(g_ref, held, axis, k, cols)
                src = x_ref.at[:, cols] if (t == 0 and q == 1) else dst
                target = peer(axis, sign)
            else:
                k = -sign * q
                src = dst = view(g_ref, held, axis, k, cols)
                target = peer(axis, -sign)
            out.append(pltpu.make_async_remote_copy(
                src_ref=src, dst_ref=dst, send_sem=send_sem.at[s, step, d],
                recv_sem=recv_sem.at[s, step, d], device_id=target,
                device_id_type=pl.DeviceIdType.MESH,
            ))
        return out

    steps = len(plans[0])
    sends = []
    for g in range(steps):
        if g == 1:
            own.wait()
        for s in range(len(STREAMS)):
            out = step_copies(s, g, True)
            if g > 0 and plans[s][g][0] == plans[s][g - 1][0]:
                for arrived, copy in zip(step_copies(s, g - 1, False), out):
                    arrived.wait_recv()
                    copy.start()
                    sends.append(copy)
                continue
            if g > 0:
                for copy in step_copies(s, g - 1, False):
                    copy.wait_recv()
            for copy in out:
                copy.start()
                sends.append(copy)
    for s in range(len(STREAMS)):
        for copy in step_copies(s, steps - 1, False):
            copy.wait_recv()
    for copy in sends:
        copy.wait_send()


def gather_rows(packed, sizes):
    rows, width = packed.shape
    tiles = width // LANES
    counts = [tiles * 8 // 21, tiles * 6 // 21]
    counts.append(tiles - sum(counts))
    spans, at = [], 0
    for c in counts:
        spans.append((at * LANES, c * LANES))
        at += c
    shape = (sizes["y"], sizes["x"], sizes["z"], rows, width)
    steps = sum(sizes[a] // 2 for a in CHIP_AXES)
    return pl.pallas_call(
        functools.partial(gather_kernel, sizes, spans),
        out_shape=jax.ShapeDtypeStruct(shape, packed.dtype),
        in_specs=[pl.BlockSpec(memory_space=pl.ANY)],
        out_specs=pl.BlockSpec(memory_space=pl.ANY),
        scratch_shapes=[
            pltpu.SemaphoreType.DMA((3, steps, 2)),
            pltpu.SemaphoreType.DMA((3, steps, 2)),
            pltpu.SemaphoreType.DMA(()),
        ],
        compiler_params=pltpu.CompilerParams(collective_id=0, has_side_effects=True),
    )(packed)


def combine(parts):
    top = jnp.max(parts[:, 0], axis=0)
    factor = jnp.exp(parts[:, 0] - top[None])
    total = jnp.sum(parts[:, 1] * factor, axis=0)
    weighted = jnp.sum(parts[:, 2] * factor, axis=0)
    picked = jnp.sum(parts[:, 3], axis=0)
    return jnp.stack([top, total, weighted, picked], axis=0)


def reduce_kernel(sizes, a_ref, out_ref, r1, c1, r2, c2, r3, send_sem, recv_sem):
    pos = {a: lax.axis_index(a) for a in AXES}

    def peer(axis, k):
        at = dict(pos)
        at[axis] = lax.rem(pos[axis] + k, sizes[axis])
        return tuple(at[a] for a in AXES)

    barrier = pltpu.get_barrier_semaphore()
    count = 0
    for axis in CHIP_AXES:
        for k in range(1, sizes[axis]):
            pl.semaphore_signal(barrier, inc=1, device_id=peer(axis, k), device_id_type=pl.DeviceIdType.MESH)
            count += 1
    pl.semaphore_wait(barrier, count)

    sends = []

    def stage(t, axis, src_of, land):
        n = sizes[axis]
        for k in range(1, n):
            copy = pltpu.make_async_remote_copy(
                src_ref=src_of(lax.rem(pos[axis] + k, n)), dst_ref=land.at[pos[axis]],
                send_sem=send_sem.at[t, k], recv_sem=recv_sem.at[t, (n - k) % n],
                device_id=peer(axis, k), device_id_type=pl.DeviceIdType.MESH,
            )
            copy.start()
            sends.append(copy)
        for j in range(1, n):
            slot = land.at[lax.rem(pos[axis] + j, n)]
            pltpu.make_async_remote_copy(
                src_ref=slot, dst_ref=slot, send_sem=send_sem.at[t, j], recv_sem=recv_sem.at[t, j],
                device_id=peer(axis, j), device_id_type=pl.DeviceIdType.MESH,
            ).wait_recv()

    r1[pos["y"]] = a_ref[pos["y"]]
    stage(0, "y", lambda i: a_ref.at[i], r1)
    c1[...] = combine(r1[...])
    own_x = pl.multiple_of(pos["x"] * LANES, LANES)
    r2[pos["x"]] = c1[:, pl.ds(own_x, LANES)]
    stage(1, "x", lambda i: c1.at[:, pl.ds(pl.multiple_of(i * LANES, LANES), LANES)], r2)
    c2[...] = combine(r2[...])
    r3[pos["z"]] = c2[...]
    stage(2, "z", lambda i: c2, r3)
    out_ref[...] = combine(r3[...])
    for copy in sends:
        copy.wait_send()


def reduce_stats(parts, sizes):
    ny, nx, nz = sizes["y"], sizes["x"], sizes["z"]
    longest = max(ny, nx, nz)
    width = parts.shape[-1]
    return pl.pallas_call(
        functools.partial(reduce_kernel, sizes),
        out_shape=jax.ShapeDtypeStruct((4, LANES), jnp.float32),
        scratch_shapes=[
            pltpu.VMEM((ny, 4, width), jnp.float32),
            pltpu.VMEM((4, width), jnp.float32),
            pltpu.VMEM((nx, 4, LANES), jnp.float32),
            pltpu.VMEM((4, LANES), jnp.float32),
            pltpu.VMEM((nz, 4, LANES), jnp.float32),
            pltpu.SemaphoreType.DMA((3, longest)),
            pltpu.SemaphoreType.DMA((3, longest)),
        ],
        compiler_params=pltpu.CompilerParams(collective_id=1, has_side_effects=True),
    )(parts)


def body(hidden, norm_gain, head, token_ids, req_len, req_owner):
    local_rows, width = hidden.shape
    columns = head.shape[1]
    size = {a: lax.axis_size(a) for a in AXES}
    pos = {a: lax.axis_index(a) for a in AXES}
    chip = (pos["z"] * size["x"] + pos["x"]) * size["y"] + pos["y"]
    core = pos["core"]
    me = chip * size["core"] + core

    values = hidden.astype(jnp.float32)
    scale = lax.rsqrt(jnp.mean(values * values, axis=-1, keepdims=True) + EPS)
    normed = (values * scale * norm_gain[None, :]).astype(jnp.bfloat16)
    coded = code_ids(token_ids)
    pad = jnp.zeros((local_rows, LANES - coded.shape[1]), jnp.bfloat16)
    packed = jnp.concatenate([normed, coded, pad], axis=1)

    other = lax.ppermute(head, "core", [(0, 1), (1, 0)])
    chip_head = jnp.where(core == 0, jnp.concatenate([head, other], axis=1), jnp.concatenate([other, head], axis=1))
    col_index = chip * (2 * columns) + jnp.arange(2 * columns, dtype=jnp.int32)
    real_cols = col_index < VOCAB_REAL

    gathered = gather_rows(packed, size).reshape(-1, packed.shape[1])
    all_rows = gathered[:, :width]
    all_ids = decode_ids(gathered[:, width:width + 3])
    stats = jnp.stack(slice_stats(all_rows, all_ids, chip_head, col_index, real_cols), axis=0)

    parts = jnp.transpose(stats.reshape(4, size["y"], -1), (1, 0, 2))
    reduced = reduce_stats(parts, size)
    mine = lax.dynamic_slice_in_dim(reduced, pos["z"] * local_rows, local_rows, axis=1)
    top, total_all, weighted_all, picked_all = mine[0], mine[1], mine[2], mine[3]

    load = jnp.sum(jnp.where(req_owner == me, req_len, 0))
    live = jnp.arange(local_rows, dtype=jnp.int32) < load
    log_total = jnp.log(total_all)
    logprob = jnp.where(live, picked_all - top - log_total, 0.0)
    entropy = jnp.where(live, top + log_total - weighted_all / total_all, 0.0)
    return (logprob, entropy)


def solution(mesh):
    split = Mesh(mesh.devices.reshape(8, 4, 4, 2), AXES)
    placed = (P(AXES, None), P(), P(None, AXES), P(AXES), P(), P())
    return jax.shard_map(
        body, mesh=split, in_specs=placed, out_specs=(P(AXES), P(AXES)), check_vma=False
    )
```

```python
import functools

import jax
import jax.numpy as jnp
from jax import lax
from jax.experimental import pallas as pl
from jax.experimental.pallas import tpu as pltpu
from jax.sharding import Mesh, PartitionSpec as P

VOCAB_REAL = 73448


EPS = 1e-05
NEG = -1e30
DIGIT = 64
AXES = ("z", "x", "y", "core")
CHIP_AXES = ("z", "x", "y")


def slice_stats(rows, chosen, head, col_index, real_cols):
    logits = jnp.dot(rows, head, preferred_element_type=jnp.float32) / 10.0
    logits = jnp.where(real_cols[None, :], logits, NEG)
    rowmax = jnp.max(logits, axis=1)
    expo = jnp.where(real_cols[None, :], jnp.exp(logits - rowmax[:, None]), 0.0)
    total = jnp.sum(expo, axis=1)
    weighted = jnp.sum(jnp.where(real_cols[None, :], expo * logits, 0.0), axis=1)
    picked = jnp.sum(jnp.where(col_index[None, :] == chosen[:, None], logits, 0.0), axis=1)
    return (rowmax, total, weighted, picked)


def code_ids(ids):
    digits = [ids // (DIGIT * DIGIT), (ids // DIGIT) % DIGIT, ids % DIGIT]
    return jnp.stack(digits, axis=1).astype(jnp.bfloat16)


def decode_ids(coded):
    d = coded.astype(jnp.int32)
    return (d[:, 0] * DIGIT + d[:, 1]) * DIGIT + d[:, 2]


STREAMS = (("z", "x", "y"), ("x", "y", "z"), ("y", "z", "x"))
LANES = 128


def gather_kernel(sizes, spans, x_ref, g_ref, send_sem, recv_sem, own_sem):
    pos = {a: lax.axis_index(a) for a in AXES}

    def peer(axis, k):
        at = dict(pos)
        at[axis] = lax.rem(pos[axis] + k + sizes[axis], sizes[axis])
        return tuple(at[a] for a in AXES)

    def view(ref, held, axis, k, cols):
        idx = []
        for a in ("y", "x", "z"):
            if a in held:
                idx.append(slice(None))
            elif a == axis:
                idx.append(lax.rem(pos[a] + k + sizes[a], sizes[a]))
            else:
                idx.append(pos[a])
        return ref.at[tuple(idx) + (slice(None), cols)]

    barrier = pltpu.get_barrier_semaphore()
    count = 0
    for axis in CHIP_AXES:
        for k in (1, -1):
            pl.semaphore_signal(barrier, inc=1, device_id=peer(axis, k), device_id_type=pl.DeviceIdType.MESH)
            count += 1
    pl.semaphore_wait(barrier, count)

    own = pltpu.make_async_copy(x_ref, g_ref.at[pos["y"], pos["x"], pos["z"]], own_sem)
    own.start()

    plans = []
    for order in STREAMS:
        plan = []
        for t, axis in enumerate(order):
            n = sizes[axis]
            for q in range(1, n // 2 + 1):
                plan.append((t, axis, q, n % 2 == 0 and q == n // 2))
        plans.append(plan)

    def step_copies(s, step, sending):
        t, axis, q, split = plans[s][step]
        c0, w = spans[s]
        order = STREAMS[s]
        held = order[:t]
        if split:
            cut = (w // LANES // 2) * LANES
            col_of = [pl.ds(c0, cut), pl.ds(c0 + cut, w - cut)]
        else:
            col_of = [pl.ds(c0, w), pl.ds(c0, w)]
        out = []
        for d, sign in enumerate((1, -1)):
            cols = col_of[d]
            if sending:
                k = -sign * (q - 1)
                dst = view(g_ref, held, axis, k, cols)
                src = x_ref.at[:, cols] if (t == 0 and q == 1) else dst
                target = peer(axis, sign)
            else:
                k = -sign * q
                src = dst = view(g_ref, held, axis, k, cols)
                target = peer(axis, -sign)
            out.append(pltpu.make_async_remote_copy(
                src_ref=src, dst_ref=dst, send_sem=send_sem.at[s, step, d],
                recv_sem=recv_sem.at[s, step, d], device_id=target,
                device_id_type=pl.DeviceIdType.MESH,
            ))
        return out

    steps = len(plans[0])
    sends = []
    for g in range(steps):
        for s in range(len(STREAMS)):
            if g > 0:
                for copy in step_copies(s, g - 1, False):
                    copy.wait_recv()
            if g == 1 and s == 0:
                own.wait()
            for copy in step_copies(s, g, True):
                copy.start()
                sends.append(copy)
    for s in range(len(STREAMS)):
        for copy in step_copies(s, steps - 1, False):
            copy.wait_recv()
    for copy in sends:
        copy.wait_send()


def gather_rows(packed, sizes):
    rows, width = packed.shape
    tiles = width // LANES
    counts = [tiles * 8 // 21, tiles * 6 // 21]
    counts.append(tiles - sum(counts))
    spans, at = [], 0
    for c in counts:
        spans.append((at * LANES, c * LANES))
        at += c
    shape = (sizes["y"], sizes["x"], sizes["z"], rows, width)
    steps = sum(sizes[a] // 2 for a in CHIP_AXES)
    return pl.pallas_call(
        functools.partial(gather_kernel, sizes, spans),
        out_shape=jax.ShapeDtypeStruct(shape, packed.dtype),
        in_specs=[pl.BlockSpec(memory_space=pl.ANY)],
        out_specs=pl.BlockSpec(memory_space=pl.ANY),
        scratch_shapes=[
            pltpu.SemaphoreType.DMA((3, steps, 2)),
            pltpu.SemaphoreType.DMA((3, steps, 2)),
            pltpu.SemaphoreType.DMA(()),
        ],
        compiler_params=pltpu.CompilerParams(collective_id=0, has_side_effects=True),
    )(packed)


def combine(parts):
    top = jnp.max(parts[:, 0], axis=0)
    factor = jnp.exp(parts[:, 0] - top[None])
    total = jnp.sum(parts[:, 1] * factor, axis=0)
    weighted = jnp.sum(parts[:, 2] * factor, axis=0)
    picked = jnp.sum(parts[:, 3], axis=0)
    return jnp.stack([top, total, weighted, picked], axis=0)


def reduce_kernel(sizes, a_ref, out_ref, r1, c1, r2, c2, r3, send_sem, recv_sem):
    pos = {a: lax.axis_index(a) for a in AXES}

    def peer(axis, k):
        at = dict(pos)
        at[axis] = lax.rem(pos[axis] + k, sizes[axis])
        return tuple(at[a] for a in AXES)

    barrier = pltpu.get_barrier_semaphore()
    count = 0
    for axis in CHIP_AXES:
        for k in range(1, sizes[axis]):
            pl.semaphore_signal(barrier, inc=1, device_id=peer(axis, k), device_id_type=pl.DeviceIdType.MESH)
            count += 1
    pl.semaphore_wait(barrier, count)

    sends = []

    def stage(t, axis, src_of, land):
        n = sizes[axis]
        for k in range(1, n):
            copy = pltpu.make_async_remote_copy(
                src_ref=src_of(lax.rem(pos[axis] + k, n)), dst_ref=land.at[pos[axis]],
                send_sem=send_sem.at[t, k], recv_sem=recv_sem.at[t, (n - k) % n],
                device_id=peer(axis, k), device_id_type=pl.DeviceIdType.MESH,
            )
            copy.start()
            sends.append(copy)
        for j in range(1, n):
            slot = land.at[lax.rem(pos[axis] + j, n)]
            pltpu.make_async_remote_copy(
                src_ref=slot, dst_ref=slot, send_sem=send_sem.at[t, j], recv_sem=recv_sem.at[t, j],
                device_id=peer(axis, j), device_id_type=pl.DeviceIdType.MESH,
            ).wait_recv()

    r1[pos["y"]] = a_ref[pos["y"]]
    stage(0, "y", lambda i: a_ref.at[i], r1)
    c1[...] = combine(r1[...])
    own_x = pl.multiple_of(pos["x"] * LANES, LANES)
    r2[pos["x"]] = c1[:, pl.ds(own_x, LANES)]
    stage(1, "x", lambda i: c1.at[:, pl.ds(pl.multiple_of(i * LANES, LANES), LANES)], r2)
    c2[...] = combine(r2[...])
    r3[pos["z"]] = c2[...]
    stage(2, "z", lambda i: c2, r3)
    out_ref[...] = combine(r3[...])
    for copy in sends:
        copy.wait_send()


def reduce_stats(parts, sizes):
    ny, nx, nz = sizes["y"], sizes["x"], sizes["z"]
    longest = max(ny, nx, nz)
    width = parts.shape[-1]
    return pl.pallas_call(
        functools.partial(reduce_kernel, sizes),
        out_shape=jax.ShapeDtypeStruct((4, LANES), jnp.float32),
        scratch_shapes=[
            pltpu.VMEM((ny, 4, width), jnp.float32),
            pltpu.VMEM((4, width), jnp.float32),
            pltpu.VMEM((nx, 4, LANES), jnp.float32),
            pltpu.VMEM((4, LANES), jnp.float32),
            pltpu.VMEM((nz, 4, LANES), jnp.float32),
            pltpu.SemaphoreType.DMA((3, longest)),
            pltpu.SemaphoreType.DMA((3, longest)),
        ],
        compiler_params=pltpu.CompilerParams(collective_id=1, has_side_effects=True),
    )(parts)


def pack_kernel(h_ref, gain_ref, ids_ref, out_ref):
    values = h_ref[...].astype(jnp.float32)
    width = values.shape[1]
    scale = lax.rsqrt(jnp.mean(values * values, axis=-1, keepdims=True) + EPS)
    out_ref[:, :width] = (values * scale * gain_ref[...]).astype(jnp.bfloat16)
    ids = ids_ref[...]
    lane = lax.broadcasted_iota(jnp.int32, (ids.shape[0], LANES), 1)
    digit = jnp.where(lane == 0, ids // (DIGIT * DIGIT), jnp.where(lane == 1, (ids // DIGIT) % DIGIT, ids % DIGIT))
    digit = jnp.where(lane < 3, digit, 0)
    out_ref[:, width:] = digit.astype(jnp.float32).astype(jnp.bfloat16)


def pack_rows(hidden, norm_gain, token_ids):
    rows, width = hidden.shape
    return pl.pallas_call(
        pack_kernel,
        out_shape=jax.ShapeDtypeStruct((rows, width + LANES), jnp.bfloat16),
    )(hidden, norm_gain.reshape(1, width), token_ids.reshape(rows, 1))


def body(hidden, norm_gain, head, token_ids, req_len, req_owner):
    local_rows, width = hidden.shape
    columns = head.shape[1]
    size = {a: lax.axis_size(a) for a in AXES}
    pos = {a: lax.axis_index(a) for a in AXES}
    chip = (pos["z"] * size["x"] + pos["x"]) * size["y"] + pos["y"]
    core = pos["core"]
    me = chip * size["core"] + core

    packed = pack_rows(hidden, norm_gain, token_ids)

    other = lax.ppermute(head, "core", [(0, 1), (1, 0)])
    chip_head = jnp.where(core == 0, jnp.concatenate([head, other], axis=1), jnp.concatenate([other, head], axis=1))
    col_index = chip * (2 * columns) + jnp.arange(2 * columns, dtype=jnp.int32)
    real_cols = col_index < VOCAB_REAL

    gathered = gather_rows(packed, size).reshape(-1, packed.shape[1])
    all_rows = gathered[:, :width]
    all_ids = decode_ids(gathered[:, width:width + 3])
    stats = jnp.stack(slice_stats(all_rows, all_ids, chip_head, col_index, real_cols), axis=0)

    parts = jnp.transpose(stats.reshape(4, size["y"], -1), (1, 0, 2))
    reduced = reduce_stats(parts, size)
    mine = lax.dynamic_slice_in_dim(reduced, pos["z"] * local_rows, local_rows, axis=1)
    top, total_all, weighted_all, picked_all = mine[0], mine[1], mine[2], mine[3]

    load = jnp.sum(jnp.where(req_owner == me, req_len, 0))
    live = jnp.arange(local_rows, dtype=jnp.int32) < load
    log_total = jnp.log(total_all)
    logprob = jnp.where(live, picked_all - top - log_total, 0.0)
    entropy = jnp.where(live, top + log_total - weighted_all / total_all, 0.0)
    return (logprob, entropy)


def solution(mesh):
    split = Mesh(mesh.devices.reshape(8, 4, 4, 2), AXES)
    placed = (P(AXES, None), P(), P(None, AXES), P(AXES), P(), P())
    return jax.shard_map(
        body, mesh=split, in_specs=placed, out_specs=(P(AXES), P(AXES)), check_vma=False
    )
```

```python
import functools

import jax
import jax.numpy as jnp
from jax import lax
from jax.experimental import pallas as pl
from jax.experimental.pallas import tpu as pltpu
from jax.sharding import Mesh, PartitionSpec as P

VOCAB_REAL = 73448


EPS = 1e-05
NEG = -1e30
DIGIT = 64
AXES = ("z", "x", "y", "core")
CHIP_AXES = ("z", "x", "y")


def slice_stats(rows, chosen, head, col_index, real_cols):
    logits = jnp.dot(rows, head, preferred_element_type=jnp.float32) / 10.0
    logits = jnp.where(real_cols[None, :], logits, NEG)
    rowmax = jnp.max(logits, axis=1)
    expo = jnp.where(real_cols[None, :], jnp.exp(logits - rowmax[:, None]), 0.0)
    total = jnp.sum(expo, axis=1)
    weighted = jnp.sum(jnp.where(real_cols[None, :], expo * logits, 0.0), axis=1)
    picked = jnp.sum(jnp.where(col_index[None, :] == chosen[:, None], logits, 0.0), axis=1)
    return (rowmax, total, weighted, picked)


def code_ids(ids):
    digits = [ids // (DIGIT * DIGIT), (ids // DIGIT) % DIGIT, ids % DIGIT]
    return jnp.stack(digits, axis=1).astype(jnp.bfloat16)


def decode_ids(coded):
    d = coded.astype(jnp.int32)
    return (d[:, 0] * DIGIT + d[:, 1]) * DIGIT + d[:, 2]


STREAMS = (("z", "x", "y"), ("x", "y", "z"), ("y", "z", "x"))
LANES = 128


def gather_kernel(sizes, spans, x_ref, g_ref, send_sem, recv_sem, own_sem):
    pos = {a: lax.axis_index(a) for a in AXES}

    def peer(axis, k):
        at = dict(pos)
        at[axis] = lax.rem(pos[axis] + k + sizes[axis], sizes[axis])
        return tuple(at[a] for a in AXES)

    def view(ref, held, axis, k, cols):
        idx = []
        for a in ("y", "x", "z"):
            if a in held:
                idx.append(slice(None))
            elif a == axis:
                idx.append(lax.rem(pos[a] + k + sizes[a], sizes[a]))
            else:
                idx.append(pos[a])
        return ref.at[tuple(idx) + (slice(None), cols)]

    barrier = pltpu.get_barrier_semaphore()
    count = 0
    for axis in CHIP_AXES:
        for k in (1, -1):
            pl.semaphore_signal(barrier, inc=1, device_id=peer(axis, k), device_id_type=pl.DeviceIdType.MESH)
            count += 1
    pl.semaphore_wait(barrier, count)

    own = pltpu.make_async_copy(x_ref, g_ref.at[pos["y"], pos["x"], pos["z"]], own_sem)
    own.start()

    plans = []
    for order in STREAMS:
        plan = []
        for t, axis in enumerate(order):
            n = sizes[axis]
            for q in range(1, n // 2 + 1):
                plan.append((t, axis, q, n % 2 == 0 and q == n // 2))
        plans.append(plan)

    def step_copies(s, step, sending):
        t, axis, q, split = plans[s][step]
        c0, w = spans[s]
        order = STREAMS[s]
        held = order[:t]
        if split:
            cut = (w // LANES // 2) * LANES
            col_of = [pl.ds(c0, cut), pl.ds(c0 + cut, w - cut)]
        else:
            col_of = [pl.ds(c0, w), pl.ds(c0, w)]
        out = []
        for d, sign in enumerate((1, -1)):
            cols = col_of[d]
            if sending:
                k = -sign * (q - 1)
                dst = view(g_ref, held, axis, k, cols)
                src = x_ref.at[:, cols] if (t == 0 and q == 1) else dst
                target = peer(axis, sign)
            else:
                k = -sign * q
                src = dst = view(g_ref, held, axis, k, cols)
                target = peer(axis, -sign)
            out.append(pltpu.make_async_remote_copy(
                src_ref=src, dst_ref=dst, send_sem=send_sem.at[s, step, d],
                recv_sem=recv_sem.at[s, step, d], device_id=target,
                device_id_type=pl.DeviceIdType.MESH,
            ))
        return out

    steps = len(plans[0])
    sends = []
    for g in range(steps):
        for s in range(len(STREAMS)):
            if g > 0:
                for copy in step_copies(s, g - 1, False):
                    copy.wait_recv()
            if g == 1 and s == 0:
                own.wait()
            for copy in step_copies(s, g, True):
                copy.start()
                sends.append(copy)
    for s in range(len(STREAMS)):
        for copy in step_copies(s, steps - 1, False):
            copy.wait_recv()
    for copy in sends:
        copy.wait_send()


def gather_rows(packed, sizes):
    rows, width = packed.shape
    tiles = width // LANES
    counts = [tiles * 8 // 21, tiles * 6 // 21]
    counts.append(tiles - sum(counts))
    spans, at = [], 0
    for c in counts:
        spans.append((at * LANES, c * LANES))
        at += c
    shape = (sizes["y"], sizes["x"], sizes["z"], rows, width)
    steps = sum(sizes[a] // 2 for a in CHIP_AXES)
    return pl.pallas_call(
        functools.partial(gather_kernel, sizes, spans),
        out_shape=jax.ShapeDtypeStruct(shape, packed.dtype),
        in_specs=[pl.BlockSpec(memory_space=pl.ANY)],
        out_specs=pl.BlockSpec(memory_space=pl.ANY),
        scratch_shapes=[
            pltpu.SemaphoreType.DMA((3, steps, 2)),
            pltpu.SemaphoreType.DMA((3, steps, 2)),
            pltpu.SemaphoreType.DMA(()),
        ],
        compiler_params=pltpu.CompilerParams(collective_id=0, has_side_effects=True),
    )(packed)


def combine(parts):
    top = jnp.max(parts[:, 0], axis=0)
    factor = jnp.exp(parts[:, 0] - top[None])
    total = jnp.sum(parts[:, 1] * factor, axis=0)
    weighted = jnp.sum(parts[:, 2] * factor, axis=0)
    picked = jnp.sum(parts[:, 3], axis=0)
    return jnp.stack([top, total, weighted, picked], axis=0)


def reduce_kernel(sizes, a_ref, out_ref, r1, c1, r2, c2, r3, send_sem, recv_sem):
    pos = {a: lax.axis_index(a) for a in AXES}

    def peer(axis, k):
        at = dict(pos)
        at[axis] = lax.rem(pos[axis] + k, sizes[axis])
        return tuple(at[a] for a in AXES)

    barrier = pltpu.get_barrier_semaphore()
    count = 0
    for axis in CHIP_AXES:
        for k in range(1, sizes[axis]):
            pl.semaphore_signal(barrier, inc=1, device_id=peer(axis, k), device_id_type=pl.DeviceIdType.MESH)
            count += 1
    pl.semaphore_wait(barrier, count)

    sends = []

    def stage(t, axis, src_of, land):
        n = sizes[axis]
        for k in range(1, n):
            copy = pltpu.make_async_remote_copy(
                src_ref=src_of(lax.rem(pos[axis] + k, n)), dst_ref=land.at[pos[axis]],
                send_sem=send_sem.at[t, k], recv_sem=recv_sem.at[t, (n - k) % n],
                device_id=peer(axis, k), device_id_type=pl.DeviceIdType.MESH,
            )
            copy.start()
            sends.append(copy)
        for j in range(1, n):
            slot = land.at[lax.rem(pos[axis] + j, n)]
            pltpu.make_async_remote_copy(
                src_ref=slot, dst_ref=slot, send_sem=send_sem.at[t, j], recv_sem=recv_sem.at[t, j],
                device_id=peer(axis, j), device_id_type=pl.DeviceIdType.MESH,
            ).wait_recv()

    r1[pos["y"]] = a_ref[pos["y"]]
    stage(0, "y", lambda i: a_ref.at[i], r1)
    c1[...] = combine(r1[...])
    own_x = pl.multiple_of(pos["x"] * LANES, LANES)
    r2[pos["x"]] = c1[:, pl.ds(own_x, LANES)]
    stage(1, "x", lambda i: c1.at[:, pl.ds(pl.multiple_of(i * LANES, LANES), LANES)], r2)
    c2[...] = combine(r2[...])
    r3[pos["z"]] = c2[...]
    stage(2, "z", lambda i: c2, r3)
    out_ref[...] = combine(r3[...])
    for copy in sends:
        copy.wait_send()


def reduce_stats(parts, sizes):
    ny, nx, nz = sizes["y"], sizes["x"], sizes["z"]
    longest = max(ny, nx, nz)
    width = parts.shape[-1]
    return pl.pallas_call(
        functools.partial(reduce_kernel, sizes),
        out_shape=jax.ShapeDtypeStruct((4, LANES), jnp.float32),
        scratch_shapes=[
            pltpu.VMEM((ny, 4, width), jnp.float32),
            pltpu.VMEM((4, width), jnp.float32),
            pltpu.VMEM((nx, 4, LANES), jnp.float32),
            pltpu.VMEM((4, LANES), jnp.float32),
            pltpu.VMEM((nz, 4, LANES), jnp.float32),
            pltpu.SemaphoreType.DMA((3, longest)),
            pltpu.SemaphoreType.DMA((3, longest)),
        ],
        compiler_params=pltpu.CompilerParams(collective_id=1, has_side_effects=True),
    )(parts)


def pack_kernel(h_ref, gain_ref, ids_ref, out_ref):
    values = h_ref[...].astype(jnp.float32)
    rows, width = values.shape
    scale = lax.rsqrt(jnp.mean(values * values, axis=-1, keepdims=True) + EPS)
    out_ref[:, :width] = (values * scale * gain_ref[...][None, :]).astype(jnp.bfloat16)
    row = lax.broadcasted_iota(jnp.int32, (rows, LANES), 0)
    lane = lax.broadcasted_iota(jnp.int32, (rows, LANES), 1)
    digit = jnp.zeros((rows, LANES), jnp.int32)
    for r in range(rows):
        v = ids_ref[r]
        for i, d in enumerate((v // (DIGIT * DIGIT), (v // DIGIT) % DIGIT, v % DIGIT)):
            digit = jnp.where((row == r) & (lane == i), d, digit)
    out_ref[:, width:] = digit.astype(jnp.float32).astype(jnp.bfloat16)


def pack_rows(hidden, norm_gain, token_ids):
    rows, width = hidden.shape
    return pl.pallas_call(
        pack_kernel,
        out_shape=jax.ShapeDtypeStruct((rows, width + LANES), jnp.bfloat16),
        in_specs=[
            pl.BlockSpec(memory_space=pltpu.VMEM),
            pl.BlockSpec(memory_space=pltpu.VMEM),
            pl.BlockSpec(memory_space=pltpu.SMEM),
        ],
    )(hidden, norm_gain, token_ids)


def body(hidden, norm_gain, head, token_ids, req_len, req_owner):
    local_rows, width = hidden.shape
    columns = head.shape[1]
    size = {a: lax.axis_size(a) for a in AXES}
    pos = {a: lax.axis_index(a) for a in AXES}
    chip = (pos["z"] * size["x"] + pos["x"]) * size["y"] + pos["y"]
    core = pos["core"]
    me = chip * size["core"] + core

    packed = pack_rows(hidden, norm_gain, token_ids)

    other = lax.ppermute(head, "core", [(0, 1), (1, 0)])
    chip_head = jnp.where(core == 0, jnp.concatenate([head, other], axis=1), jnp.concatenate([other, head], axis=1))
    col_index = chip * (2 * columns) + jnp.arange(2 * columns, dtype=jnp.int32)
    real_cols = col_index < VOCAB_REAL

    gathered = gather_rows(packed, size).reshape(-1, packed.shape[1])
    all_rows = gathered[:, :width]
    all_ids = decode_ids(gathered[:, width:width + 3])
    stats = jnp.stack(slice_stats(all_rows, all_ids, chip_head, col_index, real_cols), axis=0)

    parts = jnp.transpose(stats.reshape(4, size["y"], -1), (1, 0, 2))
    reduced = reduce_stats(parts, size)
    mine = lax.dynamic_slice_in_dim(reduced, pos["z"] * local_rows, local_rows, axis=1)
    top, total_all, weighted_all, picked_all = mine[0], mine[1], mine[2], mine[3]

    load = jnp.sum(jnp.where(req_owner == me, req_len, 0))
    live = jnp.arange(local_rows, dtype=jnp.int32) < load
    log_total = jnp.log(total_all)
    logprob = jnp.where(live, picked_all - top - log_total, 0.0)
    entropy = jnp.where(live, top + log_total - weighted_all / total_all, 0.0)
    return (logprob, entropy)


def solution(mesh):
    split = Mesh(mesh.devices.reshape(8, 4, 4, 2), AXES)
    placed = (P(AXES, None), P(), P(None, AXES), P(AXES), P(), P())
    return jax.shard_map(
        body, mesh=split, in_specs=placed, out_specs=(P(AXES), P(AXES)), check_vma=False
    )
```

```python
import functools

import jax
import jax.numpy as jnp
from jax import lax
from jax.experimental import pallas as pl
from jax.experimental.pallas import tpu as pltpu
from jax.sharding import Mesh, PartitionSpec as P

VOCAB_REAL = 73448


EPS = 1e-05
NEG = -1e30
DIGIT = 64
AXES = ("z", "x", "y", "core")
CHIP_AXES = ("z", "x", "y")


def slice_stats(rows, chosen, head, col_index, real_cols):
    logits = jnp.dot(rows, head, preferred_element_type=jnp.float32) / 10.0
    logits = jnp.where(real_cols[None, :], logits, NEG)
    rowmax = jnp.max(logits, axis=1)
    expo = jnp.where(real_cols[None, :], jnp.exp(logits - rowmax[:, None]), 0.0)
    total = jnp.sum(expo, axis=1)
    weighted = jnp.sum(jnp.where(real_cols[None, :], expo * logits, 0.0), axis=1)
    picked = jnp.sum(jnp.where(col_index[None, :] == chosen[:, None], logits, 0.0), axis=1)
    return (rowmax, total, weighted, picked)


def code_ids(ids):
    digits = [ids // (DIGIT * DIGIT), (ids // DIGIT) % DIGIT, ids % DIGIT]
    return jnp.stack(digits, axis=1).astype(jnp.bfloat16)


def decode_ids(coded):
    d = coded.astype(jnp.int32)
    return (d[:, 0] * DIGIT + d[:, 1]) * DIGIT + d[:, 2]


STREAMS = (("z", "x", "y"), ("x", "y", "z"), ("y", "z", "x"))
LANES = 128


def gather_kernel(sizes, spans, x_ref, g_ref, send_sem, recv_sem, own_sem):
    pos = {a: lax.axis_index(a) for a in AXES}

    def peer(axis, k):
        at = dict(pos)
        at[axis] = lax.rem(pos[axis] + k + sizes[axis], sizes[axis])
        return tuple(at[a] for a in AXES)

    def view(ref, held, axis, k, cols):
        idx = []
        for a in ("y", "x", "z"):
            if a in held:
                idx.append(slice(None))
            elif a == axis:
                idx.append(lax.rem(pos[a] + k + sizes[a], sizes[a]))
            else:
                idx.append(pos[a])
        return ref.at[tuple(idx) + (slice(None), cols)]

    barrier = pltpu.get_barrier_semaphore()
    count = 0
    for axis in CHIP_AXES:
        for k in (1, -1):
            pl.semaphore_signal(barrier, inc=1, device_id=peer(axis, k), device_id_type=pl.DeviceIdType.MESH)
            count += 1
    pl.semaphore_wait(barrier, count)

    own = pltpu.make_async_copy(x_ref, g_ref.at[pos["y"], pos["x"], pos["z"]], own_sem)
    own.start()

    plans = []
    for order in STREAMS:
        plan = []
        for t, axis in enumerate(order):
            n = sizes[axis]
            for q in range(1, n // 2 + 1):
                plan.append((t, axis, q, n % 2 == 0 and q == n // 2))
        plans.append(plan)

    def step_copies(s, step, sending):
        t, axis, q, split = plans[s][step]
        c0, w = spans[s]
        order = STREAMS[s]
        held = order[:t]
        if split:
            cut = (w // LANES // 2) * LANES
            col_of = [pl.ds(c0, cut), pl.ds(c0 + cut, w - cut)]
        else:
            col_of = [pl.ds(c0, w), pl.ds(c0, w)]
        out = []
        for d, sign in enumerate((1, -1)):
            cols = col_of[d]
            if sending:
                k = -sign * (q - 1)
                dst = view(g_ref, held, axis, k, cols)
                src = x_ref.at[:, cols] if (t == 0 and q == 1) else dst
                target = peer(axis, sign)
            else:
                k = -sign * q
                src = dst = view(g_ref, held, axis, k, cols)
                target = peer(axis, -sign)
            out.append(pltpu.make_async_remote_copy(
                src_ref=src, dst_ref=dst, send_sem=send_sem.at[s, step, d],
                recv_sem=recv_sem.at[s, step, d], device_id=target,
                device_id_type=pl.DeviceIdType.MESH,
            ))
        return out

    steps = len(plans[0])
    sends = []
    for g in range(steps):
        for s in range(len(STREAMS)):
            if g > 0:
                for copy in step_copies(s, g - 1, False):
                    copy.wait_recv()
            if g == 1 and s == 0:
                own.wait()
            for copy in step_copies(s, g, True):
                copy.start()
                sends.append(copy)
    for s in range(len(STREAMS)):
        for copy in step_copies(s, steps - 1, False):
            copy.wait_recv()
    for copy in sends:
        copy.wait_send()


def gather_rows(packed, sizes):
    rows, width = packed.shape
    tiles = width // LANES
    counts = [tiles * 9 // 21, tiles * 5 // 21]
    counts.append(tiles - sum(counts))
    spans, at = [], 0
    for c in counts:
        spans.append((at * LANES, c * LANES))
        at += c
    shape = (sizes["y"], sizes["x"], sizes["z"], rows, width)
    steps = sum(sizes[a] // 2 for a in CHIP_AXES)
    return pl.pallas_call(
        functools.partial(gather_kernel, sizes, spans),
        out_shape=jax.ShapeDtypeStruct(shape, packed.dtype),
        in_specs=[pl.BlockSpec(memory_space=pl.ANY)],
        out_specs=pl.BlockSpec(memory_space=pl.ANY),
        scratch_shapes=[
            pltpu.SemaphoreType.DMA((3, steps, 2)),
            pltpu.SemaphoreType.DMA((3, steps, 2)),
            pltpu.SemaphoreType.DMA(()),
        ],
        compiler_params=pltpu.CompilerParams(collective_id=0, has_side_effects=True),
    )(packed)


def combine(parts):
    top = jnp.max(parts[:, 0], axis=0)
    factor = jnp.exp(parts[:, 0] - top[None])
    total = jnp.sum(parts[:, 1] * factor, axis=0)
    weighted = jnp.sum(parts[:, 2] * factor, axis=0)
    picked = jnp.sum(parts[:, 3], axis=0)
    return jnp.stack([top, total, weighted, picked], axis=0)


def reduce_kernel(sizes, a_ref, out_ref, r1, c1, r2, c2, r3, send_sem, recv_sem):
    pos = {a: lax.axis_index(a) for a in AXES}

    def peer(axis, k):
        at = dict(pos)
        at[axis] = lax.rem(pos[axis] + k, sizes[axis])
        return tuple(at[a] for a in AXES)

    barrier = pltpu.get_barrier_semaphore()
    count = 0
    for axis in CHIP_AXES:
        for k in range(1, sizes[axis]):
            pl.semaphore_signal(barrier, inc=1, device_id=peer(axis, k), device_id_type=pl.DeviceIdType.MESH)
            count += 1
    pl.semaphore_wait(barrier, count)

    sends = []

    def stage(t, axis, src_of, land):
        n = sizes[axis]
        for k in range(1, n):
            copy = pltpu.make_async_remote_copy(
                src_ref=src_of(lax.rem(pos[axis] + k, n)), dst_ref=land.at[pos[axis]],
                send_sem=send_sem.at[t, k], recv_sem=recv_sem.at[t, (n - k) % n],
                device_id=peer(axis, k), device_id_type=pl.DeviceIdType.MESH,
            )
            copy.start()
            sends.append(copy)
        for j in range(1, n):
            slot = land.at[lax.rem(pos[axis] + j, n)]
            pltpu.make_async_remote_copy(
                src_ref=slot, dst_ref=slot, send_sem=send_sem.at[t, j], recv_sem=recv_sem.at[t, j],
                device_id=peer(axis, j), device_id_type=pl.DeviceIdType.MESH,
            ).wait_recv()

    r1[pos["y"]] = a_ref[pos["y"]]
    stage(0, "y", lambda i: a_ref.at[i], r1)
    c1[...] = combine(r1[...])
    own_x = pl.multiple_of(pos["x"] * LANES, LANES)
    r2[pos["x"]] = c1[:, pl.ds(own_x, LANES)]
    stage(1, "x", lambda i: c1.at[:, pl.ds(pl.multiple_of(i * LANES, LANES), LANES)], r2)
    c2[...] = combine(r2[...])
    r3[pos["z"]] = c2[...]
    stage(2, "z", lambda i: c2, r3)
    out_ref[...] = combine(r3[...])
    for copy in sends:
        copy.wait_send()


def reduce_stats(parts, sizes):
    ny, nx, nz = sizes["y"], sizes["x"], sizes["z"]
    longest = max(ny, nx, nz)
    width = parts.shape[-1]
    return pl.pallas_call(
        functools.partial(reduce_kernel, sizes),
        out_shape=jax.ShapeDtypeStruct((4, LANES), jnp.float32),
        scratch_shapes=[
            pltpu.VMEM((ny, 4, width), jnp.float32),
            pltpu.VMEM((4, width), jnp.float32),
            pltpu.VMEM((nx, 4, LANES), jnp.float32),
            pltpu.VMEM((4, LANES), jnp.float32),
            pltpu.VMEM((nz, 4, LANES), jnp.float32),
            pltpu.SemaphoreType.DMA((3, longest)),
            pltpu.SemaphoreType.DMA((3, longest)),
        ],
        compiler_params=pltpu.CompilerParams(collective_id=1, has_side_effects=True),
    )(parts)


def pack_kernel(h_ref, gain_ref, ids_ref, out_ref):
    values = h_ref[...].astype(jnp.float32)
    rows, width = values.shape
    scale = lax.rsqrt(jnp.mean(values * values, axis=-1, keepdims=True) + EPS)
    out_ref[:, :width] = (values * scale * gain_ref[...][None, :]).astype(jnp.bfloat16)
    row = lax.broadcasted_iota(jnp.int32, (rows, LANES), 0)
    lane = lax.broadcasted_iota(jnp.int32, (rows, LANES), 1)
    digit = jnp.zeros((rows, LANES), jnp.int32)
    for r in range(rows):
        v = ids_ref[r]
        for i, d in enumerate((v // (DIGIT * DIGIT), (v // DIGIT) % DIGIT, v % DIGIT)):
            digit = jnp.where((row == r) & (lane == i), d, digit)
    out_ref[:, width:] = digit.astype(jnp.float32).astype(jnp.bfloat16)


def pack_rows(hidden, norm_gain, token_ids):
    rows, width = hidden.shape
    return pl.pallas_call(
        pack_kernel,
        out_shape=jax.ShapeDtypeStruct((rows, width + LANES), jnp.bfloat16),
        in_specs=[
            pl.BlockSpec(memory_space=pltpu.VMEM),
            pl.BlockSpec(memory_space=pltpu.VMEM),
            pl.BlockSpec(memory_space=pltpu.SMEM),
        ],
    )(hidden, norm_gain, token_ids)


def body(hidden, norm_gain, head, token_ids, req_len, req_owner):
    local_rows, width = hidden.shape
    columns = head.shape[1]
    size = {a: lax.axis_size(a) for a in AXES}
    pos = {a: lax.axis_index(a) for a in AXES}
    chip = (pos["z"] * size["x"] + pos["x"]) * size["y"] + pos["y"]
    core = pos["core"]
    me = chip * size["core"] + core

    packed = pack_rows(hidden, norm_gain, token_ids)

    other = lax.ppermute(head, "core", [(0, 1), (1, 0)])
    chip_head = jnp.where(core == 0, jnp.concatenate([head, other], axis=1), jnp.concatenate([other, head], axis=1))
    col_index = chip * (2 * columns) + jnp.arange(2 * columns, dtype=jnp.int32)
    real_cols = col_index < VOCAB_REAL

    gathered = gather_rows(packed, size).reshape(-1, packed.shape[1])
    all_rows = gathered[:, :width]
    all_ids = decode_ids(gathered[:, width:width + 3])
    stats = jnp.stack(slice_stats(all_rows, all_ids, chip_head, col_index, real_cols), axis=0)

    parts = jnp.transpose(stats.reshape(4, size["y"], -1), (1, 0, 2))
    reduced = reduce_stats(parts, size)
    mine = lax.dynamic_slice_in_dim(reduced, pos["z"] * local_rows, local_rows, axis=1)
    top, total_all, weighted_all, picked_all = mine[0], mine[1], mine[2], mine[3]

    load = jnp.sum(jnp.where(req_owner == me, req_len, 0))
    live = jnp.arange(local_rows, dtype=jnp.int32) < load
    log_total = jnp.log(total_all)
    logprob = jnp.where(live, picked_all - top - log_total, 0.0)
    entropy = jnp.where(live, top + log_total - weighted_all / total_all, 0.0)
    return (logprob, entropy)


def solution(mesh):
    split = Mesh(mesh.devices.reshape(8, 4, 4, 2), AXES)
    placed = (P(AXES, None), P(), P(None, AXES), P(AXES), P(), P())
    return jax.shard_map(
        body, mesh=split, in_specs=placed, out_specs=(P(AXES), P(AXES)), check_vma=False
    )
```

```python
import functools

import jax
import jax.numpy as jnp
from jax import lax
from jax.experimental import pallas as pl
from jax.experimental.pallas import tpu as pltpu
from jax.sharding import Mesh, PartitionSpec as P

VOCAB_REAL = 73448


EPS = 1e-05
NEG = -1e30
DIGIT = 64
AXES = ("z", "x", "y", "core")
CHIP_AXES = ("z", "x", "y")


def slice_stats(rows, chosen, head, col_index, real_cols):
    logits = jnp.dot(rows, head, preferred_element_type=jnp.float32) / 10.0
    logits = jnp.where(real_cols[None, :], logits, NEG)
    rowmax = jnp.max(logits, axis=1)
    expo = jnp.where(real_cols[None, :], jnp.exp(logits - rowmax[:, None]), 0.0)
    total = jnp.sum(expo, axis=1)
    weighted = jnp.sum(jnp.where(real_cols[None, :], expo * logits, 0.0), axis=1)
    picked = jnp.sum(jnp.where(col_index[None, :] == chosen[:, None], logits, 0.0), axis=1)
    return (rowmax, total, weighted, picked)


def code_ids(ids):
    digits = [ids // (DIGIT * DIGIT), (ids // DIGIT) % DIGIT, ids % DIGIT]
    return jnp.stack(digits, axis=1).astype(jnp.bfloat16)


def decode_ids(coded):
    d = coded.astype(jnp.int32)
    return (d[:, 0] * DIGIT + d[:, 1]) * DIGIT + d[:, 2]


STREAMS = (("z", "x", "y"), ("x", "y", "z"), ("y", "z", "x"))
LANES = 128


def gather_kernel(sizes, spans, x_ref, g_ref, send_sem, recv_sem, own_sem):
    pos = {a: lax.axis_index(a) for a in AXES}

    def peer(axis, k):
        at = dict(pos)
        at[axis] = lax.rem(pos[axis] + k + sizes[axis], sizes[axis])
        return tuple(at[a] for a in AXES)

    def view(ref, held, axis, k, cols):
        idx = []
        for a in ("y", "x", "z"):
            if a in held:
                idx.append(slice(None))
            elif a == axis:
                idx.append(lax.rem(pos[a] + k + sizes[a], sizes[a]))
            else:
                idx.append(pos[a])
        return ref.at[tuple(idx) + (slice(None), cols)]

    barrier = pltpu.get_barrier_semaphore()
    count = 0
    for axis in CHIP_AXES:
        for k in (1, -1):
            pl.semaphore_signal(barrier, inc=1, device_id=peer(axis, k), device_id_type=pl.DeviceIdType.MESH)
            count += 1
    pl.semaphore_wait(barrier, count)

    own = pltpu.make_async_copy(x_ref, g_ref.at[pos["y"], pos["x"], pos["z"]], own_sem)
    own.start()

    plans = []
    for order in STREAMS:
        plan = []
        for t, axis in enumerate(order):
            n = sizes[axis]
            for q in range(1, n // 2 + 1):
                plan.append((t, axis, q, n % 2 == 0 and q == n // 2))
        plans.append(plan)

    def step_copies(s, step, sending):
        t, axis, q, split = plans[s][step]
        c0, w = spans[s]
        order = STREAMS[s]
        held = order[:t]
        if split:
            cut = (w // LANES // 2) * LANES
            col_of = [pl.ds(c0, cut), pl.ds(c0 + cut, w - cut)]
        else:
            col_of = [pl.ds(c0, w), pl.ds(c0, w)]
        out = []
        for d, sign in enumerate((1, -1)):
            cols = col_of[d]
            if sending:
                k = -sign * (q - 1)
                dst = view(g_ref, held, axis, k, cols)
                src = x_ref.at[:, cols] if (t == 0 and q == 1) else dst
                target = peer(axis, sign)
            else:
                k = -sign * q
                src = dst = view(g_ref, held, axis, k, cols)
                target = peer(axis, -sign)
            out.append(pltpu.make_async_remote_copy(
                src_ref=src, dst_ref=dst, send_sem=send_sem.at[s, step, d],
                recv_sem=recv_sem.at[s, step, d], device_id=target,
                device_id_type=pl.DeviceIdType.MESH,
            ))
        return out

    steps = len(plans[0])
    sends = []
    for g in range(steps):
        for s in range(len(STREAMS)):
            if g > 0:
                for copy in step_copies(s, g - 1, False):
                    copy.wait_recv()
            if g == 1 and s == 0:
                own.wait()
            for copy in step_copies(s, g, True):
                copy.start()
                sends.append(copy)
    for s in range(len(STREAMS)):
        for copy in step_copies(s, steps - 1, False):
            copy.wait_recv()
    for copy in sends:
        copy.wait_send()


def gather_rows(packed, sizes):
    rows, width = packed.shape
    tiles = width // LANES
    counts = [tiles * 10 // 21, tiles * 4 // 21]
    counts.append(tiles - sum(counts))
    spans, at = [], 0
    for c in counts:
        spans.append((at * LANES, c * LANES))
        at += c
    shape = (sizes["y"], sizes["x"], sizes["z"], rows, width)
    steps = sum(sizes[a] // 2 for a in CHIP_AXES)
    return pl.pallas_call(
        functools.partial(gather_kernel, sizes, spans),
        out_shape=jax.ShapeDtypeStruct(shape, packed.dtype),
        in_specs=[pl.BlockSpec(memory_space=pl.ANY)],
        out_specs=pl.BlockSpec(memory_space=pl.ANY),
        scratch_shapes=[
            pltpu.SemaphoreType.DMA((3, steps, 2)),
            pltpu.SemaphoreType.DMA((3, steps, 2)),
            pltpu.SemaphoreType.DMA(()),
        ],
        compiler_params=pltpu.CompilerParams(collective_id=0, has_side_effects=True),
    )(packed)


def combine(parts):
    top = jnp.max(parts[:, 0], axis=0)
    factor = jnp.exp(parts[:, 0] - top[None])
    total = jnp.sum(parts[:, 1] * factor, axis=0)
    weighted = jnp.sum(parts[:, 2] * factor, axis=0)
    picked = jnp.sum(parts[:, 3], axis=0)
    return jnp.stack([top, total, weighted, picked], axis=0)


def reduce_kernel(sizes, a_ref, out_ref, r1, c1, r2, c2, r3, send_sem, recv_sem):
    pos = {a: lax.axis_index(a) for a in AXES}

    def peer(axis, k):
        at = dict(pos)
        at[axis] = lax.rem(pos[axis] + k, sizes[axis])
        return tuple(at[a] for a in AXES)

    barrier = pltpu.get_barrier_semaphore()
    count = 0
    for axis in CHIP_AXES:
        for k in range(1, sizes[axis]):
            pl.semaphore_signal(barrier, inc=1, device_id=peer(axis, k), device_id_type=pl.DeviceIdType.MESH)
            count += 1
    pl.semaphore_wait(barrier, count)

    sends = []

    def stage(t, axis, src_of, land):
        n = sizes[axis]
        for k in range(1, n):
            copy = pltpu.make_async_remote_copy(
                src_ref=src_of(lax.rem(pos[axis] + k, n)), dst_ref=land.at[pos[axis]],
                send_sem=send_sem.at[t, k], recv_sem=recv_sem.at[t, (n - k) % n],
                device_id=peer(axis, k), device_id_type=pl.DeviceIdType.MESH,
            )
            copy.start()
            sends.append(copy)
        for j in range(1, n):
            slot = land.at[lax.rem(pos[axis] + j, n)]
            pltpu.make_async_remote_copy(
                src_ref=slot, dst_ref=slot, send_sem=send_sem.at[t, j], recv_sem=recv_sem.at[t, j],
                device_id=peer(axis, j), device_id_type=pl.DeviceIdType.MESH,
            ).wait_recv()

    r1[pos["y"]] = a_ref[pos["y"]]
    stage(0, "y", lambda i: a_ref.at[i], r1)
    c1[...] = combine(r1[...])
    own_x = pl.multiple_of(pos["x"] * LANES, LANES)
    r2[pos["x"]] = c1[:, pl.ds(own_x, LANES)]
    stage(1, "x", lambda i: c1.at[:, pl.ds(pl.multiple_of(i * LANES, LANES), LANES)], r2)
    c2[...] = combine(r2[...])
    r3[pos["z"]] = c2[...]
    stage(2, "z", lambda i: c2, r3)
    out_ref[...] = combine(r3[...])
    for copy in sends:
        copy.wait_send()


def reduce_stats(parts, sizes):
    ny, nx, nz = sizes["y"], sizes["x"], sizes["z"]
    longest = max(ny, nx, nz)
    width = parts.shape[-1]
    return pl.pallas_call(
        functools.partial(reduce_kernel, sizes),
        out_shape=jax.ShapeDtypeStruct((4, LANES), jnp.float32),
        scratch_shapes=[
            pltpu.VMEM((ny, 4, width), jnp.float32),
            pltpu.VMEM((4, width), jnp.float32),
            pltpu.VMEM((nx, 4, LANES), jnp.float32),
            pltpu.VMEM((4, LANES), jnp.float32),
            pltpu.VMEM((nz, 4, LANES), jnp.float32),
            pltpu.SemaphoreType.DMA((3, longest)),
            pltpu.SemaphoreType.DMA((3, longest)),
        ],
        compiler_params=pltpu.CompilerParams(collective_id=1, has_side_effects=True),
    )(parts)


def pack_kernel(h_ref, gain_ref, ids_ref, out_ref):
    values = h_ref[...].astype(jnp.float32)
    rows, width = values.shape
    scale = lax.rsqrt(jnp.mean(values * values, axis=-1, keepdims=True) + EPS)
    out_ref[:, :width] = (values * scale * gain_ref[...][None, :]).astype(jnp.bfloat16)
    row = lax.broadcasted_iota(jnp.int32, (rows, LANES), 0)
    lane = lax.broadcasted_iota(jnp.int32, (rows, LANES), 1)
    digit = jnp.zeros((rows, LANES), jnp.int32)
    for r in range(rows):
        v = ids_ref[r]
        for i, d in enumerate((v // (DIGIT * DIGIT), (v // DIGIT) % DIGIT, v % DIGIT)):
            digit = jnp.where((row == r) & (lane == i), d, digit)
    out_ref[:, width:] = digit.astype(jnp.float32).astype(jnp.bfloat16)


def pack_rows(hidden, norm_gain, token_ids):
    rows, width = hidden.shape
    return pl.pallas_call(
        pack_kernel,
        out_shape=jax.ShapeDtypeStruct((rows, width + LANES), jnp.bfloat16),
        in_specs=[
            pl.BlockSpec(memory_space=pltpu.VMEM),
            pl.BlockSpec(memory_space=pltpu.VMEM),
            pl.BlockSpec(memory_space=pltpu.SMEM),
        ],
    )(hidden, norm_gain, token_ids)


def body(hidden, norm_gain, head, token_ids, req_len, req_owner):
    local_rows, width = hidden.shape
    columns = head.shape[1]
    size = {a: lax.axis_size(a) for a in AXES}
    pos = {a: lax.axis_index(a) for a in AXES}
    chip = (pos["z"] * size["x"] + pos["x"]) * size["y"] + pos["y"]
    core = pos["core"]
    me = chip * size["core"] + core

    packed = pack_rows(hidden, norm_gain, token_ids)

    other = lax.ppermute(head, "core", [(0, 1), (1, 0)])
    chip_head = jnp.where(core == 0, jnp.concatenate([head, other], axis=1), jnp.concatenate([other, head], axis=1))
    col_index = chip * (2 * columns) + jnp.arange(2 * columns, dtype=jnp.int32)
    real_cols = col_index < VOCAB_REAL

    gathered = gather_rows(packed, size).reshape(-1, packed.shape[1])
    all_rows = gathered[:, :width]
    all_ids = decode_ids(gathered[:, width:width + 3])
    stats = jnp.stack(slice_stats(all_rows, all_ids, chip_head, col_index, real_cols), axis=0)

    parts = jnp.transpose(stats.reshape(4, size["y"], -1), (1, 0, 2))
    reduced = reduce_stats(parts, size)
    mine = lax.dynamic_slice_in_dim(reduced, pos["z"] * local_rows, local_rows, axis=1)
    top, total_all, weighted_all, picked_all = mine[0], mine[1], mine[2], mine[3]

    load = jnp.sum(jnp.where(req_owner == me, req_len, 0))
    live = jnp.arange(local_rows, dtype=jnp.int32) < load
    log_total = jnp.log(total_all)
    logprob = jnp.where(live, picked_all - top - log_total, 0.0)
    entropy = jnp.where(live, top + log_total - weighted_all / total_all, 0.0)
    return (logprob, entropy)


def solution(mesh):
    split = Mesh(mesh.devices.reshape(8, 4, 4, 2), AXES)
    placed = (P(AXES, None), P(), P(None, AXES), P(AXES), P(), P())
    return jax.shard_map(
        body, mesh=split, in_specs=placed, out_specs=(P(AXES), P(AXES)), check_vma=False
    )
```

```python
import functools

import jax
import jax.numpy as jnp
from jax import lax
from jax.experimental import pallas as pl
from jax.experimental.pallas import tpu as pltpu
from jax.sharding import Mesh, PartitionSpec as P

VOCAB_REAL = 73448


EPS = 1e-05
NEG = -1e30
DIGIT = 64
AXES = ("z", "x", "y", "core")
CHIP_AXES = ("z", "x", "y")


def slice_stats(rows, chosen, head, col_index, real_cols):
    logits = jnp.dot(rows, head, preferred_element_type=jnp.float32) / 10.0
    logits = jnp.where(real_cols[None, :], logits, NEG)
    rowmax = jnp.max(logits, axis=1)
    expo = jnp.where(real_cols[None, :], jnp.exp(logits - rowmax[:, None]), 0.0)
    total = jnp.sum(expo, axis=1)
    weighted = jnp.sum(jnp.where(real_cols[None, :], expo * logits, 0.0), axis=1)
    picked = jnp.sum(jnp.where(col_index[None, :] == chosen[:, None], logits, 0.0), axis=1)
    return (rowmax, total, weighted, picked)


def code_ids(ids):
    digits = [ids // (DIGIT * DIGIT), (ids // DIGIT) % DIGIT, ids % DIGIT]
    return jnp.stack(digits, axis=1).astype(jnp.bfloat16)


def decode_ids(coded):
    d = coded.astype(jnp.int32)
    return (d[:, 0] * DIGIT + d[:, 1]) * DIGIT + d[:, 2]


STREAMS = (("z", "x", "y"), ("x", "y", "z"), ("y", "z", "x"))
LANES = 128


def gather_kernel(sizes, spans, x_ref, g_ref, send_sem, recv_sem, own_sem):
    pos = {a: lax.axis_index(a) for a in AXES}

    def peer(axis, k):
        at = dict(pos)
        at[axis] = lax.rem(pos[axis] + k + sizes[axis], sizes[axis])
        return tuple(at[a] for a in AXES)

    def view(ref, held, axis, k, cols):
        idx = []
        for a in ("y", "x", "z"):
            if a in held:
                idx.append(slice(None))
            elif a == axis:
                idx.append(lax.rem(pos[a] + k + sizes[a], sizes[a]))
            else:
                idx.append(pos[a])
        return ref.at[tuple(idx) + (slice(None), cols)]

    barrier = pltpu.get_barrier_semaphore()
    count = 0
    for axis in CHIP_AXES:
        for k in (1, -1):
            pl.semaphore_signal(barrier, inc=1, device_id=peer(axis, k), device_id_type=pl.DeviceIdType.MESH)
            count += 1
    pl.semaphore_wait(barrier, count)

    own = pltpu.make_async_copy(x_ref, g_ref.at[pos["y"], pos["x"], pos["z"]], own_sem)
    own.start()

    plans = []
    for order in STREAMS:
        plan = []
        for t, axis in enumerate(order):
            n = sizes[axis]
            for q in range(1, n // 2 + 1):
                plan.append((t, axis, q, n % 2 == 0 and q == n // 2))
        plans.append(plan)

    def step_copies(s, step, sending):
        t, axis, q, split = plans[s][step]
        c0, w = spans[s]
        order = STREAMS[s]
        held = order[:t]
        if split:
            cut = (w // LANES // 2) * LANES
            col_of = [pl.ds(c0, cut), pl.ds(c0 + cut, w - cut)]
        else:
            col_of = [pl.ds(c0, w), pl.ds(c0, w)]
        out = []
        for d, sign in enumerate((1, -1)):
            cols = col_of[d]
            if sending:
                k = -sign * (q - 1)
                dst = view(g_ref, held, axis, k, cols)
                src = x_ref.at[:, cols] if (t == 0 and q == 1) else dst
                target = peer(axis, sign)
            else:
                k = -sign * q
                src = dst = view(g_ref, held, axis, k, cols)
                target = peer(axis, -sign)
            out.append(pltpu.make_async_remote_copy(
                src_ref=src, dst_ref=dst, send_sem=send_sem.at[s, step, d],
                recv_sem=recv_sem.at[s, step, d], device_id=target,
                device_id_type=pl.DeviceIdType.MESH,
            ))
        return out

    steps = len(plans[0])
    sends = []
    for g in range(steps):
        for s in range(len(STREAMS)):
            if g > 0:
                for copy in step_copies(s, g - 1, False):
                    copy.wait_recv()
            if g == 1 and s == 0:
                own.wait()
            for copy in step_copies(s, g, True):
                copy.start()
                sends.append(copy)
    for s in range(len(STREAMS)):
        for copy in step_copies(s, steps - 1, False):
            copy.wait_recv()
    for copy in sends:
        copy.wait_send()


def gather_rows(packed, sizes):
    rows, width = packed.shape
    tiles = width // LANES
    counts = [tiles * 8 // 21, tiles * 5 // 21]
    counts.append(tiles - sum(counts))
    spans, at = [], 0
    for c in counts:
        spans.append((at * LANES, c * LANES))
        at += c
    shape = (sizes["y"], sizes["x"], sizes["z"], rows, width)
    steps = sum(sizes[a] // 2 for a in CHIP_AXES)
    return pl.pallas_call(
        functools.partial(gather_kernel, sizes, spans),
        out_shape=jax.ShapeDtypeStruct(shape, packed.dtype),
        in_specs=[pl.BlockSpec(memory_space=pl.ANY)],
        out_specs=pl.BlockSpec(memory_space=pl.ANY),
        scratch_shapes=[
            pltpu.SemaphoreType.DMA((3, steps, 2)),
            pltpu.SemaphoreType.DMA((3, steps, 2)),
            pltpu.SemaphoreType.DMA(()),
        ],
        compiler_params=pltpu.CompilerParams(collective_id=0, has_side_effects=True),
    )(packed)


def combine(parts):
    top = jnp.max(parts[:, 0], axis=0)
    factor = jnp.exp(parts[:, 0] - top[None])
    total = jnp.sum(parts[:, 1] * factor, axis=0)
    weighted = jnp.sum(parts[:, 2] * factor, axis=0)
    picked = jnp.sum(parts[:, 3], axis=0)
    return jnp.stack([top, total, weighted, picked], axis=0)


def reduce_kernel(sizes, a_ref, out_ref, r1, c1, r2, c2, r3, send_sem, recv_sem):
    pos = {a: lax.axis_index(a) for a in AXES}

    def peer(axis, k):
        at = dict(pos)
        at[axis] = lax.rem(pos[axis] + k, sizes[axis])
        return tuple(at[a] for a in AXES)

    barrier = pltpu.get_barrier_semaphore()
    count = 0
    for axis in CHIP_AXES:
        for k in range(1, sizes[axis]):
            pl.semaphore_signal(barrier, inc=1, device_id=peer(axis, k), device_id_type=pl.DeviceIdType.MESH)
            count += 1
    pl.semaphore_wait(barrier, count)

    sends = []

    def stage(t, axis, src_of, land):
        n = sizes[axis]
        for k in range(1, n):
            copy = pltpu.make_async_remote_copy(
                src_ref=src_of(lax.rem(pos[axis] + k, n)), dst_ref=land.at[pos[axis]],
                send_sem=send_sem.at[t, k], recv_sem=recv_sem.at[t, (n - k) % n],
                device_id=peer(axis, k), device_id_type=pl.DeviceIdType.MESH,
            )
            copy.start()
            sends.append(copy)
        for j in range(1, n):
            slot = land.at[lax.rem(pos[axis] + j, n)]
            pltpu.make_async_remote_copy(
                src_ref=slot, dst_ref=slot, send_sem=send_sem.at[t, j], recv_sem=recv_sem.at[t, j],
                device_id=peer(axis, j), device_id_type=pl.DeviceIdType.MESH,
            ).wait_recv()

    r1[pos["y"]] = a_ref[pos["y"]]
    stage(0, "y", lambda i: a_ref.at[i], r1)
    c1[...] = combine(r1[...])
    own_x = pl.multiple_of(pos["x"] * LANES, LANES)
    r2[pos["x"]] = c1[:, pl.ds(own_x, LANES)]
    stage(1, "x", lambda i: c1.at[:, pl.ds(pl.multiple_of(i * LANES, LANES), LANES)], r2)
    c2[...] = combine(r2[...])
    r3[pos["z"]] = c2[...]
    stage(2, "z", lambda i: c2, r3)
    out_ref[...] = combine(r3[...])
    for copy in sends:
        copy.wait_send()


def reduce_stats(parts, sizes):
    ny, nx, nz = sizes["y"], sizes["x"], sizes["z"]
    longest = max(ny, nx, nz)
    width = parts.shape[-1]
    return pl.pallas_call(
        functools.partial(reduce_kernel, sizes),
        out_shape=jax.ShapeDtypeStruct((4, LANES), jnp.float32),
        scratch_shapes=[
            pltpu.VMEM((ny, 4, width), jnp.float32),
            pltpu.VMEM((4, width), jnp.float32),
            pltpu.VMEM((nx, 4, LANES), jnp.float32),
            pltpu.VMEM((4, LANES), jnp.float32),
            pltpu.VMEM((nz, 4, LANES), jnp.float32),
            pltpu.SemaphoreType.DMA((3, longest)),
            pltpu.SemaphoreType.DMA((3, longest)),
        ],
        compiler_params=pltpu.CompilerParams(collective_id=1, has_side_effects=True),
    )(parts)


def pack_kernel(h_ref, gain_ref, ids_ref, out_ref):
    values = h_ref[...].astype(jnp.float32)
    rows, width = values.shape
    scale = lax.rsqrt(jnp.mean(values * values, axis=-1, keepdims=True) + EPS)
    out_ref[:, :width] = (values * scale * gain_ref[...][None, :]).astype(jnp.bfloat16)
    row = lax.broadcasted_iota(jnp.int32, (rows, LANES), 0)
    lane = lax.broadcasted_iota(jnp.int32, (rows, LANES), 1)
    digit = jnp.zeros((rows, LANES), jnp.int32)
    for r in range(rows):
        v = ids_ref[r]
        for i, d in enumerate((v // (DIGIT * DIGIT), (v // DIGIT) % DIGIT, v % DIGIT)):
            digit = jnp.where((row == r) & (lane == i), d, digit)
    out_ref[:, width:] = digit.astype(jnp.float32).astype(jnp.bfloat16)


def pack_rows(hidden, norm_gain, token_ids):
    rows, width = hidden.shape
    return pl.pallas_call(
        pack_kernel,
        out_shape=jax.ShapeDtypeStruct((rows, width + LANES), jnp.bfloat16),
        in_specs=[
            pl.BlockSpec(memory_space=pltpu.VMEM),
            pl.BlockSpec(memory_space=pltpu.VMEM),
            pl.BlockSpec(memory_space=pltpu.SMEM),
        ],
    )(hidden, norm_gain, token_ids)


def body(hidden, norm_gain, head, token_ids, req_len, req_owner):
    local_rows, width = hidden.shape
    columns = head.shape[1]
    size = {a: lax.axis_size(a) for a in AXES}
    pos = {a: lax.axis_index(a) for a in AXES}
    chip = (pos["z"] * size["x"] + pos["x"]) * size["y"] + pos["y"]
    core = pos["core"]
    me = chip * size["core"] + core

    packed = pack_rows(hidden, norm_gain, token_ids)

    other = lax.ppermute(head, "core", [(0, 1), (1, 0)])
    chip_head = jnp.where(core == 0, jnp.concatenate([head, other], axis=1), jnp.concatenate([other, head], axis=1))
    col_index = chip * (2 * columns) + jnp.arange(2 * columns, dtype=jnp.int32)
    real_cols = col_index < VOCAB_REAL

    gathered = gather_rows(packed, size).reshape(-1, packed.shape[1])
    all_rows = gathered[:, :width]
    all_ids = decode_ids(gathered[:, width:width + 3])
    stats = jnp.stack(slice_stats(all_rows, all_ids, chip_head, col_index, real_cols), axis=0)

    parts = jnp.transpose(stats.reshape(4, size["y"], -1), (1, 0, 2))
    reduced = reduce_stats(parts, size)
    mine = lax.dynamic_slice_in_dim(reduced, pos["z"] * local_rows, local_rows, axis=1)
    top, total_all, weighted_all, picked_all = mine[0], mine[1], mine[2], mine[3]

    load = jnp.sum(jnp.where(req_owner == me, req_len, 0))
    live = jnp.arange(local_rows, dtype=jnp.int32) < load
    log_total = jnp.log(total_all)
    logprob = jnp.where(live, picked_all - top - log_total, 0.0)
    entropy = jnp.where(live, top + log_total - weighted_all / total_all, 0.0)
    return (logprob, entropy)


def solution(mesh):
    split = Mesh(mesh.devices.reshape(8, 4, 4, 2), AXES)
    placed = (P(AXES, None), P(), P(None, AXES), P(AXES), P(), P())
    return jax.shard_map(
        body, mesh=split, in_specs=placed, out_specs=(P(AXES), P(AXES)), check_vma=False
    )
```

```python
import functools

import jax
import jax.numpy as jnp
from jax import lax
from jax.experimental import pallas as pl
from jax.experimental.pallas import tpu as pltpu
from jax.sharding import Mesh, PartitionSpec as P

VOCAB_REAL = 73448


EPS = 1e-05
NEG = -1e30
DIGIT = 64
AXES = ("z", "x", "y", "core")
CHIP_AXES = ("z", "x", "y")


def slice_stats(rows, chosen, head, col_index, real_cols):
    logits = jnp.dot(rows, head, preferred_element_type=jnp.float32) / 10.0
    logits = jnp.where(real_cols[None, :], logits, NEG)
    rowmax = jnp.max(logits, axis=1)
    expo = jnp.where(real_cols[None, :], jnp.exp(logits - rowmax[:, None]), 0.0)
    total = jnp.sum(expo, axis=1)
    weighted = jnp.sum(jnp.where(real_cols[None, :], expo * logits, 0.0), axis=1)
    picked = jnp.sum(jnp.where(col_index[None, :] == chosen[:, None], logits, 0.0), axis=1)
    return (rowmax, total, weighted, picked)


def code_ids(ids):
    digits = [ids // (DIGIT * DIGIT), (ids // DIGIT) % DIGIT, ids % DIGIT]
    return jnp.stack(digits, axis=1).astype(jnp.bfloat16)


def decode_ids(coded):
    d = coded.astype(jnp.int32)
    return (d[:, 0] * DIGIT + d[:, 1]) * DIGIT + d[:, 2]


STREAMS = (("z", "x", "y"), ("x", "y", "z"), ("y", "z", "x"))
LANES = 128


def gather_kernel(sizes, spans, x_ref, g_ref, send_sem, recv_sem, own_sem):
    pos = {a: lax.axis_index(a) for a in AXES}

    def peer(axis, k):
        at = dict(pos)
        at[axis] = lax.rem(pos[axis] + k + sizes[axis], sizes[axis])
        return tuple(at[a] for a in AXES)

    def view(ref, held, axis, k, cols):
        idx = []
        for a in ("y", "x", "z"):
            if a in held:
                idx.append(slice(None))
            elif a == axis:
                idx.append(lax.rem(pos[a] + k + sizes[a], sizes[a]))
            else:
                idx.append(pos[a])
        return ref.at[tuple(idx) + (slice(None), cols)]

    barrier = pltpu.get_barrier_semaphore()
    count = 0
    for axis in CHIP_AXES:
        for k in (1, -1):
            pl.semaphore_signal(barrier, inc=1, device_id=peer(axis, k), device_id_type=pl.DeviceIdType.MESH)
            count += 1
    pl.semaphore_wait(barrier, count)

    own = pltpu.make_async_copy(x_ref, g_ref.at[pos["y"], pos["x"], pos["z"]], own_sem)
    own.start()

    plans = []
    for order in STREAMS:
        plan = []
        for t, axis in enumerate(order):
            n = sizes[axis]
            for q in range(1, n // 2 + 1):
                plan.append((t, axis, q, n % 2 == 0 and q == n // 2))
        plans.append(plan)

    def step_copies(s, step, sending):
        t, axis, q, split = plans[s][step]
        c0, w = spans[s]
        order = STREAMS[s]
        held = order[:t]
        if split:
            cut = (w // LANES // 2) * LANES
            col_of = [pl.ds(c0, cut), pl.ds(c0 + cut, w - cut)]
        else:
            col_of = [pl.ds(c0, w), pl.ds(c0, w)]
        out = []
        for d, sign in enumerate((1, -1)):
            cols = col_of[d]
            if sending:
                k = -sign * (q - 1)
                dst = view(g_ref, held, axis, k, cols)
                src = x_ref.at[:, cols] if (t == 0 and q == 1) else dst
                target = peer(axis, sign)
            else:
                k = -sign * q
                src = dst = view(g_ref, held, axis, k, cols)
                target = peer(axis, -sign)
            out.append(pltpu.make_async_remote_copy(
                src_ref=src, dst_ref=dst, send_sem=send_sem.at[s, step, d],
                recv_sem=recv_sem.at[s, step, d], device_id=target,
                device_id_type=pl.DeviceIdType.MESH,
            ))
        return out

    steps = len(plans[0])
    sends = []
    for g in range(steps):
        for s in range(len(STREAMS)):
            if g > 0:
                for copy in step_copies(s, g - 1, False):
                    copy.wait_recv()
            if g == 1 and s == 0:
                own.wait()
            for copy in step_copies(s, g, True):
                copy.start()
                sends.append(copy)
    for s in range(len(STREAMS)):
        for copy in step_copies(s, steps - 1, False):
            copy.wait_recv()
    for copy in sends:
        copy.wait_send()


def gather_rows(packed, sizes):
    rows, width = packed.shape
    tiles = width // LANES
    counts = [tiles * 9 // 21, tiles * 5 // 21]
    counts.append(tiles - sum(counts))
    spans, at = [], 0
    for c in counts:
        spans.append((at * LANES, c * LANES))
        at += c
    shape = (sizes["y"], sizes["x"], sizes["z"], rows, width)
    steps = sum(sizes[a] // 2 for a in CHIP_AXES)
    return pl.pallas_call(
        functools.partial(gather_kernel, sizes, spans),
        out_shape=jax.ShapeDtypeStruct(shape, packed.dtype),
        in_specs=[pl.BlockSpec(memory_space=pl.ANY)],
        out_specs=pl.BlockSpec(memory_space=pl.ANY),
        scratch_shapes=[
            pltpu.SemaphoreType.DMA((3, steps, 2)),
            pltpu.SemaphoreType.DMA((3, steps, 2)),
            pltpu.SemaphoreType.DMA(()),
        ],
        compiler_params=pltpu.CompilerParams(collective_id=0, has_side_effects=True),
    )(packed)


def combine(parts):
    top = jnp.max(parts[:, 0], axis=0)
    factor = jnp.exp(parts[:, 0] - top[None])
    total = jnp.sum(parts[:, 1] * factor, axis=0)
    weighted = jnp.sum(parts[:, 2] * factor, axis=0)
    picked = jnp.sum(parts[:, 3], axis=0)
    return jnp.stack([top, total, weighted, picked], axis=0)


def reduce_kernel(sizes, a_ref, out_ref, r1, c1, r2, c2, r3, send_sem, recv_sem):
    pos = {a: lax.axis_index(a) for a in AXES}

    def peer(axis, k):
        at = dict(pos)
        at[axis] = lax.rem(pos[axis] + k, sizes[axis])
        return tuple(at[a] for a in AXES)

    barrier = pltpu.get_barrier_semaphore()
    count = 0
    for axis in CHIP_AXES:
        for k in range(1, sizes[axis]):
            pl.semaphore_signal(barrier, inc=1, device_id=peer(axis, k), device_id_type=pl.DeviceIdType.MESH)
            count += 1
    pl.semaphore_wait(barrier, count)

    sends = []

    def stage(t, axis, src_of, land):
        n = sizes[axis]
        for k in range(1, n):
            copy = pltpu.make_async_remote_copy(
                src_ref=src_of(lax.rem(pos[axis] + k, n)), dst_ref=land.at[pos[axis]],
                send_sem=send_sem.at[t, k], recv_sem=recv_sem.at[t, (n - k) % n],
                device_id=peer(axis, k), device_id_type=pl.DeviceIdType.MESH,
            )
            copy.start()
            sends.append(copy)
        for j in range(1, n):
            slot = land.at[lax.rem(pos[axis] + j, n)]
            pltpu.make_async_remote_copy(
                src_ref=slot, dst_ref=slot, send_sem=send_sem.at[t, j], recv_sem=recv_sem.at[t, j],
                device_id=peer(axis, j), device_id_type=pl.DeviceIdType.MESH,
            ).wait_recv()

    r1[pos["y"]] = a_ref[pos["y"]]
    stage(0, "y", lambda i: a_ref.at[i], r1)
    c1[...] = combine(r1[...])
    own_x = pl.multiple_of(pos["x"] * LANES, LANES)
    r2[pos["x"]] = c1[:, pl.ds(own_x, LANES)]
    stage(1, "x", lambda i: c1.at[:, pl.ds(pl.multiple_of(i * LANES, LANES), LANES)], r2)
    c2[...] = combine(r2[...])
    r3[pos["z"]] = c2[...]
    stage(2, "z", lambda i: c2, r3)
    out_ref[...] = combine(r3[...])
    for copy in sends:
        copy.wait_send()


def reduce_stats(parts, sizes):
    ny, nx, nz = sizes["y"], sizes["x"], sizes["z"]
    longest = max(ny, nx, nz)
    width = parts.shape[-1]
    return pl.pallas_call(
        functools.partial(reduce_kernel, sizes),
        out_shape=jax.ShapeDtypeStruct((4, LANES), jnp.float32),
        scratch_shapes=[
            pltpu.VMEM((ny, 4, width), jnp.float32),
            pltpu.VMEM((4, width), jnp.float32),
            pltpu.VMEM((nx, 4, LANES), jnp.float32),
            pltpu.VMEM((4, LANES), jnp.float32),
            pltpu.VMEM((nz, 4, LANES), jnp.float32),
            pltpu.SemaphoreType.DMA((3, longest)),
            pltpu.SemaphoreType.DMA((3, longest)),
        ],
        compiler_params=pltpu.CompilerParams(collective_id=1, has_side_effects=True),
    )(parts)


def pack_kernel(h_ref, gain_ref, ids_ref, out_ref):
    values = h_ref[...].astype(jnp.float32)
    rows, width = values.shape
    scale = lax.rsqrt(jnp.mean(values * values, axis=-1, keepdims=True) + EPS)
    out_ref[:, :width] = (values * scale * gain_ref[...][None, :]).astype(jnp.bfloat16)
    row = lax.broadcasted_iota(jnp.int32, (rows, LANES), 0)
    lane = lax.broadcasted_iota(jnp.int32, (rows, LANES), 1)
    digit = jnp.zeros((rows, LANES), jnp.int32)
    for r in range(rows):
        v = ids_ref[r]
        for i, d in enumerate((v // (DIGIT * DIGIT), (v // DIGIT) % DIGIT, v % DIGIT)):
            digit = jnp.where((row == r) & (lane == i), d, digit)
    out_ref[:, width:] = digit.astype(jnp.float32).astype(jnp.bfloat16)


def pack_rows(hidden, norm_gain, token_ids):
    rows, width = hidden.shape
    return pl.pallas_call(
        pack_kernel,
        out_shape=jax.ShapeDtypeStruct((rows, width + LANES), jnp.bfloat16),
        in_specs=[
            pl.BlockSpec(memory_space=pltpu.VMEM),
            pl.BlockSpec(memory_space=pltpu.VMEM),
            pl.BlockSpec(memory_space=pltpu.SMEM),
        ],
    )(hidden, norm_gain, token_ids)


def body(hidden, norm_gain, head, token_ids, req_len, req_owner):
    local_rows, width = hidden.shape
    columns = head.shape[1]
    size = {a: lax.axis_size(a) for a in AXES}
    pos = {a: lax.axis_index(a) for a in AXES}
    chip = (pos["z"] * size["x"] + pos["x"]) * size["y"] + pos["y"]
    core = pos["core"]
    me = chip * size["core"] + core

    packed = pack_rows(hidden, norm_gain, token_ids)

    other = lax.ppermute(head, "core", [(0, 1), (1, 0)])
    chip_head = jnp.where(core == 0, jnp.concatenate([head, other], axis=1), jnp.concatenate([other, head], axis=1))
    col_index = chip * (2 * columns) + jnp.arange(2 * columns, dtype=jnp.int32)
    real_cols = col_index < VOCAB_REAL

    gathered = gather_rows(packed, size).reshape(-1, packed.shape[1])
    all_rows = gathered[:, :width]
    place = jnp.zeros((gathered.shape[1] - width,), jnp.bfloat16).at[:3].set(jnp.array([DIGIT * DIGIT, DIGIT, 1], jnp.bfloat16))
    all_ids = jnp.dot(gathered[:, width:], place, preferred_element_type=jnp.float32).astype(jnp.int32)
    stats = jnp.stack(slice_stats(all_rows, all_ids, chip_head, col_index, real_cols), axis=0)

    parts = jnp.transpose(stats.reshape(4, size["y"], -1), (1, 0, 2))
    reduced = reduce_stats(parts, size)
    mine = lax.dynamic_slice_in_dim(reduced, pos["z"] * local_rows, local_rows, axis=1)
    top, total_all, weighted_all, picked_all = mine[0], mine[1], mine[2], mine[3]

    load = jnp.sum(jnp.where(req_owner == me, req_len, 0))
    live = jnp.arange(local_rows, dtype=jnp.int32) < load
    log_total = jnp.log(total_all)
    logprob = jnp.where(live, picked_all - top - log_total, 0.0)
    entropy = jnp.where(live, top + log_total - weighted_all / total_all, 0.0)
    return (logprob, entropy)


def solution(mesh):
    split = Mesh(mesh.devices.reshape(8, 4, 4, 2), AXES)
    placed = (P(AXES, None), P(), P(None, AXES), P(AXES), P(), P())
    return jax.shard_map(
        body, mesh=split, in_specs=placed, out_specs=(P(AXES), P(AXES)), check_vma=False
    )
```

```python
import functools

import jax
import jax.numpy as jnp
from jax import lax
from jax.experimental import pallas as pl
from jax.experimental.pallas import tpu as pltpu
from jax.sharding import Mesh, PartitionSpec as P

VOCAB_REAL = 73448


EPS = 1e-05
NEG = -1e30
DIGIT = 64
AXES = ("z", "x", "y", "core")
CHIP_AXES = ("z", "x", "y")


def slice_stats(rows, chosen, head, col_index, real_cols):
    logits = jnp.dot(rows, head, preferred_element_type=jnp.float32) / 10.0
    logits = jnp.where(real_cols[None, :], logits, NEG)
    rowmax = jnp.max(logits, axis=1)
    expo = jnp.where(real_cols[None, :], jnp.exp(logits - rowmax[:, None]), 0.0)
    total = jnp.sum(expo, axis=1)
    weighted = jnp.sum(jnp.where(real_cols[None, :], expo * logits, 0.0), axis=1)
    picked = jnp.sum(jnp.where(col_index[None, :] == chosen[:, None], logits, 0.0), axis=1)
    return (rowmax, total, weighted, picked)


def code_ids(ids):
    digits = [ids // (DIGIT * DIGIT), (ids // DIGIT) % DIGIT, ids % DIGIT]
    return jnp.stack(digits, axis=1).astype(jnp.bfloat16)


def decode_ids(coded):
    d = coded.astype(jnp.int32)
    return (d[:, 0] * DIGIT + d[:, 1]) * DIGIT + d[:, 2]


STREAMS = (("z", "x", "y"), ("x", "y", "z"), ("y", "z", "x"))
LANES = 128


def gather_kernel(sizes, spans, x_ref, g_ref, send_sem, recv_sem, own_sem):
    pos = {a: lax.axis_index(a) for a in AXES}

    def peer(axis, k):
        at = dict(pos)
        at[axis] = lax.rem(pos[axis] + k + sizes[axis], sizes[axis])
        return tuple(at[a] for a in AXES)

    def view(ref, held, axis, k, cols):
        idx = []
        for a in ("y", "x", "z"):
            if a in held:
                idx.append(slice(None))
            elif a == axis:
                idx.append(lax.rem(pos[a] + k + sizes[a], sizes[a]))
            else:
                idx.append(pos[a])
        return ref.at[tuple(idx) + (slice(None), cols)]

    barrier = pltpu.get_barrier_semaphore()
    count = 0
    for axis in CHIP_AXES:
        for k in (1, -1):
            pl.semaphore_signal(barrier, inc=1, device_id=peer(axis, k), device_id_type=pl.DeviceIdType.MESH)
            count += 1
    pl.semaphore_wait(barrier, count)

    own = pltpu.make_async_copy(x_ref, g_ref.at[pos["y"], pos["x"], pos["z"]], own_sem)
    own.start()

    plans = []
    for order in STREAMS:
        plan = []
        for t, axis in enumerate(order):
            n = sizes[axis]
            for q in range(1, n // 2 + 1):
                plan.append((t, axis, q, n % 2 == 0 and q == n // 2))
        plans.append(plan)

    def step_copies(s, step, sending):
        t, axis, q, split = plans[s][step]
        c0, w = spans[s]
        order = STREAMS[s]
        held = order[:t]
        if split:
            cut = (w // LANES // 2) * LANES
            col_of = [pl.ds(c0, cut), pl.ds(c0 + cut, w - cut)]
        else:
            col_of = [pl.ds(c0, w), pl.ds(c0, w)]
        out = []
        for d, sign in enumerate((1, -1)):
            cols = col_of[d]
            if sending:
                k = -sign * (q - 1)
                dst = view(g_ref, held, axis, k, cols)
                src = x_ref.at[:, cols] if (t == 0 and q == 1) else dst
                target = peer(axis, sign)
            else:
                k = -sign * q
                src = dst = view(g_ref, held, axis, k, cols)
                target = peer(axis, -sign)
            out.append(pltpu.make_async_remote_copy(
                src_ref=src, dst_ref=dst, send_sem=send_sem.at[s, step, d],
                recv_sem=recv_sem.at[s, step, d], device_id=target,
                device_id_type=pl.DeviceIdType.MESH,
            ))
        return out

    steps = len(plans[0])
    sends = []
    for g in range(steps):
        for s in (1, 2, 0):
            if g > 0:
                for copy in step_copies(s, g - 1, False):
                    copy.wait_recv()
            if g == 1 and s == 1:
                own.wait()
            for copy in step_copies(s, g, True):
                copy.start()
                sends.append(copy)
    for s in range(len(STREAMS)):
        for copy in step_copies(s, steps - 1, False):
            copy.wait_recv()
    for copy in sends:
        copy.wait_send()


def gather_rows(packed, sizes):
    rows, width = packed.shape
    tiles = width // LANES
    counts = [tiles * 9 // 21, tiles * 5 // 21]
    counts.append(tiles - sum(counts))
    spans, at = [], 0
    for c in counts:
        spans.append((at * LANES, c * LANES))
        at += c
    shape = (sizes["y"], sizes["x"], sizes["z"], rows, width)
    steps = sum(sizes[a] // 2 for a in CHIP_AXES)
    return pl.pallas_call(
        functools.partial(gather_kernel, sizes, spans),
        out_shape=jax.ShapeDtypeStruct(shape, packed.dtype),
        in_specs=[pl.BlockSpec(memory_space=pl.ANY)],
        out_specs=pl.BlockSpec(memory_space=pl.ANY),
        scratch_shapes=[
            pltpu.SemaphoreType.DMA((3, steps, 2)),
            pltpu.SemaphoreType.DMA((3, steps, 2)),
            pltpu.SemaphoreType.DMA(()),
        ],
        compiler_params=pltpu.CompilerParams(collective_id=0, has_side_effects=True),
    )(packed)


def combine(parts):
    top = jnp.max(parts[:, 0], axis=0)
    factor = jnp.exp(parts[:, 0] - top[None])
    total = jnp.sum(parts[:, 1] * factor, axis=0)
    weighted = jnp.sum(parts[:, 2] * factor, axis=0)
    picked = jnp.sum(parts[:, 3], axis=0)
    return jnp.stack([top, total, weighted, picked], axis=0)


def reduce_kernel(sizes, a_ref, out_ref, r1, c1, r2, c2, r3, send_sem, recv_sem):
    pos = {a: lax.axis_index(a) for a in AXES}

    def peer(axis, k):
        at = dict(pos)
        at[axis] = lax.rem(pos[axis] + k, sizes[axis])
        return tuple(at[a] for a in AXES)

    barrier = pltpu.get_barrier_semaphore()
    count = 0
    for axis in CHIP_AXES:
        for k in range(1, sizes[axis]):
            pl.semaphore_signal(barrier, inc=1, device_id=peer(axis, k), device_id_type=pl.DeviceIdType.MESH)
            count += 1
    pl.semaphore_wait(barrier, count)

    sends = []

    def stage(t, axis, src_of, land):
        n = sizes[axis]
        for k in range(1, n):
            copy = pltpu.make_async_remote_copy(
                src_ref=src_of(lax.rem(pos[axis] + k, n)), dst_ref=land.at[pos[axis]],
                send_sem=send_sem.at[t, k], recv_sem=recv_sem.at[t, (n - k) % n],
                device_id=peer(axis, k), device_id_type=pl.DeviceIdType.MESH,
            )
            copy.start()
            sends.append(copy)
        for j in range(1, n):
            slot = land.at[lax.rem(pos[axis] + j, n)]
            pltpu.make_async_remote_copy(
                src_ref=slot, dst_ref=slot, send_sem=send_sem.at[t, j], recv_sem=recv_sem.at[t, j],
                device_id=peer(axis, j), device_id_type=pl.DeviceIdType.MESH,
            ).wait_recv()

    r1[pos["y"]] = a_ref[pos["y"]]
    stage(0, "y", lambda i: a_ref.at[i], r1)
    c1[...] = combine(r1[...])
    own_x = pl.multiple_of(pos["x"] * LANES, LANES)
    r2[pos["x"]] = c1[:, pl.ds(own_x, LANES)]
    stage(1, "x", lambda i: c1.at[:, pl.ds(pl.multiple_of(i * LANES, LANES), LANES)], r2)
    c2[...] = combine(r2[...])
    r3[pos["z"]] = c2[...]
    stage(2, "z", lambda i: c2, r3)
    out_ref[...] = combine(r3[...])
    for copy in sends:
        copy.wait_send()


def reduce_stats(parts, sizes):
    ny, nx, nz = sizes["y"], sizes["x"], sizes["z"]
    longest = max(ny, nx, nz)
    width = parts.shape[-1]
    return pl.pallas_call(
        functools.partial(reduce_kernel, sizes),
        out_shape=jax.ShapeDtypeStruct((4, LANES), jnp.float32),
        scratch_shapes=[
            pltpu.VMEM((ny, 4, width), jnp.float32),
            pltpu.VMEM((4, width), jnp.float32),
            pltpu.VMEM((nx, 4, LANES), jnp.float32),
            pltpu.VMEM((4, LANES), jnp.float32),
            pltpu.VMEM((nz, 4, LANES), jnp.float32),
            pltpu.SemaphoreType.DMA((3, longest)),
            pltpu.SemaphoreType.DMA((3, longest)),
        ],
        compiler_params=pltpu.CompilerParams(collective_id=1, has_side_effects=True),
    )(parts)


def pack_kernel(h_ref, gain_ref, ids_ref, out_ref):
    values = h_ref[...].astype(jnp.float32)
    rows, width = values.shape
    scale = lax.rsqrt(jnp.mean(values * values, axis=-1, keepdims=True) + EPS)
    out_ref[:, :width] = (values * scale * gain_ref[...][None, :]).astype(jnp.bfloat16)
    row = lax.broadcasted_iota(jnp.int32, (rows, LANES), 0)
    lane = lax.broadcasted_iota(jnp.int32, (rows, LANES), 1)
    digit = jnp.zeros((rows, LANES), jnp.int32)
    for r in range(rows):
        v = ids_ref[r]
        for i, d in enumerate((v // (DIGIT * DIGIT), (v // DIGIT) % DIGIT, v % DIGIT)):
            digit = jnp.where((row == r) & (lane == i), d, digit)
    out_ref[:, width:] = digit.astype(jnp.float32).astype(jnp.bfloat16)


def pack_rows(hidden, norm_gain, token_ids):
    rows, width = hidden.shape
    return pl.pallas_call(
        pack_kernel,
        out_shape=jax.ShapeDtypeStruct((rows, width + LANES), jnp.bfloat16),
        in_specs=[
            pl.BlockSpec(memory_space=pltpu.VMEM),
            pl.BlockSpec(memory_space=pltpu.VMEM),
            pl.BlockSpec(memory_space=pltpu.SMEM),
        ],
    )(hidden, norm_gain, token_ids)


def body(hidden, norm_gain, head, token_ids, req_len, req_owner):
    local_rows, width = hidden.shape
    columns = head.shape[1]
    size = {a: lax.axis_size(a) for a in AXES}
    pos = {a: lax.axis_index(a) for a in AXES}
    chip = (pos["z"] * size["x"] + pos["x"]) * size["y"] + pos["y"]
    core = pos["core"]
    me = chip * size["core"] + core

    packed = pack_rows(hidden, norm_gain, token_ids)

    other = lax.ppermute(head, "core", [(0, 1), (1, 0)])
    chip_head = jnp.where(core == 0, jnp.concatenate([head, other], axis=1), jnp.concatenate([other, head], axis=1))
    col_index = chip * (2 * columns) + jnp.arange(2 * columns, dtype=jnp.int32)
    real_cols = col_index < VOCAB_REAL

    gathered = gather_rows(packed, size).reshape(-1, packed.shape[1])
    all_rows = gathered[:, :width]
    all_ids = decode_ids(gathered[:, width:width + 3])
    stats = jnp.stack(slice_stats(all_rows, all_ids, chip_head, col_index, real_cols), axis=0)

    parts = jnp.transpose(stats.reshape(4, size["y"], -1), (1, 0, 2))
    reduced = reduce_stats(parts, size)
    mine = lax.dynamic_slice_in_dim(reduced, pos["z"] * local_rows, local_rows, axis=1)
    top, total_all, weighted_all, picked_all = mine[0], mine[1], mine[2], mine[3]

    load = jnp.sum(jnp.where(req_owner == me, req_len, 0))
    live = jnp.arange(local_rows, dtype=jnp.int32) < load
    log_total = jnp.log(total_all)
    logprob = jnp.where(live, picked_all - top - log_total, 0.0)
    entropy = jnp.where(live, top + log_total - weighted_all / total_all, 0.0)
    return (logprob, entropy)


def solution(mesh):
    split = Mesh(mesh.devices.reshape(8, 4, 4, 2), AXES)
    placed = (P(AXES, None), P(), P(None, AXES), P(AXES), P(), P())
    return jax.shard_map(
        body, mesh=split, in_specs=placed, out_specs=(P(AXES), P(AXES)), check_vma=False
    )
```

```python
import functools

import jax
import jax.numpy as jnp
from jax import lax
from jax.experimental import pallas as pl
from jax.experimental.pallas import tpu as pltpu
from jax.sharding import Mesh, PartitionSpec as P

VOCAB_REAL = 73448


EPS = 1e-05
NEG = -1e30
DIGIT = 64
AXES = ("z", "x", "y", "core")
CHIP_AXES = ("z", "x", "y")


def slice_stats(rows, chosen, head, col_index, real_cols):
    logits = jnp.dot(rows, head, preferred_element_type=jnp.float32) / 10.0
    logits = jnp.where(real_cols[None, :], logits, NEG)
    rowmax = jnp.max(logits, axis=1)
    expo = jnp.where(real_cols[None, :], jnp.exp(logits - rowmax[:, None]), 0.0)
    total = jnp.sum(expo, axis=1)
    weighted = jnp.sum(jnp.where(real_cols[None, :], expo * logits, 0.0), axis=1)
    picked = jnp.sum(jnp.where(col_index[None, :] == chosen[:, None], logits, 0.0), axis=1)
    return (rowmax, total, weighted, picked)


def code_ids(ids):
    digits = [ids // (DIGIT * DIGIT), (ids // DIGIT) % DIGIT, ids % DIGIT]
    return jnp.stack(digits, axis=1).astype(jnp.bfloat16)


def decode_ids(coded):
    d = coded.astype(jnp.int32)
    return (d[:, 0] * DIGIT + d[:, 1]) * DIGIT + d[:, 2]


STREAMS = (("z", "x", "y"), ("x", "y", "z"), ("y", "z", "x"))
LANES = 128


def gather_kernel(sizes, spans, x_ref, g_ref, send_sem, recv_sem, own_sem):
    pos = {a: lax.axis_index(a) for a in AXES}

    def peer(axis, k):
        at = dict(pos)
        at[axis] = lax.rem(pos[axis] + k + sizes[axis], sizes[axis])
        return tuple(at[a] for a in AXES)

    def view(ref, held, axis, k, cols):
        idx = []
        for a in ("y", "x", "z"):
            if a in held:
                idx.append(slice(None))
            elif a == axis:
                idx.append(lax.rem(pos[a] + k + sizes[a], sizes[a]))
            else:
                idx.append(pos[a])
        return ref.at[tuple(idx) + (slice(None), cols)]

    barrier = pltpu.get_barrier_semaphore()
    count = 0
    for axis in CHIP_AXES:
        for k in (1, -1):
            pl.semaphore_signal(barrier, inc=1, device_id=peer(axis, k), device_id_type=pl.DeviceIdType.MESH)
            count += 1
    pl.semaphore_wait(barrier, count)

    own = pltpu.make_async_copy(x_ref, g_ref.at[pos["y"], pos["x"], pos["z"]], own_sem)
    own.start()

    plans = []
    for order in STREAMS:
        plan = []
        for t, axis in enumerate(order):
            n = sizes[axis]
            for q in range(1, n // 2 + 1):
                plan.append((t, axis, q, n % 2 == 0 and q == n // 2))
        plans.append(plan)

    def step_copies(s, step, sending):
        t, axis, q, split = plans[s][step]
        c0, w = spans[s]
        order = STREAMS[s]
        held = order[:t]
        if split:
            cut = (w // LANES // 2) * LANES
            col_of = [pl.ds(c0, cut), pl.ds(c0 + cut, w - cut)]
        else:
            col_of = [pl.ds(c0, w), pl.ds(c0, w)]
        out = []
        for d, sign in enumerate((1, -1)):
            cols = col_of[d]
            if sending:
                k = -sign * (q - 1)
                dst = view(g_ref, held, axis, k, cols)
                src = x_ref.at[:, cols] if (t == 0 and q == 1) else dst
                target = peer(axis, sign)
            else:
                k = -sign * q
                src = dst = view(g_ref, held, axis, k, cols)
                target = peer(axis, -sign)
            out.append(pltpu.make_async_remote_copy(
                src_ref=src, dst_ref=dst, send_sem=send_sem.at[s, step, d],
                recv_sem=recv_sem.at[s, step, d], device_id=target,
                device_id_type=pl.DeviceIdType.MESH,
            ))
        return out

    steps = len(plans[0])
    sends = []
    for g in range(steps):
        for s in (0, 2, 1):
            if g > 0:
                for copy in step_copies(s, g - 1, False):
                    copy.wait_recv()
            if g == 1 and s == 0:
                own.wait()
            for copy in step_copies(s, g, True):
                copy.start()
                sends.append(copy)
    for s in range(len(STREAMS)):
        for copy in step_copies(s, steps - 1, False):
            copy.wait_recv()
    for copy in sends:
        copy.wait_send()


def gather_rows(packed, sizes):
    rows, width = packed.shape
    tiles = width // LANES
    counts = [tiles * 9 // 21, tiles * 5 // 21]
    counts.append(tiles - sum(counts))
    spans, at = [], 0
    for c in counts:
        spans.append((at * LANES, c * LANES))
        at += c
    shape = (sizes["y"], sizes["x"], sizes["z"], rows, width)
    steps = sum(sizes[a] // 2 for a in CHIP_AXES)
    return pl.pallas_call(
        functools.partial(gather_kernel, sizes, spans),
        out_shape=jax.ShapeDtypeStruct(shape, packed.dtype),
        in_specs=[pl.BlockSpec(memory_space=pl.ANY)],
        out_specs=pl.BlockSpec(memory_space=pl.ANY),
        scratch_shapes=[
            pltpu.SemaphoreType.DMA((3, steps, 2)),
            pltpu.SemaphoreType.DMA((3, steps, 2)),
            pltpu.SemaphoreType.DMA(()),
        ],
        compiler_params=pltpu.CompilerParams(collective_id=0, has_side_effects=True),
    )(packed)


def combine(parts):
    top = jnp.max(parts[:, 0], axis=0)
    factor = jnp.exp(parts[:, 0] - top[None])
    total = jnp.sum(parts[:, 1] * factor, axis=0)
    weighted = jnp.sum(parts[:, 2] * factor, axis=0)
    picked = jnp.sum(parts[:, 3], axis=0)
    return jnp.stack([top, total, weighted, picked], axis=0)


def reduce_kernel(sizes, a_ref, out_ref, r1, c1, r2, c2, r3, send_sem, recv_sem):
    pos = {a: lax.axis_index(a) for a in AXES}

    def peer(axis, k):
        at = dict(pos)
        at[axis] = lax.rem(pos[axis] + k, sizes[axis])
        return tuple(at[a] for a in AXES)

    barrier = pltpu.get_barrier_semaphore()
    count = 0
    for axis in CHIP_AXES:
        for k in range(1, sizes[axis]):
            pl.semaphore_signal(barrier, inc=1, device_id=peer(axis, k), device_id_type=pl.DeviceIdType.MESH)
            count += 1
    pl.semaphore_wait(barrier, count)

    sends = []

    def stage(t, axis, src_of, land):
        n = sizes[axis]
        for k in range(1, n):
            copy = pltpu.make_async_remote_copy(
                src_ref=src_of(lax.rem(pos[axis] + k, n)), dst_ref=land.at[pos[axis]],
                send_sem=send_sem.at[t, k], recv_sem=recv_sem.at[t, (n - k) % n],
                device_id=peer(axis, k), device_id_type=pl.DeviceIdType.MESH,
            )
            copy.start()
            sends.append(copy)
        for j in range(1, n):
            slot = land.at[lax.rem(pos[axis] + j, n)]
            pltpu.make_async_remote_copy(
                src_ref=slot, dst_ref=slot, send_sem=send_sem.at[t, j], recv_sem=recv_sem.at[t, j],
                device_id=peer(axis, j), device_id_type=pl.DeviceIdType.MESH,
            ).wait_recv()

    r1[pos["y"]] = a_ref[pos["y"]]
    stage(0, "y", lambda i: a_ref.at[i], r1)
    c1[...] = combine(r1[...])
    own_x = pl.multiple_of(pos["x"] * LANES, LANES)
    r2[pos["x"]] = c1[:, pl.ds(own_x, LANES)]
    stage(1, "x", lambda i: c1.at[:, pl.ds(pl.multiple_of(i * LANES, LANES), LANES)], r2)
    c2[...] = combine(r2[...])
    r3[pos["z"]] = c2[...]
    stage(2, "z", lambda i: c2, r3)
    out_ref[...] = combine(r3[...])
    for copy in sends:
        copy.wait_send()


def reduce_stats(parts, sizes):
    ny, nx, nz = sizes["y"], sizes["x"], sizes["z"]
    longest = max(ny, nx, nz)
    width = parts.shape[-1]
    return pl.pallas_call(
        functools.partial(reduce_kernel, sizes),
        out_shape=jax.ShapeDtypeStruct((4, LANES), jnp.float32),
        scratch_shapes=[
            pltpu.VMEM((ny, 4, width), jnp.float32),
            pltpu.VMEM((4, width), jnp.float32),
            pltpu.VMEM((nx, 4, LANES), jnp.float32),
            pltpu.VMEM((4, LANES), jnp.float32),
            pltpu.VMEM((nz, 4, LANES), jnp.float32),
            pltpu.SemaphoreType.DMA((3, longest)),
            pltpu.SemaphoreType.DMA((3, longest)),
        ],
        compiler_params=pltpu.CompilerParams(collective_id=1, has_side_effects=True),
    )(parts)


def pack_kernel(h_ref, gain_ref, ids_ref, out_ref):
    values = h_ref[...].astype(jnp.float32)
    rows, width = values.shape
    scale = lax.rsqrt(jnp.mean(values * values, axis=-1, keepdims=True) + EPS)
    out_ref[:, :width] = (values * scale * gain_ref[...][None, :]).astype(jnp.bfloat16)
    row = lax.broadcasted_iota(jnp.int32, (rows, LANES), 0)
    lane = lax.broadcasted_iota(jnp.int32, (rows, LANES), 1)
    digit = jnp.zeros((rows, LANES), jnp.int32)
    for r in range(rows):
        v = ids_ref[r]
        for i, d in enumerate((v // (DIGIT * DIGIT), (v // DIGIT) % DIGIT, v % DIGIT)):
            digit = jnp.where((row == r) & (lane == i), d, digit)
    out_ref[:, width:] = digit.astype(jnp.float32).astype(jnp.bfloat16)


def pack_rows(hidden, norm_gain, token_ids):
    rows, width = hidden.shape
    return pl.pallas_call(
        pack_kernel,
        out_shape=jax.ShapeDtypeStruct((rows, width + LANES), jnp.bfloat16),
        in_specs=[
            pl.BlockSpec(memory_space=pltpu.VMEM),
            pl.BlockSpec(memory_space=pltpu.VMEM),
            pl.BlockSpec(memory_space=pltpu.SMEM),
        ],
    )(hidden, norm_gain, token_ids)


def body(hidden, norm_gain, head, token_ids, req_len, req_owner):
    local_rows, width = hidden.shape
    columns = head.shape[1]
    size = {a: lax.axis_size(a) for a in AXES}
    pos = {a: lax.axis_index(a) for a in AXES}
    chip = (pos["z"] * size["x"] + pos["x"]) * size["y"] + pos["y"]
    core = pos["core"]
    me = chip * size["core"] + core

    packed = pack_rows(hidden, norm_gain, token_ids)

    other = lax.ppermute(head, "core", [(0, 1), (1, 0)])
    chip_head = jnp.where(core == 0, jnp.concatenate([head, other], axis=1), jnp.concatenate([other, head], axis=1))
    col_index = chip * (2 * columns) + jnp.arange(2 * columns, dtype=jnp.int32)
    real_cols = col_index < VOCAB_REAL

    gathered = gather_rows(packed, size).reshape(-1, packed.shape[1])
    all_rows = gathered[:, :width]
    all_ids = decode_ids(gathered[:, width:width + 3])
    stats = jnp.stack(slice_stats(all_rows, all_ids, chip_head, col_index, real_cols), axis=0)

    parts = jnp.transpose(stats.reshape(4, size["y"], -1), (1, 0, 2))
    reduced = reduce_stats(parts, size)
    mine = lax.dynamic_slice_in_dim(reduced, pos["z"] * local_rows, local_rows, axis=1)
    top, total_all, weighted_all, picked_all = mine[0], mine[1], mine[2], mine[3]

    load = jnp.sum(jnp.where(req_owner == me, req_len, 0))
    live = jnp.arange(local_rows, dtype=jnp.int32) < load
    log_total = jnp.log(total_all)
    logprob = jnp.where(live, picked_all - top - log_total, 0.0)
    entropy = jnp.where(live, top + log_total - weighted_all / total_all, 0.0)
    return (logprob, entropy)


def solution(mesh):
    split = Mesh(mesh.devices.reshape(8, 4, 4, 2), AXES)
    placed = (P(AXES, None), P(), P(None, AXES), P(AXES), P(), P())
    return jax.shard_map(
        body, mesh=split, in_specs=placed, out_specs=(P(AXES), P(AXES)), check_vma=False
    )
```

```python
import functools

import jax
import jax.numpy as jnp
from jax import lax
from jax.experimental import pallas as pl
from jax.experimental.pallas import tpu as pltpu
from jax.sharding import Mesh, PartitionSpec as P

VOCAB_REAL = 73448


EPS = 1e-05
NEG = -1e30
DIGIT = 64
AXES = ("z", "x", "y", "core")
CHIP_AXES = ("z", "x", "y")


def slice_stats(rows, chosen, head, col_index, real_cols):
    logits = jnp.dot(rows, head, preferred_element_type=jnp.float32) / 10.0
    logits = jnp.where(real_cols[None, :], logits, NEG)
    rowmax = jnp.max(logits, axis=1)
    expo = jnp.where(real_cols[None, :], jnp.exp(logits - rowmax[:, None]), 0.0)
    total = jnp.sum(expo, axis=1)
    weighted = jnp.sum(jnp.where(real_cols[None, :], expo * logits, 0.0), axis=1)
    picked = jnp.sum(jnp.where(col_index[None, :] == chosen[:, None], logits, 0.0), axis=1)
    return (rowmax, total, weighted, picked)


def code_ids(ids):
    digits = [ids // (DIGIT * DIGIT), (ids // DIGIT) % DIGIT, ids % DIGIT]
    return jnp.stack(digits, axis=1).astype(jnp.bfloat16)


def decode_ids(coded):
    d = coded.astype(jnp.int32)
    return (d[:, 0] * DIGIT + d[:, 1]) * DIGIT + d[:, 2]


STREAMS = (("z", "x", "y"), ("x", "y", "z"), ("y", "z", "x"))
LANES = 128


def gather_kernel(sizes, spans, x_ref, g_ref, send_sem, recv_sem, own_sem):
    pos = {a: lax.axis_index(a) for a in AXES}

    def peer(axis, k):
        at = dict(pos)
        at[axis] = lax.rem(pos[axis] + k + sizes[axis], sizes[axis])
        return tuple(at[a] for a in AXES)

    def view(ref, held, axis, k, cols):
        idx = []
        for a in ("y", "x", "z"):
            if a in held:
                idx.append(slice(None))
            elif a == axis:
                idx.append(lax.rem(pos[a] + k + sizes[a], sizes[a]))
            else:
                idx.append(pos[a])
        return ref.at[tuple(idx) + (slice(None), cols)]

    barrier = pltpu.get_barrier_semaphore()
    count = 0
    for axis in CHIP_AXES:
        for k in (1, -1):
            pl.semaphore_signal(barrier, inc=1, device_id=peer(axis, k), device_id_type=pl.DeviceIdType.MESH)
            count += 1
    pl.semaphore_wait(barrier, count)

    own = pltpu.make_async_copy(x_ref, g_ref.at[pos["y"], pos["x"], pos["z"]], own_sem)
    own.start()

    plans = []
    for order in STREAMS:
        plan = []
        for t, axis in enumerate(order):
            n = sizes[axis]
            for q in range(1, n // 2 + 1):
                plan.append((t, axis, q, n % 2 == 0 and q == n // 2))
        plans.append(plan)

    def step_copies(s, step, sending):
        t, axis, q, split = plans[s][step]
        c0, w = spans[s]
        order = STREAMS[s]
        held = order[:t]
        if split:
            cut = (w // LANES // 2) * LANES
            col_of = [pl.ds(c0, cut), pl.ds(c0 + cut, w - cut)]
        else:
            col_of = [pl.ds(c0, w), pl.ds(c0, w)]
        out = []
        for d, sign in enumerate((1, -1)):
            cols = col_of[d]
            if sending:
                k = -sign * (q - 1)
                dst = view(g_ref, held, axis, k, cols)
                src = x_ref.at[:, cols] if (t == 0 and q == 1) else dst
                target = peer(axis, sign)
            else:
                k = -sign * q
                src = dst = view(g_ref, held, axis, k, cols)
                target = peer(axis, -sign)
            out.append(pltpu.make_async_remote_copy(
                src_ref=src, dst_ref=dst, send_sem=send_sem.at[s, step, d],
                recv_sem=recv_sem.at[s, step, d], device_id=target,
                device_id_type=pl.DeviceIdType.MESH,
            ))
        return out

    steps = len(plans[0])
    sends = []
    for g in range(steps):
        for s in range(len(STREAMS)):
            if g > 0:
                for copy in step_copies(s, g - 1, False):
                    copy.wait_recv()
            if g == 1 and s == 0:
                own.wait()
            for copy in step_copies(s, g, True):
                copy.start()
                sends.append(copy)
    for s in range(len(STREAMS)):
        for copy in step_copies(s, steps - 1, False):
            copy.wait_recv()
    for copy in sends:
        copy.wait_send()


def gather_rows(packed, sizes):
    rows, width = packed.shape
    tiles = width // LANES
    counts = [tiles * 9 // 21, tiles * 4 // 21]
    counts.append(tiles - sum(counts))
    spans, at = [], 0
    for c in counts:
        spans.append((at * LANES, c * LANES))
        at += c
    shape = (sizes["y"], sizes["x"], sizes["z"], rows, width)
    steps = sum(sizes[a] // 2 for a in CHIP_AXES)
    return pl.pallas_call(
        functools.partial(gather_kernel, sizes, spans),
        out_shape=jax.ShapeDtypeStruct(shape, packed.dtype),
        in_specs=[pl.BlockSpec(memory_space=pl.ANY)],
        out_specs=pl.BlockSpec(memory_space=pl.ANY),
        scratch_shapes=[
            pltpu.SemaphoreType.DMA((3, steps, 2)),
            pltpu.SemaphoreType.DMA((3, steps, 2)),
            pltpu.SemaphoreType.DMA(()),
        ],
        compiler_params=pltpu.CompilerParams(collective_id=0, has_side_effects=True),
    )(packed)


def combine(parts):
    top = jnp.max(parts[:, 0], axis=0)
    factor = jnp.exp(parts[:, 0] - top[None])
    total = jnp.sum(parts[:, 1] * factor, axis=0)
    weighted = jnp.sum(parts[:, 2] * factor, axis=0)
    picked = jnp.sum(parts[:, 3], axis=0)
    return jnp.stack([top, total, weighted, picked], axis=0)


def reduce_kernel(sizes, a_ref, out_ref, r1, c1, r2, c2, r3, send_sem, recv_sem):
    pos = {a: lax.axis_index(a) for a in AXES}

    def peer(axis, k):
        at = dict(pos)
        at[axis] = lax.rem(pos[axis] + k, sizes[axis])
        return tuple(at[a] for a in AXES)

    barrier = pltpu.get_barrier_semaphore()
    count = 0
    for axis in CHIP_AXES:
        for k in range(1, sizes[axis]):
            pl.semaphore_signal(barrier, inc=1, device_id=peer(axis, k), device_id_type=pl.DeviceIdType.MESH)
            count += 1
    pl.semaphore_wait(barrier, count)

    sends = []

    def stage(t, axis, src_of, land):
        n = sizes[axis]
        for k in range(1, n):
            copy = pltpu.make_async_remote_copy(
                src_ref=src_of(lax.rem(pos[axis] + k, n)), dst_ref=land.at[pos[axis]],
                send_sem=send_sem.at[t, k], recv_sem=recv_sem.at[t, (n - k) % n],
                device_id=peer(axis, k), device_id_type=pl.DeviceIdType.MESH,
            )
            copy.start()
            sends.append(copy)
        for j in range(1, n):
            slot = land.at[lax.rem(pos[axis] + j, n)]
            pltpu.make_async_remote_copy(
                src_ref=slot, dst_ref=slot, send_sem=send_sem.at[t, j], recv_sem=recv_sem.at[t, j],
                device_id=peer(axis, j), device_id_type=pl.DeviceIdType.MESH,
            ).wait_recv()

    r1[pos["y"]] = a_ref[pos["y"]]
    stage(0, "y", lambda i: a_ref.at[i], r1)
    c1[...] = combine(r1[...])
    own_x = pl.multiple_of(pos["x"] * LANES, LANES)
    r2[pos["x"]] = c1[:, pl.ds(own_x, LANES)]
    stage(1, "x", lambda i: c1.at[:, pl.ds(pl.multiple_of(i * LANES, LANES), LANES)], r2)
    c2[...] = combine(r2[...])
    r3[pos["z"]] = c2[...]
    stage(2, "z", lambda i: c2, r3)
    out_ref[...] = combine(r3[...])
    for copy in sends:
        copy.wait_send()


def reduce_stats(parts, sizes):
    ny, nx, nz = sizes["y"], sizes["x"], sizes["z"]
    longest = max(ny, nx, nz)
    width = parts.shape[-1]
    return pl.pallas_call(
        functools.partial(reduce_kernel, sizes),
        out_shape=jax.ShapeDtypeStruct((4, LANES), jnp.float32),
        scratch_shapes=[
            pltpu.VMEM((ny, 4, width), jnp.float32),
            pltpu.VMEM((4, width), jnp.float32),
            pltpu.VMEM((nx, 4, LANES), jnp.float32),
            pltpu.VMEM((4, LANES), jnp.float32),
            pltpu.VMEM((nz, 4, LANES), jnp.float32),
            pltpu.SemaphoreType.DMA((3, longest)),
            pltpu.SemaphoreType.DMA((3, longest)),
        ],
        compiler_params=pltpu.CompilerParams(collective_id=1, has_side_effects=True),
    )(parts)


def pack_kernel(h_ref, gain_ref, ids_ref, out_ref):
    values = h_ref[...].astype(jnp.float32)
    rows, width = values.shape
    scale = lax.rsqrt(jnp.mean(values * values, axis=-1, keepdims=True) + EPS)
    out_ref[:, :width] = (values * scale * gain_ref[...][None, :]).astype(jnp.bfloat16)
    row = lax.broadcasted_iota(jnp.int32, (rows, LANES), 0)
    lane = lax.broadcasted_iota(jnp.int32, (rows, LANES), 1)
    digit = jnp.zeros((rows, LANES), jnp.int32)
    for r in range(rows):
        v = ids_ref[r]
        for i, d in enumerate((v // (DIGIT * DIGIT), (v // DIGIT) % DIGIT, v % DIGIT)):
            digit = jnp.where((row == r) & (lane == i), d, digit)
    out_ref[:, width:] = digit.astype(jnp.float32).astype(jnp.bfloat16)


def pack_rows(hidden, norm_gain, token_ids):
    rows, width = hidden.shape
    return pl.pallas_call(
        pack_kernel,
        out_shape=jax.ShapeDtypeStruct((rows, width + LANES), jnp.bfloat16),
        in_specs=[
            pl.BlockSpec(memory_space=pltpu.VMEM),
            pl.BlockSpec(memory_space=pltpu.VMEM),
            pl.BlockSpec(memory_space=pltpu.SMEM),
        ],
    )(hidden, norm_gain, token_ids)


def body(hidden, norm_gain, head, token_ids, req_len, req_owner):
    local_rows, width = hidden.shape
    columns = head.shape[1]
    size = {a: lax.axis_size(a) for a in AXES}
    pos = {a: lax.axis_index(a) for a in AXES}
    chip = (pos["z"] * size["x"] + pos["x"]) * size["y"] + pos["y"]
    core = pos["core"]
    me = chip * size["core"] + core

    packed = pack_rows(hidden, norm_gain, token_ids)

    other = lax.ppermute(head, "core", [(0, 1), (1, 0)])
    chip_head = jnp.where(core == 0, jnp.concatenate([head, other], axis=1), jnp.concatenate([other, head], axis=1))
    col_index = chip * (2 * columns) + jnp.arange(2 * columns, dtype=jnp.int32)
    real_cols = col_index < VOCAB_REAL

    gathered = gather_rows(packed, size).reshape(-1, packed.shape[1])
    all_rows = gathered[:, :width]
    all_ids = decode_ids(gathered[:, width:width + 3])
    stats = jnp.stack(slice_stats(all_rows, all_ids, chip_head, col_index, real_cols), axis=0)

    parts = jnp.transpose(stats.reshape(4, size["y"], -1), (1, 0, 2))
    reduced = reduce_stats(parts, size)
    mine = lax.dynamic_slice_in_dim(reduced, pos["z"] * local_rows, local_rows, axis=1)
    top, total_all, weighted_all, picked_all = mine[0], mine[1], mine[2], mine[3]

    load = jnp.sum(jnp.where(req_owner == me, req_len, 0))
    live = jnp.arange(local_rows, dtype=jnp.int32) < load
    log_total = jnp.log(total_all)
    logprob = jnp.where(live, picked_all - top - log_total, 0.0)
    entropy = jnp.where(live, top + log_total - weighted_all / total_all, 0.0)
    return (logprob, entropy)


def solution(mesh):
    split = Mesh(mesh.devices.reshape(8, 4, 4, 2), AXES)
    placed = (P(AXES, None), P(), P(None, AXES), P(AXES), P(), P())
    return jax.shard_map(
        body, mesh=split, in_specs=placed, out_specs=(P(AXES), P(AXES)), check_vma=False
    )
```

```python
import functools

import jax
import jax.numpy as jnp
from jax import lax
from jax.experimental import pallas as pl
from jax.experimental.pallas import tpu as pltpu
from jax.sharding import Mesh, PartitionSpec as P

VOCAB_REAL = 73448


EPS = 1e-05
NEG = -1e30
DIGIT = 64
AXES = ("z", "x", "y", "core")
CHIP_AXES = ("z", "x", "y")


def slice_stats(rows, chosen, head, col_index, real_cols):
    logits = jnp.dot(rows, head, preferred_element_type=jnp.float32) / 10.0
    logits = jnp.where(real_cols[None, :], logits, NEG)
    rowmax = jnp.max(logits, axis=1)
    expo = jnp.where(real_cols[None, :], jnp.exp(logits - rowmax[:, None]), 0.0)
    total = jnp.sum(expo, axis=1)
    weighted = jnp.sum(jnp.where(real_cols[None, :], expo * logits, 0.0), axis=1)
    picked = jnp.sum(jnp.where(col_index[None, :] == chosen[:, None], logits, 0.0), axis=1)
    return (rowmax, total, weighted, picked)


def code_ids(ids):
    digits = [ids // (DIGIT * DIGIT), (ids // DIGIT) % DIGIT, ids % DIGIT]
    return jnp.stack(digits, axis=1).astype(jnp.bfloat16)


def decode_ids(coded):
    d = coded.astype(jnp.int32)
    return (d[:, 0] * DIGIT + d[:, 1]) * DIGIT + d[:, 2]


STREAMS = (("z", "x", "y"), ("x", "y", "z"), ("y", "z", "x"))
LANES = 128


def gather_kernel(sizes, spans, x_ref, g_ref, send_sem, recv_sem, own_sem):
    pos = {a: lax.axis_index(a) for a in AXES}

    def peer(axis, k):
        at = dict(pos)
        at[axis] = lax.rem(pos[axis] + k + sizes[axis], sizes[axis])
        return tuple(at[a] for a in AXES)

    def view(ref, held, axis, k, cols):
        idx = []
        for a in ("y", "x", "z"):
            if a in held:
                idx.append(slice(None))
            elif a == axis:
                idx.append(lax.rem(pos[a] + k + sizes[a], sizes[a]))
            else:
                idx.append(pos[a])
        return ref.at[tuple(idx) + (slice(None), cols)]

    barrier = pltpu.get_barrier_semaphore()
    count = 0
    for axis in CHIP_AXES:
        for k in (1, -1):
            pl.semaphore_signal(barrier, inc=1, device_id=peer(axis, k), device_id_type=pl.DeviceIdType.MESH)
            count += 1
    pl.semaphore_wait(barrier, count)

    own = pltpu.make_async_copy(x_ref, g_ref.at[pos["y"], pos["x"], pos["z"]], own_sem)
    own.start()

    plans = []
    for order in STREAMS:
        plan = []
        for t, axis in enumerate(order):
            n = sizes[axis]
            for q in range(1, n // 2 + 1):
                plan.append((t, axis, q, n % 2 == 0 and q == n // 2))
        plans.append(plan)

    def step_copies(s, step, sending):
        t, axis, q, split = plans[s][step]
        c0, w = spans[s]
        order = STREAMS[s]
        held = order[:t]
        if split:
            cut = (w // LANES // 2) * LANES
            col_of = [pl.ds(c0, cut), pl.ds(c0 + cut, w - cut)]
        else:
            col_of = [pl.ds(c0, w), pl.ds(c0, w)]
        out = []
        for d, sign in enumerate((1, -1)):
            cols = col_of[d]
            if sending:
                k = -sign * (q - 1)
                dst = view(g_ref, held, axis, k, cols)
                src = x_ref.at[:, cols] if (t == 0 and q == 1) else dst
                target = peer(axis, sign)
            else:
                k = -sign * q
                src = dst = view(g_ref, held, axis, k, cols)
                target = peer(axis, -sign)
            out.append(pltpu.make_async_remote_copy(
                src_ref=src, dst_ref=dst, send_sem=send_sem.at[s, step, d],
                recv_sem=recv_sem.at[s, step, d], device_id=target,
                device_id_type=pl.DeviceIdType.MESH,
            ))
        return out

    steps = len(plans[0])
    sends = []
    for g in range(steps):
        if g == 1:
            own.wait()
        for s in range(len(STREAMS)):
            out = step_copies(s, g, True)
            if g > 0 and plans[s][g][0] == plans[s][g - 1][0]:
                for arrived, copy in zip(step_copies(s, g - 1, False), out):
                    arrived.wait_recv()
                    copy.start()
                    sends.append(copy)
                continue
            if g > 0:
                for copy in step_copies(s, g - 1, False):
                    copy.wait_recv()
            for copy in out:
                copy.start()
                sends.append(copy)
    for s in range(len(STREAMS)):
        for copy in step_copies(s, steps - 1, False):
            copy.wait_recv()
    for copy in sends:
        copy.wait_send()


def gather_rows(packed, sizes):
    rows, width = packed.shape
    tiles = width // LANES
    counts = [tiles * 9 // 21, tiles * 5 // 21]
    counts.append(tiles - sum(counts))
    spans, at = [], 0
    for c in counts:
        spans.append((at * LANES, c * LANES))
        at += c
    shape = (sizes["y"], sizes["x"], sizes["z"], rows, width)
    steps = sum(sizes[a] // 2 for a in CHIP_AXES)
    return pl.pallas_call(
        functools.partial(gather_kernel, sizes, spans),
        out_shape=jax.ShapeDtypeStruct(shape, packed.dtype),
        in_specs=[pl.BlockSpec(memory_space=pl.ANY)],
        out_specs=pl.BlockSpec(memory_space=pl.ANY),
        scratch_shapes=[
            pltpu.SemaphoreType.DMA((3, steps, 2)),
            pltpu.SemaphoreType.DMA((3, steps, 2)),
            pltpu.SemaphoreType.DMA(()),
        ],
        compiler_params=pltpu.CompilerParams(collective_id=0, has_side_effects=True),
    )(packed)


def combine(parts):
    top = jnp.max(parts[:, 0], axis=0)
    factor = jnp.exp(parts[:, 0] - top[None])
    total = jnp.sum(parts[:, 1] * factor, axis=0)
    weighted = jnp.sum(parts[:, 2] * factor, axis=0)
    picked = jnp.sum(parts[:, 3], axis=0)
    return jnp.stack([top, total, weighted, picked], axis=0)


def reduce_kernel(sizes, a_ref, out_ref, r1, c1, r2, c2, r3, send_sem, recv_sem):
    pos = {a: lax.axis_index(a) for a in AXES}

    def peer(axis, k):
        at = dict(pos)
        at[axis] = lax.rem(pos[axis] + k, sizes[axis])
        return tuple(at[a] for a in AXES)

    barrier = pltpu.get_barrier_semaphore()
    count = 0
    for axis in CHIP_AXES:
        for k in range(1, sizes[axis]):
            pl.semaphore_signal(barrier, inc=1, device_id=peer(axis, k), device_id_type=pl.DeviceIdType.MESH)
            count += 1
    pl.semaphore_wait(barrier, count)

    sends = []

    def stage(t, axis, src_of, land):
        n = sizes[axis]
        for k in range(1, n):
            copy = pltpu.make_async_remote_copy(
                src_ref=src_of(lax.rem(pos[axis] + k, n)), dst_ref=land.at[pos[axis]],
                send_sem=send_sem.at[t, k], recv_sem=recv_sem.at[t, (n - k) % n],
                device_id=peer(axis, k), device_id_type=pl.DeviceIdType.MESH,
            )
            copy.start()
            sends.append(copy)
        for j in range(1, n):
            slot = land.at[lax.rem(pos[axis] + j, n)]
            pltpu.make_async_remote_copy(
                src_ref=slot, dst_ref=slot, send_sem=send_sem.at[t, j], recv_sem=recv_sem.at[t, j],
                device_id=peer(axis, j), device_id_type=pl.DeviceIdType.MESH,
            ).wait_recv()

    r1[pos["y"]] = a_ref[pos["y"]]
    stage(0, "y", lambda i: a_ref.at[i], r1)
    c1[...] = combine(r1[...])
    own_x = pl.multiple_of(pos["x"] * LANES, LANES)
    r2[pos["x"]] = c1[:, pl.ds(own_x, LANES)]
    stage(1, "x", lambda i: c1.at[:, pl.ds(pl.multiple_of(i * LANES, LANES), LANES)], r2)
    c2[...] = combine(r2[...])
    r3[pos["z"]] = c2[...]
    stage(2, "z", lambda i: c2, r3)
    out_ref[...] = combine(r3[...])
    for copy in sends:
        copy.wait_send()


def reduce_stats(parts, sizes):
    ny, nx, nz = sizes["y"], sizes["x"], sizes["z"]
    longest = max(ny, nx, nz)
    width = parts.shape[-1]
    return pl.pallas_call(
        functools.partial(reduce_kernel, sizes),
        out_shape=jax.ShapeDtypeStruct((4, LANES), jnp.float32),
        scratch_shapes=[
            pltpu.VMEM((ny, 4, width), jnp.float32),
            pltpu.VMEM((4, width), jnp.float32),
            pltpu.VMEM((nx, 4, LANES), jnp.float32),
            pltpu.VMEM((4, LANES), jnp.float32),
            pltpu.VMEM((nz, 4, LANES), jnp.float32),
            pltpu.SemaphoreType.DMA((3, longest)),
            pltpu.SemaphoreType.DMA((3, longest)),
        ],
        compiler_params=pltpu.CompilerParams(collective_id=1, has_side_effects=True),
    )(parts)


def pack_kernel(h_ref, gain_ref, ids_ref, out_ref):
    values = h_ref[...].astype(jnp.float32)
    rows, width = values.shape
    scale = lax.rsqrt(jnp.mean(values * values, axis=-1, keepdims=True) + EPS)
    out_ref[:, :width] = (values * scale * gain_ref[...][None, :]).astype(jnp.bfloat16)
    row = lax.broadcasted_iota(jnp.int32, (rows, LANES), 0)
    lane = lax.broadcasted_iota(jnp.int32, (rows, LANES), 1)
    digit = jnp.zeros((rows, LANES), jnp.int32)
    for r in range(rows):
        v = ids_ref[r]
        for i, d in enumerate((v // (DIGIT * DIGIT), (v // DIGIT) % DIGIT, v % DIGIT)):
            digit = jnp.where((row == r) & (lane == i), d, digit)
    out_ref[:, width:] = digit.astype(jnp.float32).astype(jnp.bfloat16)


def pack_rows(hidden, norm_gain, token_ids):
    rows, width = hidden.shape
    return pl.pallas_call(
        pack_kernel,
        out_shape=jax.ShapeDtypeStruct((rows, width + LANES), jnp.bfloat16),
        in_specs=[
            pl.BlockSpec(memory_space=pltpu.VMEM),
            pl.BlockSpec(memory_space=pltpu.VMEM),
            pl.BlockSpec(memory_space=pltpu.SMEM),
        ],
    )(hidden, norm_gain, token_ids)


def body(hidden, norm_gain, head, token_ids, req_len, req_owner):
    local_rows, width = hidden.shape
    columns = head.shape[1]
    size = {a: lax.axis_size(a) for a in AXES}
    pos = {a: lax.axis_index(a) for a in AXES}
    chip = (pos["z"] * size["x"] + pos["x"]) * size["y"] + pos["y"]
    core = pos["core"]
    me = chip * size["core"] + core

    packed = pack_rows(hidden, norm_gain, token_ids)

    other = lax.ppermute(head, "core", [(0, 1), (1, 0)])
    chip_head = jnp.where(core == 0, jnp.concatenate([head, other], axis=1), jnp.concatenate([other, head], axis=1))
    col_index = chip * (2 * columns) + jnp.arange(2 * columns, dtype=jnp.int32)
    real_cols = col_index < VOCAB_REAL

    gathered = gather_rows(packed, size).reshape(-1, packed.shape[1])
    all_rows = gathered[:, :width]
    all_ids = decode_ids(gathered[:, width:width + 3])
    stats = jnp.stack(slice_stats(all_rows, all_ids, chip_head, col_index, real_cols), axis=0)

    parts = jnp.transpose(stats.reshape(4, size["y"], -1), (1, 0, 2))
    reduced = reduce_stats(parts, size)
    mine = lax.dynamic_slice_in_dim(reduced, pos["z"] * local_rows, local_rows, axis=1)
    top, total_all, weighted_all, picked_all = mine[0], mine[1], mine[2], mine[3]

    load = jnp.sum(jnp.where(req_owner == me, req_len, 0))
    live = jnp.arange(local_rows, dtype=jnp.int32) < load
    log_total = jnp.log(total_all)
    logprob = jnp.where(live, picked_all - top - log_total, 0.0)
    entropy = jnp.where(live, top + log_total - weighted_all / total_all, 0.0)
    return (logprob, entropy)


def solution(mesh):
    split = Mesh(mesh.devices.reshape(8, 4, 4, 2), AXES)
    placed = (P(AXES, None), P(), P(None, AXES), P(AXES), P(), P())
    return jax.shard_map(
        body, mesh=split, in_specs=placed, out_specs=(P(AXES), P(AXES)), check_vma=False
    )
```

```python
import functools

import jax
import jax.numpy as jnp
from jax import lax
from jax.experimental import pallas as pl
from jax.experimental.pallas import tpu as pltpu
from jax.sharding import Mesh, PartitionSpec as P

VOCAB_REAL = 73448


EPS = 1e-05
NEG = -1e30
DIGIT = 64
AXES = ("z", "x", "y", "core")
CHIP_AXES = ("z", "x", "y")


def slice_stats(rows, chosen, head, col_index, real_cols):
    logits = jnp.dot(rows, head, preferred_element_type=jnp.float32) / 10.0
    logits = jnp.where(real_cols[None, :], logits, NEG)
    rowmax = jnp.max(logits, axis=1)
    expo = jnp.where(real_cols[None, :], jnp.exp(logits - rowmax[:, None]), 0.0)
    total = jnp.sum(expo, axis=1)
    weighted = jnp.sum(jnp.where(real_cols[None, :], expo * logits, 0.0), axis=1)
    picked = jnp.sum(jnp.where(col_index[None, :] == chosen[:, None], logits, 0.0), axis=1)
    return (rowmax, total, weighted, picked)


def code_ids(ids):
    digits = [ids // (DIGIT * DIGIT), (ids // DIGIT) % DIGIT, ids % DIGIT]
    return jnp.stack(digits, axis=1).astype(jnp.bfloat16)


def decode_ids(coded):
    d = coded.astype(jnp.int32)
    return (d[:, 0] * DIGIT + d[:, 1]) * DIGIT + d[:, 2]


STREAMS = (("z", "x", "y"), ("x", "y", "z"), ("y", "z", "x"))
LANES = 128


def gather_kernel(sizes, spans, x_ref, g_ref, send_sem, recv_sem, own_sem):
    pos = {a: lax.axis_index(a) for a in AXES}

    def peer(axis, k):
        at = dict(pos)
        at[axis] = lax.rem(pos[axis] + k + sizes[axis], sizes[axis])
        return tuple(at[a] for a in AXES)

    def view(ref, held, axis, k, cols):
        idx = []
        for a in ("y", "x", "z"):
            if a in held:
                idx.append(slice(None))
            elif a == axis:
                idx.append(lax.rem(pos[a] + k + sizes[a], sizes[a]))
            else:
                idx.append(pos[a])
        return ref.at[tuple(idx) + (slice(None), cols)]

    barrier = pltpu.get_barrier_semaphore()
    count = 0
    for axis in CHIP_AXES:
        for k in (1, -1):
            pl.semaphore_signal(barrier, inc=1, device_id=peer(axis, k), device_id_type=pl.DeviceIdType.MESH)
            count += 1
    pl.semaphore_wait(barrier, count)

    own = pltpu.make_async_copy(x_ref, g_ref.at[pos["y"], pos["x"], pos["z"]], own_sem)
    own.start()

    plans = []
    for order in STREAMS:
        plan = []
        for t, axis in enumerate(order):
            n = sizes[axis]
            for q in range(1, n // 2 + 1):
                plan.append((t, axis, q, n % 2 == 0 and q == n // 2))
        plans.append(plan)

    def step_copies(s, step, sending):
        t, axis, q, split = plans[s][step]
        c0, w = spans[s]
        order = STREAMS[s]
        held = order[:t]
        if split:
            cut = (w // LANES // 2) * LANES
            col_of = [pl.ds(c0, cut), pl.ds(c0 + cut, w - cut)]
        else:
            col_of = [pl.ds(c0, w), pl.ds(c0, w)]
        out = []
        for d, sign in enumerate((1, -1)):
            cols = col_of[d]
            if sending:
                k = -sign * (q - 1)
                dst = view(g_ref, held, axis, k, cols)
                src = x_ref.at[:, cols] if (t == 0 and q == 1) else dst
                target = peer(axis, sign)
            else:
                k = -sign * q
                src = dst = view(g_ref, held, axis, k, cols)
                target = peer(axis, -sign)
            out.append(pltpu.make_async_remote_copy(
                src_ref=src, dst_ref=dst, send_sem=send_sem.at[s, step, d],
                recv_sem=recv_sem.at[s, step, d], device_id=target,
                device_id_type=pl.DeviceIdType.MESH,
            ))
        return out

    steps = len(plans[0])
    sends = []
    for g in range(steps):
        for s in range(len(STREAMS)):
            if g > 0:
                for copy in step_copies(s, g - 1, False):
                    copy.wait_recv()
            if g == 1 and s == 0:
                own.wait()
            for copy in step_copies(s, g, True):
                copy.start()
                sends.append(copy)
    for s in range(len(STREAMS)):
        for copy in step_copies(s, steps - 1, False):
            copy.wait_recv()
    for copy in sends:
        copy.wait_send()


def gather_rows(packed, sizes):
    rows, width = packed.shape
    tiles = width // LANES
    counts = [tiles * 9 // 21, tiles * 5 // 21]
    counts.append(tiles - sum(counts))
    spans, at = [], 0
    for c in counts:
        spans.append((at * LANES, c * LANES))
        at += c
    shape = (sizes["y"], sizes["x"], sizes["z"], rows, width)
    steps = sum(sizes[a] // 2 for a in CHIP_AXES)
    return pl.pallas_call(
        functools.partial(gather_kernel, sizes, spans),
        out_shape=jax.ShapeDtypeStruct(shape, packed.dtype),
        in_specs=[pl.BlockSpec(memory_space=pl.ANY)],
        out_specs=pl.BlockSpec(memory_space=pl.ANY),
        scratch_shapes=[
            pltpu.SemaphoreType.DMA((3, steps, 2)),
            pltpu.SemaphoreType.DMA((3, steps, 2)),
            pltpu.SemaphoreType.DMA(()),
        ],
        compiler_params=pltpu.CompilerParams(collective_id=0, has_side_effects=True),
    )(packed)


def combine(parts):
    top = jnp.max(parts[:, 0], axis=0)
    factor = jnp.exp(parts[:, 0] - top[None])
    total = jnp.sum(parts[:, 1] * factor, axis=0)
    weighted = jnp.sum(parts[:, 2] * factor, axis=0)
    picked = jnp.sum(parts[:, 3], axis=0)
    return jnp.stack([top, total, weighted, picked], axis=0)


def reduce_kernel(sizes, a_ref, out_ref, r1, c1, r2, send_sem, recv_sem):
    pos = {a: lax.axis_index(a) for a in AXES}
    ny, nx, nz = sizes["y"], sizes["x"], sizes["z"]

    def peer(offsets):
        at = dict(pos)
        for a, k in offsets.items():
            at[a] = lax.rem(pos[a] + k, sizes[a])
        return tuple(at[a] for a in AXES)

    plane = [(ky, kx) for ky in range(ny) for kx in range(nx) if (ky, kx) != (0, 0)]
    barrier = pltpu.get_barrier_semaphore()
    targets = [{"y": ky, "x": kx} for ky, kx in plane] + [{"z": k} for k in range(1, nz)]
    for offsets in targets:
        pl.semaphore_signal(barrier, inc=1, device_id=peer(offsets), device_id_type=pl.DeviceIdType.MESH)
    pl.semaphore_wait(barrier, len(targets))

    sends = []
    mine = pos["y"] * nx + pos["x"]
    r1[mine] = a_ref[mine]
    for ky, kx in plane:
        there = lax.rem(pos["y"] + ky, ny) * nx + lax.rem(pos["x"] + kx, nx)
        copy = pltpu.make_async_remote_copy(
            src_ref=a_ref.at[there], dst_ref=r1.at[mine], send_sem=send_sem.at[0, ky * nx + kx],
            recv_sem=recv_sem.at[0, ((ny - ky) % ny) * nx + (nx - kx) % nx],
            device_id=peer({"y": ky, "x": kx}), device_id_type=pl.DeviceIdType.MESH,
        )
        copy.start()
        sends.append(copy)
    for jy, jx in plane:
        slot = r1.at[lax.rem(pos["y"] + jy, ny) * nx + lax.rem(pos["x"] + jx, nx)]
        pltpu.make_async_remote_copy(
            src_ref=slot, dst_ref=slot, send_sem=send_sem.at[0, jy * nx + jx], recv_sem=recv_sem.at[0, jy * nx + jx],
            device_id=peer({"y": jy, "x": jx}), device_id_type=pl.DeviceIdType.MESH,
        ).wait_recv()
    c1[...] = combine(r1[...])
    r2[pos["z"]] = c1[...]
    for k in range(1, nz):
        copy = pltpu.make_async_remote_copy(
            src_ref=c1, dst_ref=r2.at[pos["z"]], send_sem=send_sem.at[1, k], recv_sem=recv_sem.at[1, (nz - k) % nz],
            device_id=peer({"z": k}), device_id_type=pl.DeviceIdType.MESH,
        )
        copy.start()
        sends.append(copy)
    for j in range(1, nz):
        slot = r2.at[lax.rem(pos["z"] + j, nz)]
        pltpu.make_async_remote_copy(
            src_ref=slot, dst_ref=slot, send_sem=send_sem.at[1, j], recv_sem=recv_sem.at[1, j],
            device_id=peer({"z": j}), device_id_type=pl.DeviceIdType.MESH,
        ).wait_recv()
    out_ref[...] = combine(r2[...])
    for copy in sends:
        copy.wait_send()


def reduce_stats(parts, sizes):
    planes, nz = parts.shape[0], sizes["z"]
    labels = max(planes, nz)
    return pl.pallas_call(
        functools.partial(reduce_kernel, sizes),
        out_shape=jax.ShapeDtypeStruct((4, LANES), jnp.float32),
        scratch_shapes=[
            pltpu.VMEM((planes, 4, LANES), jnp.float32),
            pltpu.VMEM((4, LANES), jnp.float32),
            pltpu.VMEM((nz, 4, LANES), jnp.float32),
            pltpu.SemaphoreType.DMA((2, labels)),
            pltpu.SemaphoreType.DMA((2, labels)),
        ],
        compiler_params=pltpu.CompilerParams(collective_id=1, has_side_effects=True),
    )(parts)


def pack_kernel(h_ref, gain_ref, ids_ref, out_ref):
    values = h_ref[...].astype(jnp.float32)
    rows, width = values.shape
    scale = lax.rsqrt(jnp.mean(values * values, axis=-1, keepdims=True) + EPS)
    out_ref[:, :width] = (values * scale * gain_ref[...][None, :]).astype(jnp.bfloat16)
    row = lax.broadcasted_iota(jnp.int32, (rows, LANES), 0)
    lane = lax.broadcasted_iota(jnp.int32, (rows, LANES), 1)
    digit = jnp.zeros((rows, LANES), jnp.int32)
    for r in range(rows):
        v = ids_ref[r]
        for i, d in enumerate((v // (DIGIT * DIGIT), (v // DIGIT) % DIGIT, v % DIGIT)):
            digit = jnp.where((row == r) & (lane == i), d, digit)
    out_ref[:, width:] = digit.astype(jnp.float32).astype(jnp.bfloat16)


def pack_rows(hidden, norm_gain, token_ids):
    rows, width = hidden.shape
    return pl.pallas_call(
        pack_kernel,
        out_shape=jax.ShapeDtypeStruct((rows, width + LANES), jnp.bfloat16),
        in_specs=[
            pl.BlockSpec(memory_space=pltpu.VMEM),
            pl.BlockSpec(memory_space=pltpu.VMEM),
            pl.BlockSpec(memory_space=pltpu.SMEM),
        ],
    )(hidden, norm_gain, token_ids)


def body(hidden, norm_gain, head, token_ids, req_len, req_owner):
    local_rows, width = hidden.shape
    columns = head.shape[1]
    size = {a: lax.axis_size(a) for a in AXES}
    pos = {a: lax.axis_index(a) for a in AXES}
    chip = (pos["z"] * size["x"] + pos["x"]) * size["y"] + pos["y"]
    core = pos["core"]
    me = chip * size["core"] + core

    packed = pack_rows(hidden, norm_gain, token_ids)

    other = lax.ppermute(head, "core", [(0, 1), (1, 0)])
    chip_head = jnp.where(core == 0, jnp.concatenate([head, other], axis=1), jnp.concatenate([other, head], axis=1))
    col_index = chip * (2 * columns) + jnp.arange(2 * columns, dtype=jnp.int32)
    real_cols = col_index < VOCAB_REAL

    gathered = gather_rows(packed, size).reshape(-1, packed.shape[1])
    all_rows = gathered[:, :width]
    all_ids = decode_ids(gathered[:, width:width + 3])
    stats = jnp.stack(slice_stats(all_rows, all_ids, chip_head, col_index, real_cols), axis=0)

    parts = jnp.transpose(stats.reshape(4, size["y"] * size["x"], -1), (1, 0, 2))
    reduced = reduce_stats(parts, size)
    mine = lax.dynamic_slice_in_dim(reduced, pos["z"] * local_rows, local_rows, axis=1)
    top, total_all, weighted_all, picked_all = mine[0], mine[1], mine[2], mine[3]

    load = jnp.sum(jnp.where(req_owner == me, req_len, 0))
    live = jnp.arange(local_rows, dtype=jnp.int32) < load
    log_total = jnp.log(total_all)
    logprob = jnp.where(live, picked_all - top - log_total, 0.0)
    entropy = jnp.where(live, top + log_total - weighted_all / total_all, 0.0)
    return (logprob, entropy)


def solution(mesh):
    split = Mesh(mesh.devices.reshape(8, 4, 4, 2), AXES)
    placed = (P(AXES, None), P(), P(None, AXES), P(AXES), P(), P())
    return jax.shard_map(
        body, mesh=split, in_specs=placed, out_specs=(P(AXES), P(AXES)), check_vma=False
    )
```

```python
import functools

import jax
import jax.numpy as jnp
from jax import lax
from jax.experimental import pallas as pl
from jax.experimental.pallas import tpu as pltpu
from jax.sharding import Mesh, PartitionSpec as P

VOCAB_REAL = 73448


EPS = 1e-05
NEG = -1e30
DIGIT = 64
AXES = ("z", "x", "y", "core")
CHIP_AXES = ("z", "x", "y")


def slice_stats(rows, chosen, head, col_index, real_cols):
    logits = jnp.dot(rows, head, preferred_element_type=jnp.float32) / 10.0
    logits = jnp.where(real_cols[None, :], logits, NEG)
    rowmax = jnp.max(logits, axis=1)
    expo = jnp.where(real_cols[None, :], jnp.exp(logits - rowmax[:, None]), 0.0)
    total = jnp.sum(expo, axis=1)
    weighted = jnp.sum(jnp.where(real_cols[None, :], expo * logits, 0.0), axis=1)
    picked = jnp.sum(jnp.where(col_index[None, :] == chosen[:, None], logits, 0.0), axis=1)
    return (rowmax, total, weighted, picked)


def code_ids(ids):
    digits = [ids // (DIGIT * DIGIT), (ids // DIGIT) % DIGIT, ids % DIGIT]
    return jnp.stack(digits, axis=1).astype(jnp.bfloat16)


def decode_ids(coded):
    d = coded.astype(jnp.int32)
    return (d[:, 0] * DIGIT + d[:, 1]) * DIGIT + d[:, 2]


STREAMS = (("z", "x", "y"), ("x", "y", "z"), ("y", "z", "x"))
LANES = 128


def gather_kernel(sizes, spans, x_ref, g_ref, send_sem, recv_sem, own_sem):
    pos = {a: lax.axis_index(a) for a in AXES}

    def peer(axis, k):
        at = dict(pos)
        at[axis] = lax.rem(pos[axis] + k + sizes[axis], sizes[axis])
        return tuple(at[a] for a in AXES)

    def view(ref, held, axis, k, cols):
        idx = []
        for a in ("y", "x", "z"):
            if a in held:
                idx.append(slice(None))
            elif a == axis:
                idx.append(lax.rem(pos[a] + k + sizes[a], sizes[a]))
            else:
                idx.append(pos[a])
        return ref.at[tuple(idx) + (slice(None), cols)]

    barrier = pltpu.get_barrier_semaphore()
    count = 0
    for axis in CHIP_AXES:
        for k in (1, -1):
            pl.semaphore_signal(barrier, inc=1, device_id=peer(axis, k), device_id_type=pl.DeviceIdType.MESH)
            count += 1
    pl.semaphore_wait(barrier, count)

    own = pltpu.make_async_copy(x_ref, g_ref.at[pos["y"], pos["x"], pos["z"]], own_sem)
    own.start()

    plans = []
    for order in STREAMS:
        plan = []
        for t, axis in enumerate(order):
            n = sizes[axis]
            for q in range(1, n // 2 + 1):
                plan.append((t, axis, q, n % 2 == 0 and q == n // 2))
        plans.append(plan)

    def step_copies(s, step, sending):
        t, axis, q, split = plans[s][step]
        c0, w = spans[s]
        order = STREAMS[s]
        held = order[:t]
        if split:
            cut = (w // LANES // 2) * LANES
            col_of = [pl.ds(c0, cut), pl.ds(c0 + cut, w - cut)]
        else:
            col_of = [pl.ds(c0, w), pl.ds(c0, w)]
        out = []
        for d, sign in enumerate((1, -1)):
            cols = col_of[d]
            if sending:
                k = -sign * (q - 1)
                dst = view(g_ref, held, axis, k, cols)
                src = x_ref.at[:, cols] if (t == 0 and q == 1) else dst
                target = peer(axis, sign)
            else:
                k = -sign * q
                src = dst = view(g_ref, held, axis, k, cols)
                target = peer(axis, -sign)
            out.append(pltpu.make_async_remote_copy(
                src_ref=src, dst_ref=dst, send_sem=send_sem.at[s, step, d],
                recv_sem=recv_sem.at[s, step, d], device_id=target,
                device_id_type=pl.DeviceIdType.MESH,
            ))
        return out

    steps = len(plans[0])
    sends = []
    for g in range(steps):
        for s in range(len(STREAMS)):
            if g > 0:
                for copy in step_copies(s, g - 1, False):
                    copy.wait_recv()
            if g == 1 and s == 0:
                own.wait()
            for copy in step_copies(s, g, True):
                copy.start()
                sends.append(copy)
    for s in range(len(STREAMS)):
        for copy in step_copies(s, steps - 1, False):
            copy.wait_recv()
    for copy in sends:
        copy.wait_send()


def gather_rows(packed, sizes):
    rows, width = packed.shape
    tiles = width // LANES
    counts = [tiles * 9 // 21, tiles * 5 // 21]
    counts.append(tiles - sum(counts))
    spans, at = [], 0
    for c in counts:
        spans.append((at * LANES, c * LANES))
        at += c
    shape = (sizes["y"], sizes["x"], sizes["z"], rows, width)
    steps = sum(sizes[a] // 2 for a in CHIP_AXES)
    return pl.pallas_call(
        functools.partial(gather_kernel, sizes, spans),
        out_shape=jax.ShapeDtypeStruct(shape, packed.dtype),
        in_specs=[pl.BlockSpec(memory_space=pl.ANY)],
        out_specs=pl.BlockSpec(memory_space=pl.ANY),
        scratch_shapes=[
            pltpu.SemaphoreType.DMA((3, steps, 2)),
            pltpu.SemaphoreType.DMA((3, steps, 2)),
            pltpu.SemaphoreType.DMA(()),
        ],
        compiler_params=pltpu.CompilerParams(collective_id=0, has_side_effects=True),
    )(packed)


def combine(parts):
    top = jnp.max(parts[:, 0], axis=0)
    factor = jnp.exp(parts[:, 0] - top[None])
    total = jnp.sum(parts[:, 1] * factor, axis=0)
    weighted = jnp.sum(parts[:, 2] * factor, axis=0)
    picked = jnp.sum(parts[:, 3], axis=0)
    return jnp.stack([top, total, weighted, picked], axis=0)


def reduce_kernel(sizes, a_ref, out_ref, r, send_sem, recv_sem):
    pos = {a: lax.axis_index(a) for a in AXES}
    ny, nx, nz = sizes["y"], sizes["x"], sizes["z"]
    count = ny * nx * nz

    def offsets(i):
        return i // (nx * nz), (i // nz) % nx, i % nz

    def chip(dy, dx, dz):
        return (lax.rem(pos["y"] + dy, ny) * nx + lax.rem(pos["x"] + dx, nx)) * nz + lax.rem(pos["z"] + dz, nz)

    def device(dy, dx, dz):
        return (lax.rem(pos["z"] + dz, nz), lax.rem(pos["x"] + dx, nx), lax.rem(pos["y"] + dy, ny), pos["core"])

    def label(dy, dx, dz):
        return ((ny - dy) % ny * nx + (nx - dx) % nx) * nz + (nz - dz) % nz

    def copy_to(i):
        dy, dx, dz = offsets(i)
        return pltpu.make_async_remote_copy(
            src_ref=a_ref.at[chip(dy, dx, dz)], dst_ref=r.at[chip(0, 0, 0)], send_sem=send_sem.at[i],
            recv_sem=recv_sem.at[label(dy, dx, dz)], device_id=device(dy, dx, dz),
            device_id_type=pl.DeviceIdType.MESH,
        )

    def copy_from(j):
        dy, dx, dz = offsets(j)
        slot = r.at[chip(dy, dx, dz)]
        return pltpu.make_async_remote_copy(
            src_ref=slot, dst_ref=slot, send_sem=send_sem.at[j], recv_sem=recv_sem.at[j],
            device_id=device(dy, dx, dz), device_id_type=pl.DeviceIdType.MESH,
        )

    barrier = pltpu.get_barrier_semaphore()

    def greet(i, carry):
        pl.semaphore_signal(barrier, inc=1, device_id=device(*offsets(i)), device_id_type=pl.DeviceIdType.MESH)
        return carry

    lax.fori_loop(1, count, greet, 0)
    pl.semaphore_wait(barrier, count - 1)

    mine = chip(0, 0, 0)
    r[mine] = a_ref[mine]

    def send(i, carry):
        copy_to(i).start()
        return carry

    def receive(j, carry):
        copy_from(j).wait_recv()
        return carry

    def sent(i, carry):
        copy_to(i).wait_send()
        return carry

    lax.fori_loop(1, count, send, 0)
    lax.fori_loop(1, count, receive, 0)
    out_ref[...] = combine(r[...])
    lax.fori_loop(1, count, sent, 0)


def reduce_stats(parts, sizes):
    count = parts.shape[0]
    return pl.pallas_call(
        functools.partial(reduce_kernel, sizes),
        out_shape=jax.ShapeDtypeStruct(parts.shape[1:], jnp.float32),
        scratch_shapes=[
            pltpu.VMEM(parts.shape, jnp.float32),
            pltpu.SemaphoreType.DMA((count,)),
            pltpu.SemaphoreType.DMA((count,)),
        ],
        compiler_params=pltpu.CompilerParams(collective_id=1, has_side_effects=True),
    )(parts)


def pack_kernel(h_ref, gain_ref, ids_ref, out_ref):
    values = h_ref[...].astype(jnp.float32)
    rows, width = values.shape
    scale = lax.rsqrt(jnp.mean(values * values, axis=-1, keepdims=True) + EPS)
    out_ref[:, :width] = (values * scale * gain_ref[...][None, :]).astype(jnp.bfloat16)
    row = lax.broadcasted_iota(jnp.int32, (rows, LANES), 0)
    lane = lax.broadcasted_iota(jnp.int32, (rows, LANES), 1)
    digit = jnp.zeros((rows, LANES), jnp.int32)
    for r in range(rows):
        v = ids_ref[r]
        for i, d in enumerate((v // (DIGIT * DIGIT), (v // DIGIT) % DIGIT, v % DIGIT)):
            digit = jnp.where((row == r) & (lane == i), d, digit)
    out_ref[:, width:] = digit.astype(jnp.float32).astype(jnp.bfloat16)


def pack_rows(hidden, norm_gain, token_ids):
    rows, width = hidden.shape
    return pl.pallas_call(
        pack_kernel,
        out_shape=jax.ShapeDtypeStruct((rows, width + LANES), jnp.bfloat16),
        in_specs=[
            pl.BlockSpec(memory_space=pltpu.VMEM),
            pl.BlockSpec(memory_space=pltpu.VMEM),
            pl.BlockSpec(memory_space=pltpu.SMEM),
        ],
    )(hidden, norm_gain, token_ids)


def body(hidden, norm_gain, head, token_ids, req_len, req_owner):
    local_rows, width = hidden.shape
    columns = head.shape[1]
    size = {a: lax.axis_size(a) for a in AXES}
    pos = {a: lax.axis_index(a) for a in AXES}
    chip = (pos["z"] * size["x"] + pos["x"]) * size["y"] + pos["y"]
    core = pos["core"]
    me = chip * size["core"] + core

    packed = pack_rows(hidden, norm_gain, token_ids)

    other = lax.ppermute(head, "core", [(0, 1), (1, 0)])
    chip_head = jnp.where(core == 0, jnp.concatenate([head, other], axis=1), jnp.concatenate([other, head], axis=1))
    col_index = chip * (2 * columns) + jnp.arange(2 * columns, dtype=jnp.int32)
    real_cols = col_index < VOCAB_REAL

    gathered = gather_rows(packed, size).reshape(-1, packed.shape[1])
    all_rows = gathered[:, :width]
    all_ids = decode_ids(gathered[:, width:width + 3])
    stats = jnp.stack(slice_stats(all_rows, all_ids, chip_head, col_index, real_cols), axis=0)

    parts = jnp.transpose(stats.reshape(4, -1, local_rows), (1, 0, 2))
    mine = reduce_stats(parts, size)
    top, total_all, weighted_all, picked_all = mine[0], mine[1], mine[2], mine[3]

    load = jnp.sum(jnp.where(req_owner == me, req_len, 0))
    live = jnp.arange(local_rows, dtype=jnp.int32) < load
    log_total = jnp.log(total_all)
    logprob = jnp.where(live, picked_all - top - log_total, 0.0)
    entropy = jnp.where(live, top + log_total - weighted_all / total_all, 0.0)
    return (logprob, entropy)


def solution(mesh):
    split = Mesh(mesh.devices.reshape(8, 4, 4, 2), AXES)
    placed = (P(AXES, None), P(), P(None, AXES), P(AXES), P(), P())
    return jax.shard_map(
        body, mesh=split, in_specs=placed, out_specs=(P(AXES), P(AXES)), check_vma=False
    )
```

```python
import functools

import jax
import jax.numpy as jnp
from jax import lax
from jax.experimental import pallas as pl
from jax.experimental.pallas import tpu as pltpu
from jax.sharding import Mesh, PartitionSpec as P

VOCAB_REAL = 73448


EPS = 1e-05
NEG = -1e30
DIGIT = 64
AXES = ("z", "x", "y", "core")
CHIP_AXES = ("z", "x", "y")


def slice_stats(rows, chosen, head, col_index, real_cols):
    logits = jnp.dot(rows, head, preferred_element_type=jnp.float32) / 10.0
    logits = jnp.where(real_cols[None, :], logits, NEG)
    rowmax = jnp.max(logits, axis=1)
    expo = jnp.where(real_cols[None, :], jnp.exp(logits - rowmax[:, None]), 0.0)
    total = jnp.sum(expo, axis=1)
    weighted = jnp.sum(jnp.where(real_cols[None, :], expo * logits, 0.0), axis=1)
    picked = jnp.sum(jnp.where(col_index[None, :] == chosen[:, None], logits, 0.0), axis=1)
    return (rowmax, total, weighted, picked)


def code_ids(ids):
    digits = [ids // (DIGIT * DIGIT), (ids // DIGIT) % DIGIT, ids % DIGIT]
    return jnp.stack(digits, axis=1).astype(jnp.bfloat16)


def decode_ids(coded):
    d = coded.astype(jnp.int32)
    return (d[:, 0] * DIGIT + d[:, 1]) * DIGIT + d[:, 2]


STREAMS = (("z", "x", "y"), ("x", "y", "z"), ("y", "z", "x"))
LANES = 128


def gather_kernel(sizes, spans, x_ref, g_ref, send_sem, recv_sem, own_sem):
    pos = {a: lax.axis_index(a) for a in AXES}

    def peer(axis, k):
        at = dict(pos)
        at[axis] = lax.rem(pos[axis] + k + sizes[axis], sizes[axis])
        return tuple(at[a] for a in AXES)

    def view(ref, held, axis, k, cols):
        idx = []
        for a in ("y", "x", "z"):
            if a in held:
                idx.append(slice(None))
            elif a == axis:
                idx.append(lax.rem(pos[a] + k + sizes[a], sizes[a]))
            else:
                idx.append(pos[a])
        return ref.at[tuple(idx) + (slice(None), cols)]

    barrier = pltpu.get_barrier_semaphore()
    count = 0
    for axis in CHIP_AXES:
        reach = range(1, sizes[axis]) if axis == STREAMS[1][0] else (1, -1)
        for k in reach:
            pl.semaphore_signal(barrier, inc=1, device_id=peer(axis, k), device_id_type=pl.DeviceIdType.MESH)
            count += 1
    pl.semaphore_wait(barrier, count)

    own = pltpu.make_async_copy(x_ref, g_ref.at[pos["y"], pos["x"], pos["z"]], own_sem)
    own.start()

    plans = []
    for order in STREAMS:
        direct = order == STREAMS[1]
        plan = [(0, order[0], 0, False)] if direct else []
        for t, axis in enumerate(order[1:] if direct else order, start=1 if direct else 0):
            n = sizes[axis]
            for q in range(1, n // 2 + 1):
                plan.append((t, axis, q, n % 2 == 0 and q == n // 2))
        plans.append(plan)

    def step_copies(s, step, sending):
        t, axis, q, split = plans[s][step]
        c0, w = spans[s]
        order = STREAMS[s]
        held = order[:t]
        n = sizes[axis]
        out = []
        if q == 0:
            cols = pl.ds(c0, w)
            for k in range(1, n):
                if sending:
                    dst = view(g_ref, held, axis, 0, cols)
                    src = x_ref.at[:, cols] if t == 0 else dst
                    target, label = peer(axis, k), (n - k) % n
                else:
                    src = dst = view(g_ref, held, axis, k, cols)
                    target, label = peer(axis, k), k
                out.append(pltpu.make_async_remote_copy(
                    src_ref=src, dst_ref=dst, send_sem=send_sem.at[s, step, k if sending else label],
                    recv_sem=recv_sem.at[s, step, label], device_id=target,
                    device_id_type=pl.DeviceIdType.MESH,
                ))
            return out
        if split:
            cut = (w // LANES // 2) * LANES
            col_of = [pl.ds(c0, cut), pl.ds(c0 + cut, w - cut)]
        else:
            col_of = [pl.ds(c0, w), pl.ds(c0, w)]
        for d, sign in enumerate((1, -1)):
            cols = col_of[d]
            if sending:
                k = -sign * (q - 1)
                dst = view(g_ref, held, axis, k, cols)
                src = x_ref.at[:, cols] if (t == 0 and q == 1) else dst
                target = peer(axis, sign)
            else:
                k = -sign * q
                src = dst = view(g_ref, held, axis, k, cols)
                target = peer(axis, -sign)
            out.append(pltpu.make_async_remote_copy(
                src_ref=src, dst_ref=dst, send_sem=send_sem.at[s, step, d],
                recv_sem=recv_sem.at[s, step, d], device_id=target,
                device_id_type=pl.DeviceIdType.MESH,
            ))
        return out

    steps = max(len(p) for p in plans)
    sends = []
    for g in range(steps):
        for s in range(len(STREAMS)):
            if g >= len(plans[s]):
                continue
            if g > 0:
                for copy in step_copies(s, g - 1, False):
                    copy.wait_recv()
            if g == 1 and s == 0:
                own.wait()
            for copy in step_copies(s, g, True):
                copy.start()
                sends.append(copy)
    for s in range(len(STREAMS)):
        for copy in step_copies(s, len(plans[s]) - 1, False):
            copy.wait_recv()
    for copy in sends:
        copy.wait_send()


def gather_rows(packed, sizes):
    rows, width = packed.shape
    tiles = width // LANES
    counts = [tiles * 9 // 21, tiles * 5 // 21]
    counts.append(tiles - sum(counts))
    spans, at = [], 0
    for c in counts:
        spans.append((at * LANES, c * LANES))
        at += c
    shape = (sizes["y"], sizes["x"], sizes["z"], rows, width)
    steps = sum(sizes[a] // 2 for a in CHIP_AXES)
    longest = max(sizes[a] for a in CHIP_AXES)
    return pl.pallas_call(
        functools.partial(gather_kernel, sizes, spans),
        out_shape=jax.ShapeDtypeStruct(shape, packed.dtype),
        in_specs=[pl.BlockSpec(memory_space=pl.ANY)],
        out_specs=pl.BlockSpec(memory_space=pl.ANY),
        scratch_shapes=[
            pltpu.SemaphoreType.DMA((3, steps, longest)),
            pltpu.SemaphoreType.DMA((3, steps, longest)),
            pltpu.SemaphoreType.DMA(()),
        ],
        compiler_params=pltpu.CompilerParams(collective_id=0, has_side_effects=True),
    )(packed)


def combine(parts):
    top = jnp.max(parts[:, 0], axis=0)
    factor = jnp.exp(parts[:, 0] - top[None])
    total = jnp.sum(parts[:, 1] * factor, axis=0)
    weighted = jnp.sum(parts[:, 2] * factor, axis=0)
    picked = jnp.sum(parts[:, 3], axis=0)
    return jnp.stack([top, total, weighted, picked], axis=0)


def reduce_kernel(sizes, a_ref, out_ref, r1, c1, r2, send_sem, recv_sem):
    pos = {a: lax.axis_index(a) for a in AXES}
    ny, nx, nz = sizes["y"], sizes["x"], sizes["z"]

    def peer(offsets):
        at = dict(pos)
        for a, k in offsets.items():
            at[a] = lax.rem(pos[a] + k, sizes[a])
        return tuple(at[a] for a in AXES)

    plane = [(ky, kx) for ky in range(ny) for kx in range(nx) if (ky, kx) != (0, 0)]
    barrier = pltpu.get_barrier_semaphore()
    targets = [{"y": ky, "x": kx} for ky, kx in plane] + [{"z": k} for k in range(1, nz)]
    for offsets in targets:
        pl.semaphore_signal(barrier, inc=1, device_id=peer(offsets), device_id_type=pl.DeviceIdType.MESH)
    pl.semaphore_wait(barrier, len(targets))

    sends = []
    mine = pos["y"] * nx + pos["x"]
    r1[mine] = a_ref[mine]
    for ky, kx in plane:
        there = lax.rem(pos["y"] + ky, ny) * nx + lax.rem(pos["x"] + kx, nx)
        copy = pltpu.make_async_remote_copy(
            src_ref=a_ref.at[there], dst_ref=r1.at[mine], send_sem=send_sem.at[0, ky * nx + kx],
            recv_sem=recv_sem.at[0, ((ny - ky) % ny) * nx + (nx - kx) % nx],
            device_id=peer({"y": ky, "x": kx}), device_id_type=pl.DeviceIdType.MESH,
        )
        copy.start()
        sends.append(copy)
    for jy, jx in plane:
        slot = r1.at[lax.rem(pos["y"] + jy, ny) * nx + lax.rem(pos["x"] + jx, nx)]
        pltpu.make_async_remote_copy(
            src_ref=slot, dst_ref=slot, send_sem=send_sem.at[0, jy * nx + jx], recv_sem=recv_sem.at[0, jy * nx + jx],
            device_id=peer({"y": jy, "x": jx}), device_id_type=pl.DeviceIdType.MESH,
        ).wait_recv()
    c1[...] = combine(r1[...])
    r2[pos["z"]] = c1[...]
    for k in range(1, nz):
        copy = pltpu.make_async_remote_copy(
            src_ref=c1, dst_ref=r2.at[pos["z"]], send_sem=send_sem.at[1, k], recv_sem=recv_sem.at[1, (nz - k) % nz],
            device_id=peer({"z": k}), device_id_type=pl.DeviceIdType.MESH,
        )
        copy.start()
        sends.append(copy)
    for j in range(1, nz):
        slot = r2.at[lax.rem(pos["z"] + j, nz)]
        pltpu.make_async_remote_copy(
            src_ref=slot, dst_ref=slot, send_sem=send_sem.at[1, j], recv_sem=recv_sem.at[1, j],
            device_id=peer({"z": j}), device_id_type=pl.DeviceIdType.MESH,
        ).wait_recv()
    out_ref[...] = combine(r2[...])
    for copy in sends:
        copy.wait_send()


def reduce_stats(parts, sizes):
    planes, nz = parts.shape[0], sizes["z"]
    labels = max(planes, nz)
    return pl.pallas_call(
        functools.partial(reduce_kernel, sizes),
        out_shape=jax.ShapeDtypeStruct((4, LANES), jnp.float32),
        scratch_shapes=[
            pltpu.VMEM((planes, 4, LANES), jnp.float32),
            pltpu.VMEM((4, LANES), jnp.float32),
            pltpu.VMEM((nz, 4, LANES), jnp.float32),
            pltpu.SemaphoreType.DMA((2, labels)),
            pltpu.SemaphoreType.DMA((2, labels)),
        ],
        compiler_params=pltpu.CompilerParams(collective_id=1, has_side_effects=True),
    )(parts)


def pack_kernel(h_ref, gain_ref, ids_ref, out_ref):
    values = h_ref[...].astype(jnp.float32)
    rows, width = values.shape
    scale = lax.rsqrt(jnp.mean(values * values, axis=-1, keepdims=True) + EPS)
    out_ref[:, :width] = (values * scale * gain_ref[...][None, :]).astype(jnp.bfloat16)
    row = lax.broadcasted_iota(jnp.int32, (rows, LANES), 0)
    lane = lax.broadcasted_iota(jnp.int32, (rows, LANES), 1)
    digit = jnp.zeros((rows, LANES), jnp.int32)
    for r in range(rows):
        v = ids_ref[r]
        for i, d in enumerate((v // (DIGIT * DIGIT), (v // DIGIT) % DIGIT, v % DIGIT)):
            digit = jnp.where((row == r) & (lane == i), d, digit)
    out_ref[:, width:] = digit.astype(jnp.float32).astype(jnp.bfloat16)


def pack_rows(hidden, norm_gain, token_ids):
    rows, width = hidden.shape
    return pl.pallas_call(
        pack_kernel,
        out_shape=jax.ShapeDtypeStruct((rows, width + LANES), jnp.bfloat16),
        in_specs=[
            pl.BlockSpec(memory_space=pltpu.VMEM),
            pl.BlockSpec(memory_space=pltpu.VMEM),
            pl.BlockSpec(memory_space=pltpu.SMEM),
        ],
    )(hidden, norm_gain, token_ids)


def body(hidden, norm_gain, head, token_ids, req_len, req_owner):
    local_rows, width = hidden.shape
    columns = head.shape[1]
    size = {a: lax.axis_size(a) for a in AXES}
    pos = {a: lax.axis_index(a) for a in AXES}
    chip = (pos["z"] * size["x"] + pos["x"]) * size["y"] + pos["y"]
    core = pos["core"]
    me = chip * size["core"] + core

    packed = pack_rows(hidden, norm_gain, token_ids)

    other = lax.ppermute(head, "core", [(0, 1), (1, 0)])
    chip_head = jnp.where(core == 0, jnp.concatenate([head, other], axis=1), jnp.concatenate([other, head], axis=1))
    col_index = chip * (2 * columns) + jnp.arange(2 * columns, dtype=jnp.int32)
    real_cols = col_index < VOCAB_REAL

    gathered = gather_rows(packed, size).reshape(-1, packed.shape[1])
    all_rows = gathered[:, :width]
    all_ids = decode_ids(gathered[:, width:width + 3])
    stats = jnp.stack(slice_stats(all_rows, all_ids, chip_head, col_index, real_cols), axis=0)

    parts = jnp.transpose(stats.reshape(4, size["y"] * size["x"], -1), (1, 0, 2))
    reduced = reduce_stats(parts, size)
    mine = lax.dynamic_slice_in_dim(reduced, pos["z"] * local_rows, local_rows, axis=1)
    top, total_all, weighted_all, picked_all = mine[0], mine[1], mine[2], mine[3]

    load = jnp.sum(jnp.where(req_owner == me, req_len, 0))
    live = jnp.arange(local_rows, dtype=jnp.int32) < load
    log_total = jnp.log(total_all)
    logprob = jnp.where(live, picked_all - top - log_total, 0.0)
    entropy = jnp.where(live, top + log_total - weighted_all / total_all, 0.0)
    return (logprob, entropy)


def solution(mesh):
    split = Mesh(mesh.devices.reshape(8, 4, 4, 2), AXES)
    placed = (P(AXES, None), P(), P(None, AXES), P(AXES), P(), P())
    return jax.shard_map(
        body, mesh=split, in_specs=placed, out_specs=(P(AXES), P(AXES)), check_vma=False
    )
```
